32 devices in a mesh: groups: 2 (over y), row: 4 (over z), col: 2 (over x), rep: 2 (over core).
Axes of the slice: x: 2, y: 2, z: 4, core: 2. Of those that a mesh axis runs over, the one named last changes fastest.
Arguments:
- amplitudes: bfloat16 [256, 256, 256], P(('groups', 'row', 'col')), parts along dimension 0, may hold values from -3 to 3
- integrals: bfloat16 [256, 256, 256], P(('groups', 'row', 'col')), parts along dimension 0, may hold values from -27 to 27
- fock_matrix: bfloat16 [256, 256, 256], P(('groups', 'row', 'col')), parts along dimension 0, may hold values from -0.2625 to 4
- intersection: bfloat16 [256, 256, 256], P(('groups', 'row', 'col')), parts along dimension 0, may hold values from -0.1875 to 1
- occ_energy: float32 [128], P('groups'), parts along dimension 0, may hold values from -2 to -0.5
- first_occ: int32 [256], P(('groups', 'row', 'col')), parts along dimension 0, may hold values from 0 to 63
- second_occ: int32 [256], P(('groups', 'row', 'col')), parts along dimension 0, may hold values from 0 to 63
- near_slot: int32 [256, 11], P(('groups', 'row', 'col')), parts along dimension 0, may hold values from 0 to 15
- near_count: int32 [256], P(('groups', 'row', 'col')), parts along dimension 0, may hold values from 4 to 11
- near_weight: bfloat16 [256, 11], P(('groups', 'row', 'col')), parts along dimension 0, may hold values from -0.59765625 to 0.59765625
- far_chip: int32 [256, 1], P(('groups', 'row', 'col')), parts along dimension 0, may hold values from 0 to 3; in each aligned block of 16 rows (0 to 15, 16 to 31, ...) at most 8 rows name the same one
- far_slot: int32 [256, 1], P(('groups', 'row', 'col')), parts along dimension 0, may hold values from 0 to 15
- far_weight: bfloat16 [256, 1], P(('groups', 'row', 'col')), parts along dimension 0, may hold values from 0.29882812 to 0.8984375
Outputs:
- final_amps: bfloat16 [256, 256, 256], P(('groups', 'row', 'col')), parts along dimension 0
- occ_density: float32 [128], P('groups'), parts along dimension 0
The draws below stay inside these ranges and needn't reach their ends.
There are 2 independent parts, one for each index of `groups`. The reference program is written for one: setup_inputs(seed, part) draws one part's arguments, and reference() takes and returns one part's arrays. A program takes and returns all parts, laid end to end along the dimension named above; each array names one. Nothing has to cross between parts.
Inputs may be any that keep to these rules, and one draw needn't show every extreme that they name: `far_chip`: no value is named by more than 8 of the 16 pairs of one chip.
All inputs are finite; a program needn't handle non-finite values.
Results may differ from the reference program's by a relative error of at most 0.0026.
Values may be sent and summed in bfloat16 or wider, within the bound.
No kernel may reach another device: no remote copies, remote signals or barrier semaphores. Data moves between devices by JAX's collectives and lax.ppermute only.
A program may use at most 128 MiB of HBM per device.

```python
import math
import jax
import jax.numpy as jnp
import numpy as np
from jax import lax

VIRT = 256
NOCC = 64
NLOC = 11
ITERS = 2
PAIR_CHIP = 16
CAP = 8
PAIRS = 128
N_ROW = 4
N_COL = 2


def unit_noise(key, shape):
    return jnp.clip(jax.random.normal(key, shape, jnp.float32), -6.0, 6.0)


def draw_integrals(key, part):
    noise = unit_noise(jax.random.fold_in(key, 11), (PAIRS, VIRT, VIRT))
    growth = 1.0 + 2.0 * jnp.arange(PAIRS, dtype=jnp.float32) / (PAIRS - 1)
    return (1.5 * noise * growth[:, None, None]).astype(jnp.bfloat16)


def draw_fock_matrix(key, part):
    noise = unit_noise(jax.random.fold_in(key, 23), (PAIRS, VIRT, VIRT))
    coupling = (noise + jnp.swapaxes(noise, 1, 2)) * (0.35 / VIRT ** 0.5)
    levels = jnp.exp(jax.random.uniform(jax.random.fold_in(key, 29), (PAIRS, VIRT), jnp.float32, 0.0, 1.3862944))
    identity = jnp.eye(VIRT, dtype=jnp.float32)[None, :, :] > 0.5
    return jnp.where(identity, levels[:, :, None], coupling).astype(jnp.bfloat16)


def draw_intersection(key, part):
    noise = unit_noise(jax.random.fold_in(key, 37), (PAIRS, VIRT, VIRT)) * (0.5 / VIRT ** 0.5)
    identity = jnp.eye(VIRT, dtype=jnp.float32)[None, :, :] > 0.5
    return jnp.where(identity, jnp.float32(1.0), noise).astype(jnp.bfloat16)


def with_ends(values, rng, low, top_value):
    longest = values.shape.index(max(values.shape))
    spots = []
    for shift in (0, 1):
        where = [jax.random.randint(jax.random.fold_in(rng, axis), (), 0, length) for axis, length in enumerate(values.shape)]
        where[longest] = (where[longest] + shift) % values.shape[longest]
        spots.append(tuple(where))
    return values.at[spots[0]].set(low).at[spots[1]].set(top_value)


def block_scale(own_key, shape, pieces, low, top_value):
    loudness, own = 1.0, jax.random.fold_in(own_key, 6)
    for position, shards_of in pieces:
        steps = jnp.exp(jax.random.uniform(jax.random.fold_in(own, position), (shards_of,), jnp.float32, low / len(pieces), top_value / len(pieces)))
        loudness = loudness * jnp.repeat(steps, shape[position] // shards_of).reshape([-1 if axis == position else 1 for axis in range(len(shape))])
    return loudness


def deal_out(own_key, own, number, rows, count, top, limit, skew):
    sequence = jax.random.permutation(own_key, count)
    packed, common = portions_of(count, rows * top, limit, skew, True), portions_of(count, rows * top, limit, skew, False)
    places = jnp.arange(count)

    def named(lengths, rotation):
        used = int((lengths > 0).sum())
        fixed = max(1, used // 4)
        moved = fixed + (places - fixed + rotation * (used - fixed)) % max(1, count - fixed)
        return jnp.zeros((count,), jnp.int32).at[sequence[jnp.where(places < fixed, places, moved)]].set(jnp.asarray(lengths, jnp.int32))

    lengths = jnp.where(number % 4 == 0, named(packed, number // 4), named(common, number - number // 4 - 1))
    mixed = jax.random.permutation(jax.random.fold_in(own, 3), count)
    giver, receiver = mixed[0:count // 2 * 2:2], mixed[1:count // 2 * 2:2]
    margin = jnp.minimum(lengths[giver] - 1, limit - lengths[receiver]) // 2
    margin = jnp.where((giver == sequence[0]) | (receiver == sequence[0]) | (lengths[receiver] == 0), 0, jnp.maximum(margin, 0))
    moved = jax.random.randint(jax.random.fold_in(own, 4), (count // 2,), 0, 1 << 20) % (margin + 1)
    lengths = lengths.at[giver].add(-moved).at[receiver].add(moved)
    items = jnp.searchsorted(jnp.cumsum(lengths), jnp.arange(rows * top), side="right").astype(jnp.int32)
    grid = items.reshape(top, rows).T
    grid = grid[jax.random.permutation(jax.random.fold_in(own, 1), rows)]
    rotation = jax.random.randint(jax.random.fold_in(own, 2), (rows, 1), 0, top)
    return jnp.take_along_axis(grid, (jnp.arange(top)[None, :] + rotation) % top, axis=1)


def portions_of(amount, total, bound, lean, full):
    portions = [(1 << 20) // math.isqrt(grade ** lean) + 1 for grade in range(1, amount + 1)]
    largest = bound if full else min(bound, max(-(-total // amount), total * portions[0] // sum(portions)))
    least = 1 if total - largest >= amount - 1 else 0
    counts, rest = [largest] + [least] * (amount - 1), total - largest - least * (amount - 1)
    while rest > 0:
        movable = [i for i in range(1, amount) if counts[i] < largest] or [i for i in range(1, amount) if counts[i] < bound]
        mass, budget = sum([portions[i] for i in movable]), rest
        for i in movable:
            more = min(bound - counts[i], max(1, budget * portions[i] // mass), rest)
            counts[i] = counts[i] + more
            rest = rest - more
    return np.array(counts)


def centred(stream_key, dims, spread, limit, pieces=(), kind=jnp.bfloat16):
    factor_of = block_scale(stream_key, dims, pieces, -0.22, 0.18) if pieces else 1.0
    array = jax.random.normal(stream_key, dims, jnp.float32) * spread * factor_of
    return jnp.minimum(jnp.maximum(array, -limit), limit).astype(kind)


def setup_inputs(seed: int = 0, part: int = 0) -> dict:
    key_of = jax.random.split(jax.random.key(seed), 14)
    part_keys = jax.random.split(jax.random.fold_in(key_of[13], part), 14)
    amplitudes = centred(part_keys[0], (PAIRS, VIRT, VIRT), 0.5, 3.0, ((0, 8),))
    integrals = draw_integrals(jax.random.fold_in(jax.random.fold_in(key_of[13], part), 71), part)
    fock_matrix = draw_fock_matrix(jax.random.fold_in(jax.random.fold_in(key_of[13], part), 71), part)
    intersection = draw_intersection(jax.random.fold_in(jax.random.fold_in(key_of[13], part), 71), part)
    occ_energy = jnp.clip(jax.random.uniform(part_keys[4], (NOCC,), jnp.float32, -2.0, -0.5), -2.0, -0.5)
    first_occ = with_ends(jax.random.randint(part_keys[5], (PAIRS,), 0, NOCC), jax.random.fold_in(part_keys[5], 1), 0, NOCC - 1).astype(jnp.int32)
    second_occ = with_ends(jax.random.randint(part_keys[6], (PAIRS,), 0, NOCC), jax.random.fold_in(part_keys[6], 1), 0, NOCC - 1).astype(jnp.int32)
    near_slot = with_ends(jax.random.randint(part_keys[7], (PAIRS, NLOC), 0, PAIR_CHIP), jax.random.fold_in(part_keys[7], 1), 0, PAIR_CHIP - 1).astype(jnp.int32)
    near_count = with_ends(jax.random.randint(part_keys[8], (PAIRS,), 4, NLOC + 1), jax.random.fold_in(part_keys[8], 1), 4, NLOC).astype(jnp.int32)
    near_weight = jnp.clip(jax.random.uniform(part_keys[9], (PAIRS, NLOC), jnp.float32, -0.59765625, 0.59765625) * block_scale(part_keys[9], (PAIRS, NLOC), ((0, 8),), -0.4, 0.0), -0.59765625, 0.59765625).astype(jnp.bfloat16)
    far_chip_keys = jax.random.split(jax.random.fold_in(part_keys[10], 1), PAIRS // PAIR_CHIP)
    far_chip_turns = jax.random.permutation(jax.random.fold_in(part_keys[10], 3), PAIRS // PAIR_CHIP)
    far_chip = jax.vmap(lambda own, number: deal_out(jax.random.fold_in(part_keys[10], 2), own, number, PAIR_CHIP, N_ROW, 1, CAP, 2))(far_chip_keys, far_chip_turns).reshape((PAIRS, 1))
    far_slot = with_ends(jax.random.randint(part_keys[11], (PAIRS, 1), 0, PAIR_CHIP), jax.random.fold_in(part_keys[11], 1), 0, PAIR_CHIP - 1).astype(jnp.int32)
    far_weight = jnp.clip(jnp.exp(math.log(0.8984375) - 1.1007886 * jax.random.uniform(part_keys[12], (PAIRS, 1), jnp.float32) ** block_scale(part_keys[12], (PAIRS, 1), ((0, 8),), -0.2, 0.2)), 0.29882812, 0.8984375).astype(jnp.bfloat16)
    return dict(amplitudes=amplitudes, integrals=integrals, fock_matrix=fock_matrix, intersection=intersection, occ_energy=occ_energy, first_occ=first_occ, second_occ=second_occ, near_slot=near_slot, near_count=near_count, near_weight=near_weight, far_chip=far_chip, far_slot=far_slot, far_weight=far_weight)


def reference(amplitudes, integrals, fock_matrix, intersection, occ_energy, first_occ, second_occ, near_slot, near_count, near_weight, far_chip, far_slot, far_weight):
    chip_count = PAIRS // PAIR_CHIP
    domain = VIRT
    pair_ids = jnp.arange(PAIRS, dtype=jnp.int32)
    slot_ids = jnp.arange(PAIR_CHIP, dtype=jnp.int32)
    near_pos = jnp.arange(NLOC, dtype=jnp.int32)
    alive_mask = near_pos[None, :] < near_count[:, None]
    matches = (near_slot[:, :, None] == slot_ids[None, None, :]) & alive_mask[:, :, None]
    local_weights = jnp.sum(jnp.where(matches, near_weight.astype(jnp.float32)[:, :, None], jnp.float32(0.0)), axis=1).astype(jnp.bfloat16)
    local_weights = local_weights.reshape(chip_count, PAIR_CHIP, PAIR_CHIP).astype(jnp.float32)
    col_index = (pair_ids // PAIR_CHIP) % N_COL
    far_pair = ((far_chip[:, 0] * N_COL + col_index) * PAIR_CHIP + far_slot[:, 0]).astype(jnp.int32)
    orbitals = jnp.arange(NOCC, dtype=jnp.int32)
    occ_shift = jnp.sum(jnp.where(first_occ[:, None] == orbitals[None, :], occ_energy[None, :], jnp.float32(0.0)), axis=1)
    occ_shift = occ_shift + jnp.sum(jnp.where(second_occ[:, None] == orbitals[None, :], occ_energy[None, :], jnp.float32(0.0)), axis=1)
    energies = jnp.diagonal(fock_matrix, axis1=1, axis2=2).astype(jnp.float32)
    denominator = energies[:, :, None] + energies[:, None, :] - occ_shift[:, None, None]
    fock_wide = fock_matrix.astype(jnp.float32)
    over_wide = intersection.astype(jnp.float32)
    integ_wide = integrals.astype(jnp.float32)
    far_scale = far_weight[:, 0].astype(jnp.float32)
    amps = amplitudes
    for sweep in range(ITERS):
        amps_wide = amps.astype(jnp.float32)
        flat_amps = amps_wide.reshape(chip_count, PAIR_CHIP, domain * domain)
        local_sum = jnp.einsum("cps,csv->cpv", local_weights, flat_amps).reshape(PAIRS, domain, domain)
        remote = far_scale[:, None, None] * amps_wide[far_pair]
        coupled_sum = lax.optimization_barrier((local_sum + remote).astype(jnp.bfloat16)).astype(jnp.float32)
        projected = jnp.einsum("pab,pbc->pac", over_wide, coupled_sum)
        projected = lax.optimization_barrier(projected.astype(jnp.bfloat16)).astype(jnp.float32)
        coupled = jnp.einsum("pab,pcb->pac", projected, over_wide)
        fock_left = jnp.einsum("pab,pbc->pac", fock_wide, amps_wide)
        fock_right = jnp.einsum("pab,pbc->pac", amps_wide, fock_wide)
        residual = integ_wide + fock_left + fock_right - occ_shift[:, None, None] * amps_wide - coupled
        amps = (amps_wide - residual / denominator).astype(jnp.bfloat16)
    final_wide = amps.astype(jnp.float32)
    pair_norm = jnp.sum((2.0 * final_wide - jnp.swapaxes(final_wide, 1, 2)) * final_wide, axis=(1, 2))
    occ_sum = jax.ops.segment_sum(pair_norm, first_occ, num_segments=NOCC) + jax.ops.segment_sum(pair_norm, second_occ, num_segments=NOCC)
    occ_density = occ_sum * (NOCC / (2.0 * PAIRS * domain * domain))
    return amps, occ_density
```

```python
import jax
import jax.numpy as jnp
from jax import lax
from jax.experimental import pallas as pl
from jax.experimental.pallas import tpu as pltpu
from jax.sharding import PartitionSpec as P

ITERS = 2
ANY = pl.ANY
SMEM = pltpu.SMEM
LANES = 16


def rotation(rows, shift):
    return [(r, (r + shift) % rows) for r in range(rows)]


def gather_sends(requests, place, where, stores, rows, cap):
    pairs = requests[0].shape[0]
    blocks = (rows - 1) * cap
    domain = stores[0].shape[1]
    depth = stores[0].shape[0]

    def body(place_ref, where_ref, *refs):
        lists = refs[: rows - 1]
        sources = refs[rows - 1 : rows - 1 + len(stores)]
        outs = refs[rows - 1 + len(stores) : rows - 1 + len(stores) + rows - 1]
        hold, asked, in_sem, out_sem = refs[-4:]
        me = place_ref[0]
        core = place_ref[1]
        for shift in range(rows - 1):
            for k in range(cap):
                asked[shift * cap + k] = 0
            count = jnp.int32(0)
            for p in range(pairs):
                count = count + (lists[shift][p] // pairs < me).astype(jnp.int32)
            filled = jnp.int32(0)
            for p in range(pairs):
                packed = lists[shift][p]
                mine = packed // pairs == me
                taken = mine & (count % 2 == core)

                @pl.when(taken)
                def _(filled=filled, packed=packed):
                    asked[shift * cap + filled] = packed % pairs

                count = count + mine.astype(jnp.int32)
                filled = jnp.minimum(filled + taken.astype(jnp.int32), cap - 1)
        for b in range(blocks):
            spot = where_ref[asked[b]]
            for n, source in enumerate(sources):

                @pl.when(spot // depth == n)
                def _(source=source, spot=spot, b=b):
                    pltpu.make_async_copy(
                        source.at[spot % depth], hold.at[b], in_sem.at[b]
                    ).start()

        for b in range(blocks):
            pltpu.make_async_copy(sources[0].at[0], hold.at[b], in_sem.at[b]).wait()
            pltpu.make_async_copy(
                hold.at[b], outs[b // cap].at[b % cap], out_sem.at[b]
            ).start()
        for b in range(blocks):
            pltpu.make_async_copy(
                hold.at[b], outs[b // cap].at[b % cap], out_sem.at[b]
            ).wait()

    size = blocks * domain * domain * 2
    return pl.pallas_call(
        body,
        out_shape=[jax.ShapeDtypeStruct((cap, domain, domain), jnp.bfloat16)] * (rows - 1),
        in_specs=[pl.BlockSpec(memory_space=SMEM)] * (rows + 1)
        + [pl.BlockSpec(memory_space=ANY)] * len(stores),
        out_specs=[pl.BlockSpec(memory_space=ANY)] * (rows - 1),
        scratch_shapes=[
            pltpu.VMEM((blocks, domain, domain), jnp.bfloat16),
            pltpu.SMEM((blocks,), jnp.int32),
            pltpu.SemaphoreType.DMA((blocks,)),
            pltpu.SemaphoreType.DMA((blocks,)),
        ],
        cost_estimate=pl.CostEstimate(flops=0, transcendentals=0, bytes_accessed=2 * size),
        name="gather_sends",
    )(place, where, *requests, *stores)


def prepare(own, at, shift, spread, stores, integrals, fock_matrix):
    half = own.shape[0]
    domain = integrals.shape[1]
    total = spread.shape[1] // LANES
    groups = domain // LANES // half
    strip = groups * LANES

    def body(own_ref, at_ref, shift_ref, spread_ref, *refs):
        sources = refs[: len(stores)]
        integ_ref, fock_ref, local_ref, rest_ref, across_ref, down_ref = refs[len(stores) :]
        i = pl.program_id(0)
        for g in range(groups):
            rows = pl.ds(pl.multiple_of(i * strip + g * LANES, LANES), LANES)
            part = [s[:, rows, :].reshape(s.shape[0] * LANES, domain) for s in sources]
            part = part[0] if len(part) == 1 else jnp.concatenate(part, axis=0)
            sums = jnp.dot(spread_ref[...], part, preferred_element_type=jnp.float32)
            local_ref[:, g * LANES : (g + 1) * LANES, :] = sums.reshape(half, LANES, domain)
        amps = sources[0][at_ref[i]]
        fock = fock_ref[0]
        wide = amps.astype(jnp.float32)
        left = jnp.dot(fock, amps, preferred_element_type=jnp.float32)
        right = jnp.dot(amps, fock, preferred_element_type=jnp.float32)
        row_id = lax.broadcasted_iota(jnp.int32, (domain, domain), 0)
        col_id = lax.broadcasted_iota(jnp.int32, (domain, domain), 1)
        diagonal = jnp.where(row_id == col_id, fock.astype(jnp.float32), 0.0)
        across = jnp.sum(diagonal, axis=0, keepdims=True)
        down = jnp.sum(diagonal, axis=1, keepdims=True)
        across_ref[0] = across
        down_ref[0] = down
        residual = integ_ref[0].astype(jnp.float32) + left + right - shift_ref[i] * wide
        rest_ref[0] = wide - residual / (down + across - shift_ref[i])

    block = (1, domain, domain)
    mine = pl.BlockSpec(block, lambda i, own, *_: (own[i], 0, 0))
    in_turn = pl.BlockSpec(block, lambda i, *_: (i, 0, 0))
    shape = jax.ShapeDtypeStruct
    return pl.pallas_call(
        body,
        grid_spec=pltpu.PrefetchScalarGridSpec(
            num_scalar_prefetch=3,
            grid=(half,),
            in_specs=[pl.BlockSpec(spread.shape, lambda i, *_: (0, 0))]
            + [pl.BlockSpec(s.shape, lambda i, *_: (0, 0, 0)) for s in stores]
            + [mine, mine],
            out_specs=[
                pl.BlockSpec((half, strip, domain), lambda i, *_: (0, i, 0)),
                in_turn,
                pl.BlockSpec((1, 1, domain), lambda i, *_: (i, 0, 0)),
                pl.BlockSpec((1, domain, 1), lambda i, *_: (i, 0, 0)),
            ],
        ),
        out_shape=[
            shape((half, domain, domain), jnp.float32),
            shape((half, domain, domain), jnp.float32),
            shape((half, 1, domain), jnp.float32),
            shape((half, domain, 1), jnp.float32),
        ],
        cost_estimate=pl.CostEstimate(
            flops=2 * half * domain**3 * 3,
            transcendentals=0,
            bytes_accessed=(total + 2 * half) * domain * domain * 2 + half * domain * domain * 8,
        ),
        name="prepare",
    )(own, at, shift, spread, *stores, integrals, fock_matrix)


def finish(own, shift, far_scale, far_shift, far_place, first, second, prepared, intersection,
           arrived, stores, slots, occ_count):
    local, rest, across, down = prepared
    half = own.shape[0]
    domain = intersection.shape[1]
    depth = stores[0].shape[0]
    remote = len(arrived)
    last = slots is not None

    def body(own_ref, shift_ref, scale_ref, from_ref, place_ref, first_ref, second_ref, *refs):
        local_ref, rest_ref, across_ref, down_ref, over_ref = refs[:5]
        sources = refs[5 : 5 + remote + len(stores)]
        outs = refs[5 + remote + len(stores) : -2]
        hold, sem = refs[-2:]
        i = pl.program_id(0)

        @pl.when(i == 0)
        def _():
            for n in range(half):
                for d in range(remote):

                    @pl.when(from_ref[n] == d + 1)
                    def _(n=n, d=d):
                        pltpu.make_async_copy(
                            sources[d].at[place_ref[n]], hold.at[n], sem.at[n]
                        ).start()

                for s in range(len(stores)):

                    @pl.when((from_ref[n] == 0) & (place_ref[n] // depth == s))
                    def _(n=n, s=s):
                        pltpu.make_async_copy(
                            sources[remote + s].at[place_ref[n] % depth], hold.at[n], sem.at[n]
                        ).start()

        pltpu.make_async_copy(sources[-1].at[0], hold.at[i], sem.at[i]).wait()
        coupled = (local_ref[0] + scale_ref[i] * hold[i].astype(jnp.float32)).astype(jnp.bfloat16)
        over = over_ref[0]
        projected = jnp.dot(over, coupled, preferred_element_type=jnp.float32)
        back = lax.dot_general(
            projected.astype(jnp.bfloat16),
            over,
            (((1,), (1,)), ((), ())),
            preferred_element_type=jnp.float32,
        )
        denominator = down_ref[0] + across_ref[0] - shift_ref[i]
        fresh = (rest_ref[0] + back / denominator).astype(jnp.bfloat16)
        outs[0][0] = fresh
        if last:
            outs[1][0] = fresh
            wide = fresh.astype(jnp.float32)
            square = jnp.dot(fresh, fresh, preferred_element_type=jnp.float32)
            row_id = lax.broadcasted_iota(jnp.int32, (domain, domain), 0)
            col_id = lax.broadcasted_iota(jnp.int32, (domain, domain), 1)
            terms = 2.0 * wide * wide - jnp.where(row_id == col_id, square, 0.0)
            norm = jnp.sum(jnp.sum(terms, axis=0, keepdims=True), axis=1, keepdims=True)
            orbital = lax.broadcasted_iota(jnp.int32, (1, occ_count), 1)
            picks = (orbital == first_ref[i]).astype(jnp.float32)
            picks = picks + (orbital == second_ref[i]).astype(jnp.float32)

            @pl.when(i == 0)
            def _():
                outs[2][...] = jnp.zeros_like(outs[2])

            outs[2][...] += norm * picks

    block = (1, domain, domain)
    mine = pl.BlockSpec(block, lambda i, own, *_: (own[i], 0, 0))
    in_turn = pl.BlockSpec(block, lambda i, *_: (i, 0, 0))
    shape = jax.ShapeDtypeStruct
    out_specs = [in_turn]
    out_shape = [shape((half, domain, domain), jnp.bfloat16)]
    if last:
        out_specs += [mine, pl.BlockSpec((1, occ_count), lambda i, *_: (0, 0))]
        out_shape += [
            shape((slots, domain, domain), jnp.bfloat16),
            shape((1, occ_count), jnp.float32),
        ]
    return pl.pallas_call(
        body,
        grid_spec=pltpu.PrefetchScalarGridSpec(
            num_scalar_prefetch=7,
            grid=(half,),
            in_specs=[
                in_turn,
                in_turn,
                pl.BlockSpec((1, 1, domain), lambda i, *_: (i, 0, 0)),
                pl.BlockSpec((1, domain, 1), lambda i, *_: (i, 0, 0)),
                mine,
            ]
            + [pl.BlockSpec(memory_space=ANY)] * (remote + len(stores)),
            out_specs=out_specs,
            scratch_shapes=[
                pltpu.VMEM((half, domain, domain), jnp.bfloat16),
                pltpu.SemaphoreType.DMA((half,)),
            ],
        ),
        out_shape=out_shape,
        cost_estimate=pl.CostEstimate(
            flops=2 * half * domain**3 * 2,
            transcendentals=0,
            bytes_accessed=half * domain * domain * 14,
        ),
        name="finish",
    )(own, shift, far_scale, far_shift, far_place, first, second, local, rest, across, down,
      intersection, *arrived, *stores)


def place_rest(other, blocks, whole):
    half, domain = blocks.shape[:2]

    def body(other_ref, blocks_ref, whole_ref, out_ref, hold, in_sem, out_sem):
        copies_in = [
            pltpu.make_async_copy(blocks_ref.at[n], hold.at[n], in_sem.at[n]) for n in range(half)
        ]
        copies_out = [
            pltpu.make_async_copy(hold.at[n], out_ref.at[other_ref[n]], out_sem.at[n])
            for n in range(half)
        ]
        for copy in copies_in:
            copy.start()
        for n in range(half):
            copies_in[n].wait()
            copies_out[n].start()
        for copy in copies_out:
            copy.wait()

    return pl.pallas_call(
        body,
        out_shape=jax.ShapeDtypeStruct(whole.shape, whole.dtype),
        in_specs=[pl.BlockSpec(memory_space=SMEM)] + [pl.BlockSpec(memory_space=ANY)] * 2,
        out_specs=pl.BlockSpec(memory_space=ANY),
        scratch_shapes=[
            pltpu.VMEM(blocks.shape, blocks.dtype),
            pltpu.SemaphoreType.DMA((half,)),
            pltpu.SemaphoreType.DMA((half,)),
        ],
        input_output_aliases={2: 0},
        cost_estimate=pl.CostEstimate(
            flops=0, transcendentals=0, bytes_accessed=half * domain * domain * 4
        ),
        name="place_rest",
    )(other, blocks, whole)


def add_all(values, axes):
    for name in axes:
        size = lax.axis_size(name)
        if size & (size - 1):
            values = lax.psum(values, name)
            continue
        step = 1
        while step < size:
            values = values + lax.ppermute(values, name, [(r, r ^ step) for r in range(size)])
            step *= 2
    return values


def per_device(
    amplitudes,
    integrals,
    fock_matrix,
    intersection,
    occ_energy,
    first_occ,
    second_occ,
    near_slot,
    near_count,
    near_weight,
    far_chip,
    far_slot,
    far_weight,
):
    pairs, domain = amplitudes.shape[:2]
    rows = lax.axis_size("row")
    half = pairs // 2
    cap = pairs // rows
    row = lax.axis_index("row")
    core = lax.axis_index("rep")
    occ_count = occ_energy.shape[0]
    slot_ids = jnp.arange(pairs, dtype=jnp.int32)
    source = far_chip[:, 0]
    packed = source * pairs + far_slot[:, 0]
    requests = [lax.ppermute(packed, "row", rotation(rows, d)) for d in range(1, rows)]

    same = source[:, None] == source[None, :]
    before = (source[None, :] < source[:, None]) | (same & (slot_ids[None, :] < slot_ids[:, None]))
    turn = jnp.sum(before.astype(jnp.int32), axis=1)
    like = same & (turn[:, None] % 2 == turn[None, :] % 2) & (turn[None, :] < turn[:, None])
    place = jnp.sum(like.astype(jnp.int32), axis=1)
    mine = jnp.arange(half, dtype=jnp.int32) * 2 + core
    own_pick = mine[:, None] == turn[None, :]
    other_pick = (mine ^ 1)[:, None] == turn[None, :]

    def pick(chosen, values):
        return jnp.sum(jnp.where(chosen, values[None, :], jnp.zeros((), values.dtype)), axis=1)

    own = pick(own_pick, slot_ids)
    other = pick(other_pick, slot_ids)
    far_shift = pick(own_pick, (source - row) % rows)
    own_far = pick(own_pick, far_slot[:, 0])
    own_place = pick(own_pick, place)
    far_scale = pick(own_pick, far_weight[:, 0].astype(jnp.float32))
    first = pick(own_pick, first_occ)
    second = pick(own_pick, second_occ)
    orbitals = jnp.arange(occ_count, dtype=jnp.int32)

    def energy_of(index):
        found = index[:, None] == orbitals[None, :]
        return jnp.sum(jnp.where(found, occ_energy[None, :], jnp.float32(0.0)), axis=1)

    shift = energy_of(first) + energy_of(second)

    near_pos = jnp.arange(near_slot.shape[1], dtype=jnp.int32)
    alive = near_pos[None, :] < near_count[:, None]
    matches = (near_slot[:, :, None] == slot_ids[None, None, :]) & alive[:, :, None]
    weights = jnp.sum(
        jnp.where(matches, near_weight.astype(jnp.float32)[:, :, None], jnp.float32(0.0)), axis=1
    ).astype(jnp.bfloat16)

    def choose(chosen, table):
        spread = jnp.where(chosen[:, :, None], table[None], jnp.zeros((), table.dtype))
        return jnp.sum(spread.astype(jnp.float32), axis=1).astype(table.dtype)

    own_weights = choose(own_pick, weights)
    by_core = jnp.concatenate([choose(own_pick, own_weights.T).T, choose(other_pick, own_weights.T).T], axis=1)
    lane = jnp.arange(LANES)
    unit = lane[:, None] == lane[None, :]

    def spread_of(table):
        grid = jnp.where(
            unit[None, :, None, :], table[:, None, :, None], jnp.zeros((), table.dtype)
        )
        return grid.reshape(half * LANES, pairs * LANES)

    here = jnp.stack([row, core]).astype(jnp.int32)
    by_slot = turn // 2 + jnp.where(turn % 2 == core, 0, half)

    stores = (amplitudes,)
    where = slot_ids
    at = own
    spread = spread_of(own_weights)
    for sweep in range(ITERS):
        last = sweep == ITERS - 1
        sends = gather_sends(requests, here, where, stores, rows, cap)
        arrived = [
            lax.ppermute(block, "row", rotation(rows, -d)) for d, block in enumerate(sends, 1)
        ]
        prepared = prepare(own, at, shift, spread, stores, integrals, fock_matrix)
        far_place = jnp.where(far_shift == 0, pick_where(own_far, where), own_place)
        done = finish(own, shift, far_scale, far_shift, far_place, first, second, prepared,
                      intersection, arrived, stores, pairs if last else None, occ_count)
        given = lax.ppermute(done[0], "rep", [(0, 1), (1, 0)])
        if last:
            final = place_rest(other, given, done[1])
            occ_sum = add_all(done[2][0], ("rep", "col", "row"))
        else:
            stores = (done[0], given)
            where = by_slot
            at = jnp.arange(half, dtype=jnp.int32)
            spread = spread_of(by_core)
    total_pairs = pairs * rows * lax.axis_size("col")
    occ_density = occ_sum * (occ_count / (2.0 * total_pairs * domain * domain))
    return (final, occ_density)


def pick_where(index, table):
    ids = jnp.arange(table.shape[0], dtype=jnp.int32)
    return jnp.sum(jnp.where(index[:, None] == ids[None, :], table[None, :], 0), axis=1)


def solution(mesh):
    pair_spec = P(("groups", "row", "col"), None, None)
    flat = P(("groups", "row", "col"))
    table = P(("groups", "row", "col"), None)
    return jax.shard_map(
        per_device,
        mesh=mesh,
        in_specs=(
            pair_spec, pair_spec, pair_spec, pair_spec,
            P("groups"), flat, flat, table, flat, table, table, table, table,
        ),
        out_specs=(pair_spec, P("groups")),
        check_vma=False,
    )
```

```python
import jax
import jax.numpy as jnp
from jax import lax
from jax.experimental import pallas as pl
from jax.experimental.pallas import tpu as pltpu
from jax.sharding import PartitionSpec as P

ITERS = 2
ANY = pl.ANY
SMEM = pltpu.SMEM
VMEM = pltpu.VMEM
LANES = 16
MIB = 1 << 20


def exchanges(rows, shift):
    if rows & (rows - 1):
        return [(r, (r - shift) % rows) for r in range(rows)]
    return [(r, r ^ shift) for r in range(rows)]


def returns(rows, shift):
    return [(b, a) for a, b in exchanges(rows, shift)]


def apart(rows, source, row):
    if rows & (rows - 1):
        return (row - source) % rows
    return source ^ row


def limits(mib):
    return pltpu.CompilerParams(vmem_limit_bytes=mib * MIB)


def cost(flops, size):
    return pl.CostEstimate(flops=flops, transcendentals=0, bytes_accessed=size)


def fetch(candidates, spot, target, sem):
    for offset, ref in candidates:

        @pl.when((spot >= offset) & (spot < offset + ref.shape[0]))
        def _(offset=offset, ref=ref):
            pltpu.make_async_copy(ref.at[spot - offset], target, sem).start()


def laid(refs, offset=0):
    placed = []
    for ref in refs:
        placed.append((offset, ref))
        offset += ref.shape[0]
    return placed


def gather_first(requests, place, amplitudes, rows, cap):
    pairs, domain = amplitudes.shape[:2]
    blocks = (rows - 1) * cap

    def body(place_ref, *refs):
        lists = refs[: rows - 1]
        store = refs[rows - 1]
        asked = refs[rows]
        outs = refs[rows + 1 : 2 * rows]
        sem = refs[-1]
        me = place_ref[0]
        core = place_ref[1]
        for b in range(blocks):
            asked[b] = 0
        for shift in range(1, rows):
            asker = apart(rows, me, shift) if rows & (rows - 1) == 0 else (me + shift) % rows
            sources = [lists[shift - 1][p] // pairs for p in range(pairs)]
            count = jnp.int32(0)
            for p in range(pairs):
                count = count + (apart(rows, sources[p], asker) < shift).astype(jnp.int32)
            filled = jnp.int32((shift - 1) * cap)
            for p in range(pairs):
                mine = sources[p] == me
                taken = mine & (count % 2 == core)

                @pl.when(taken)
                def _(filled=filled, p=p, shift=shift):
                    asked[filled] = lists[shift - 1][p] % pairs

                count = count + mine.astype(jnp.int32)
                filled = jnp.minimum(filled + taken.astype(jnp.int32), shift * cap - 1)
            for k in range(cap):
                b = (shift - 1) * cap + k
                pltpu.make_async_copy(
                    store.at[asked[b]], outs[shift - 1].at[k], sem.at[b]
                ).start()
        for b in range(blocks):
            pltpu.make_async_copy(store.at[0], outs[b // cap].at[b % cap], sem.at[b]).wait()

    shape = (cap, domain, domain)
    return pl.pallas_call(
        body,
        out_shape=[jax.ShapeDtypeStruct((blocks,), jnp.int32)]
        + [VMEM(shape, jnp.bfloat16)] * (rows - 1),
        in_specs=[pl.BlockSpec(memory_space=SMEM)] * rows + [pl.BlockSpec(memory_space=ANY)],
        out_specs=[pl.BlockSpec(memory_space=SMEM)]
        + [pl.BlockSpec(memory_space=VMEM)] * (rows - 1),
        scratch_shapes=[pltpu.SemaphoreType.DMA((blocks,))],
        cost_estimate=cost(0, blocks * domain * domain * 4),
        compiler_params=limits(8),
        name="gather_first",
    )(place, *requests, amplitudes)


def gather_again(asked, where, stores, rows, cap):
    domain = stores[0].shape[1]
    blocks = (rows - 1) * cap

    def body(asked_ref, where_ref, *refs):
        sources = laid(refs[: len(stores)])
        outs = refs[len(stores) : len(stores) + rows - 1]
        sem = refs[-1]
        for b in range(blocks):
            fetch(sources, where_ref[asked_ref[b]], outs[b // cap].at[b % cap], sem.at[b])
        for b in range(blocks):
            pltpu.make_async_copy(
                sources[0][1].at[0], outs[b // cap].at[b % cap], sem.at[b]
            ).wait()

    return pl.pallas_call(
        body,
        out_shape=[VMEM((cap, domain, domain), jnp.bfloat16)] * (rows - 1),
        in_specs=[pl.BlockSpec(memory_space=SMEM)] * 2
        + [pl.BlockSpec(memory_space=ANY)] * len(stores),
        out_specs=[pl.BlockSpec(memory_space=VMEM)] * (rows - 1),
        scratch_shapes=[pltpu.SemaphoreType.DMA((blocks,))],
        cost_estimate=cost(0, blocks * domain * domain * 4),
        compiler_params=limits(8),
        name="gather_again",
    )(asked, where, *stores)


def prepare(own, at, shift, spread, stores, integrals, fock_matrix, intersection):
    half = own.shape[0]
    domain = integrals.shape[1]
    total = spread.shape[1] // LANES
    groups = domain // LANES // half
    strip = groups * LANES

    def body(own_ref, at_ref, shift_ref, spread_ref, *refs):
        sources = refs[: len(stores)]
        integ_ref, fock_ref, over_ref, local_ref, rest_ref, recip_ref, keep_ref = refs[len(stores) :]
        i = pl.program_id(0)
        for g in range(groups):
            rows = pl.ds(pl.multiple_of(i * strip + g * LANES, LANES), LANES)
            part = [s[:, rows, :].reshape(s.shape[0] * LANES, domain) for s in sources]
            part = part[0] if len(part) == 1 else jnp.concatenate(part, axis=0)
            sums = jnp.dot(spread_ref[...], part, preferred_element_type=jnp.float32)
            local_ref[:, g * LANES : (g + 1) * LANES, :] = sums.reshape(half, LANES, domain)
        amps = sources[0][at_ref[i]]
        fock = fock_ref[0]
        wide = amps.astype(jnp.float32)
        left = jnp.dot(fock, amps, preferred_element_type=jnp.float32)
        right = jnp.dot(amps, fock, preferred_element_type=jnp.float32)
        row_id = lax.broadcasted_iota(jnp.int32, (domain, domain), 0)
        col_id = lax.broadcasted_iota(jnp.int32, (domain, domain), 1)
        diagonal = jnp.where(row_id == col_id, fock.astype(jnp.float32), 0.0)
        across = jnp.sum(diagonal, axis=0, keepdims=True)
        down = jnp.sum(diagonal, axis=1, keepdims=True)
        residual = integ_ref[0].astype(jnp.float32) + left + right - shift_ref[i] * wide
        recip = 1.0 / (down + across - shift_ref[i])
        recip_ref[0] = recip
        rest_ref[0] = wide - residual * recip
        keep_ref[0] = over_ref[0]

    block = (1, domain, domain)
    mine = pl.BlockSpec(block, lambda i, own, *_: (own[i], 0, 0))
    in_turn = pl.BlockSpec(block, lambda i, *_: (i, 0, 0))
    wide_shape = jax.ShapeDtypeStruct((half, domain, domain), jnp.float32)
    return pl.pallas_call(
        body,
        grid_spec=pltpu.PrefetchScalarGridSpec(
            num_scalar_prefetch=3,
            grid=(half,),
            in_specs=[pl.BlockSpec(spread.shape, lambda i, *_: (0, 0))]
            + [pl.BlockSpec(s.shape, lambda i, *_: (0, 0, 0)) for s in stores]
            + [mine, mine, mine],
            out_specs=[
                pl.BlockSpec((half, strip, domain), lambda i, *_: (0, i, 0)),
                in_turn,
                in_turn,
                in_turn,
            ],
        ),
        out_shape=[
            wide_shape,
            wide_shape,
            wide_shape,
            jax.ShapeDtypeStruct((half, domain, domain), jnp.bfloat16),
        ],
        cost_estimate=cost(
            2 * half * domain**3 * 3,
            (total + 4 * half) * domain * domain * 2 + half * domain * domain * 12,
        ),
        compiler_params=limits(20),
        name="prepare",
    )(own, at, shift, spread, *stores, integrals, fock_matrix, intersection)


def finish(start, count, numbers, scale, prepared, arrived, stores, occ_count, last):
    half, domain = prepared[0].shape[:2]

    def body(number_ref, scale_ref, local_ref, rest_ref, recip_ref, over_ref, *refs):
        candidates = [
            (offset, ref) for offset, ref in zip([o for o, _ in arrived + stores], refs)
        ]
        outs = refs[len(candidates) : -2]
        hold, sem = refs[-2:]
        for n in range(count):
            fetch(candidates, number_ref[start + n], hold.at[n], sem.at[n])
        if last:
            row_id = lax.broadcasted_iota(jnp.int32, (domain, domain), 0)
            col_id = lax.broadcasted_iota(jnp.int32, (domain, domain), 1)
            on_diagonal = row_id == col_id
            orbital = lax.broadcasted_iota(jnp.int32, (1, occ_count), 1)
            density = jnp.zeros((1, occ_count), jnp.float32)
        for n in range(count):
            pltpu.make_async_copy(candidates[0][1].at[0], hold.at[n], sem.at[n]).wait()
        for n in range(count):
            i = start + n
            coupled = local_ref[i] + scale_ref[i] * hold[n].astype(jnp.float32)
            over = over_ref[i]
            projected = jnp.dot(
                over, coupled.astype(jnp.bfloat16), preferred_element_type=jnp.float32
            )
            back = lax.dot_general(
                projected.astype(jnp.bfloat16),
                over,
                (((1,), (1,)), ((), ())),
                preferred_element_type=jnp.float32,
            )
            fresh = (rest_ref[i] + back * recip_ref[i]).astype(jnp.bfloat16)
            outs[0][n] = fresh
            if last:
                wide = fresh.astype(jnp.float32)
                square = jnp.dot(fresh, fresh, preferred_element_type=jnp.float32)
                terms = 2.0 * wide * wide - jnp.where(on_diagonal, square, 0.0)
                norm = jnp.sum(jnp.sum(terms, axis=0, keepdims=True), axis=1, keepdims=True)
                picks = (orbital == number_ref[half + i]).astype(jnp.float32)
                picks = picks + (orbital == number_ref[2 * half + i]).astype(jnp.float32)
                density = density + norm * picks
        if last:
            outs[1][...] = density

    out_shape = [VMEM((count, domain, domain), jnp.bfloat16)]
    if last:
        out_shape.append(VMEM((1, occ_count), jnp.float32))
    return pl.pallas_call(
        body,
        out_shape=out_shape,
        in_specs=[pl.BlockSpec(memory_space=SMEM)] * 2
        + [pl.BlockSpec(memory_space=VMEM)] * 4
        + [pl.BlockSpec(memory_space=ANY)] * len(arrived + stores),
        out_specs=[pl.BlockSpec(memory_space=VMEM)] * len(out_shape),
        scratch_shapes=[
            VMEM((count, domain, domain), jnp.bfloat16),
            pltpu.SemaphoreType.DMA((count,)),
        ],
        cost_estimate=cost(2 * count * domain**3 * 2, count * domain * domain * 18),
        compiler_params=limits(16),
        name="finish",
    )(numbers, scale, *prepared, *[a for _, a in arrived + stores])


def put_in_slots(slots, stores):
    domain = stores[0].shape[1]
    total = slots.shape[0]

    def body(slot_ref, *refs):
        sources = refs[: len(stores)]
        out_ref, sem = refs[-2:]
        copies = []
        for source in sources:
            for n in range(source.shape[0]):
                at = len(copies)
                copies.append(
                    pltpu.make_async_copy(source.at[n], out_ref.at[slot_ref[at]], sem.at[at])
                )
        for copy in copies:
            copy.start()
        for copy in copies:
            copy.wait()

    return pl.pallas_call(
        body,
        out_shape=jax.ShapeDtypeStruct((total, domain, domain), jnp.bfloat16),
        in_specs=[pl.BlockSpec(memory_space=SMEM)]
        + [pl.BlockSpec(memory_space=VMEM)] * len(stores),
        out_specs=pl.BlockSpec(memory_space=ANY),
        scratch_shapes=[pltpu.SemaphoreType.DMA((total,))],
        cost_estimate=cost(0, total * domain * domain * 4),
        compiler_params=limits(8),
        name="put_in_slots",
    )(slots, *stores)


def add_over(values, name):
    size = lax.axis_size(name)
    if size & (size - 1):
        return lax.psum(values, name)
    step = 1
    while step < size:
        values = values + lax.ppermute(values, name, [(r, r ^ step) for r in range(size)])
        step *= 2
    return values


def per_device(
    amplitudes,
    integrals,
    fock_matrix,
    intersection,
    occ_energy,
    first_occ,
    second_occ,
    near_slot,
    near_count,
    near_weight,
    far_chip,
    far_slot,
    far_weight,
):
    pairs, domain = amplitudes.shape[:2]
    rows = lax.axis_size("row")
    half = pairs // 2
    cap = pairs // rows
    row = lax.axis_index("row")
    core = lax.axis_index("rep")
    occ_count = occ_energy.shape[0]
    slot_ids = jnp.arange(pairs, dtype=jnp.int32)
    source = far_chip[:, 0]
    packed = source * pairs + far_slot[:, 0]
    requests = [lax.ppermute(packed, "row", exchanges(rows, d)) for d in range(1, rows)]
    here = jnp.stack([row, core]).astype(jnp.int32)
    asked, *sends = gather_first(requests, here, amplitudes, rows, cap)

    step = apart(rows, source, row)
    same = step[:, None] == step[None, :]
    before = (step[None, :] < step[:, None]) | (same & (slot_ids[None, :] < slot_ids[:, None]))
    turn = jnp.sum(before.astype(jnp.int32), axis=1)
    like = same & (turn[:, None] % 2 == turn[None, :] % 2) & (turn[None, :] < turn[:, None])
    place = jnp.sum(like.astype(jnp.int32), axis=1)
    mine = jnp.arange(half, dtype=jnp.int32) * 2 + core
    own_pick = mine[:, None] == turn[None, :]
    other_pick = (mine ^ 1)[:, None] == turn[None, :]

    def pick(chosen, values):
        return jnp.sum(jnp.where(chosen, values[None, :], jnp.zeros((), values.dtype)), axis=1)

    own = pick(own_pick, slot_ids)
    other = pick(other_pick, slot_ids)
    far_step = pick(own_pick, step)
    own_far = pick(own_pick, far_slot[:, 0])
    own_place = pick(own_pick, place)
    far_scale = pick(own_pick, far_weight[:, 0].astype(jnp.float32))
    first = pick(own_pick, first_occ)
    second = pick(own_pick, second_occ)
    orbitals = jnp.arange(occ_count, dtype=jnp.int32)

    def energy_of(index):
        found = index[:, None] == orbitals[None, :]
        return jnp.sum(jnp.where(found, occ_energy[None, :], jnp.float32(0.0)), axis=1)

    shift = energy_of(first) + energy_of(second)

    near_pos = jnp.arange(near_slot.shape[1], dtype=jnp.int32)
    alive = near_pos[None, :] < near_count[:, None]
    matches = (near_slot[:, :, None] == slot_ids[None, None, :]) & alive[:, :, None]
    weights = jnp.sum(
        jnp.where(matches, near_weight.astype(jnp.float32)[:, :, None], jnp.float32(0.0)), axis=1
    ).astype(jnp.bfloat16)

    def choose(chosen, table):
        spread = jnp.where(chosen[:, :, None], table[None], jnp.zeros((), table.dtype))
        return jnp.sum(spread.astype(jnp.float32), axis=1).astype(table.dtype)

    own_weights = choose(own_pick, weights)
    by_core = jnp.concatenate(
        [choose(own_pick, own_weights.T).T, choose(other_pick, own_weights.T).T], axis=1
    )
    lane = jnp.arange(LANES)
    unit = lane[:, None] == lane[None, :]

    def spread_of(table):
        grid = jnp.where(
            unit[None, :, None, :], table[:, None, :, None], jnp.zeros((), table.dtype)
        )
        return grid.reshape(half * LANES, pairs * LANES)

    by_slot = turn // 2 + jnp.where(turn % 2 == core, 0, half)
    early = half - cap
    swap = [(0, 1), (1, 0)]
    remote = (rows - 1) * cap
    local_spots = [
        slot_ids,
        jnp.where(
            by_slot < half,
            by_slot + jnp.where(by_slot % half < early, 0, early),
            by_slot - half + jnp.where(by_slot % half < early, early, half),
        ),
    ]
    tables = []
    for where in local_spots:
        at_home = remote + jnp.sum(
            jnp.where(own_far[:, None] == slot_ids[None, :], where[None, :], 0), axis=1
        )
        spot = jnp.where(far_step == 0, at_home, (far_step - 1) * cap + own_place)
        tables.append(jnp.concatenate([spot, first, second]))
    spreads = [spread_of(own_weights), spread_of(by_core)]
    ats = [own, jnp.arange(half, dtype=jnp.int32)]
    slots = jnp.concatenate([own[:early], other[:early], own[early:], other[early:]])
    (own, shift, far_scale, *moved) = lax.optimization_barrier(
        (own, shift, far_scale, *tables, *spreads, *ats, slots, *sends)
    )
    tables, spreads, ats, slots = moved[:2], moved[2:4], moved[4:6], moved[6]

    stores = [amplitudes]
    whole = [amplitudes]
    for sweep in range(ITERS):
        last = sweep == ITERS - 1
        late = min(sweep, 1)
        if sweep > 0:
            sends = gather_again(asked, local_spots[late], stores, rows, cap)
        arrived = [
            lax.ppermute(block, "row", returns(rows, d)) for d, block in enumerate(sends, 1)
        ]
        prepared = prepare(
            own, ats[late], shift, spreads[late], whole, integrals, fock_matrix, intersection
        )
        spots = laid(arrived)
        homes = laid(stores, remote)
        done_early = finish(
            0, early, tables[late], far_scale, prepared, spots[:-1], homes, occ_count, last
        )
        given_early = lax.ppermute(done_early[0], "rep", swap)
        done_late = finish(
            early, cap, tables[late], far_scale, prepared, spots, homes, occ_count, last
        )
        given_late = lax.ppermute(done_late[0], "rep", swap)
        stores = [done_early[0], given_early, done_late[0], given_late]
        whole = [
            jnp.concatenate([done_early[0], done_late[0]], axis=0),
            jnp.concatenate([given_early, given_late], axis=0),
        ]
    final = put_in_slots(slots, stores)
    occ_sum = (done_early[1] + done_late[1])[0]
    occ_sum = add_over(add_over(occ_sum, "rep"), "col")
    occ_sum, final = lax.optimization_barrier((occ_sum, final))
    occ_sum = add_over(occ_sum, "row")
    total_pairs = pairs * rows * lax.axis_size("col")
    occ_density = occ_sum * (occ_count / (2.0 * total_pairs * domain * domain))
    return (final, occ_density)


def solution(mesh):
    pair_spec = P(("groups", "row", "col"), None, None)
    flat = P(("groups", "row", "col"))
    table = P(("groups", "row", "col"), None)
    return jax.shard_map(
        per_device,
        mesh=mesh,
        in_specs=(
            pair_spec, pair_spec, pair_spec, pair_spec,
            P("groups"), flat, flat, table, flat, table, table, table, table,
        ),
        out_specs=(pair_spec, P("groups")),
        check_vma=False,
    )
```

```python
import jax
import jax.numpy as jnp
from jax import lax
from jax.experimental import pallas as pl
from jax.experimental.pallas import tpu as pltpu
from jax.sharding import PartitionSpec as P


ITERS = 2
ANY = pl.ANY
SMEM = pltpu.SMEM
VMEM = pltpu.VMEM
LANES = 16
MIB = 1 << 20


def exchanges(rows, shift):
    if rows & (rows - 1):
        return [(r, (r - shift) % rows) for r in range(rows)]
    return [(r, r ^ shift) for r in range(rows)]


def returns(rows, shift):
    return [(b, a) for a, b in exchanges(rows, shift)]


def apart(rows, source, row):
    if rows & (rows - 1):
        return (row - source) % rows
    return source ^ row


def limits(mib):
    return pltpu.CompilerParams(vmem_limit_bytes=mib * MIB)


def cost(flops, size):
    return pl.CostEstimate(flops=flops, transcendentals=0, bytes_accessed=size)


def fetch(candidates, spot, target):
    for offset, ref in candidates:

        @pl.when((spot >= offset) & (spot < offset + ref.shape[0]))
        def _(offset=offset, ref=ref):
            target[...] = ref[spot - offset]


def laid(refs, offset=0):
    placed = []
    for ref in refs:
        placed.append((offset, ref))
        offset += ref.shape[0]
    return placed


def gather_first(requests, place, amplitudes, rows, cap):
    pairs, domain = amplitudes.shape[:2]
    blocks = (rows - 1) * cap

    def body(place_ref, *refs):
        lists = refs[: rows - 1]
        store = refs[rows - 1]
        asked = refs[rows]
        outs = refs[rows + 1 :]
        me = place_ref[0]
        core = place_ref[1]
        for shift in range(1, rows):
            base = (shift - 1) * (cap + 1)
            asker = apart(rows, me, shift) if rows & (rows - 1) == 0 else (me + shift) % rows
            for k in range(cap):
                asked[base + k] = 0
            sources = [lists[shift - 1][p] // pairs for p in range(pairs)]
            count = jnp.int32(0)
            for p in range(pairs):
                count = count + (apart(rows, sources[p], asker) < shift).astype(jnp.int32)
            filled = jnp.int32(0)
            for p in range(pairs):
                mine = sources[p] == me
                taken = mine & (count % 2 == core)
                asked[base + jnp.minimum(filled, cap)] = lists[shift - 1][p] % pairs
                count = count + mine.astype(jnp.int32)
                filled = filled + taken.astype(jnp.int32)
            for k in range(cap):
                outs[shift - 1][k] = store[asked[base + k]]

    shape = (cap, domain, domain)
    return pl.pallas_call(
        body,
        out_shape=[jax.ShapeDtypeStruct(((rows - 1) * (cap + 1),), jnp.int32)]
        + [VMEM(shape, jnp.bfloat16)] * (rows - 1),
        in_specs=[pl.BlockSpec(memory_space=SMEM)] * rows + [pl.BlockSpec(memory_space=VMEM)],
        out_specs=[pl.BlockSpec(memory_space=SMEM)]
        + [pl.BlockSpec(memory_space=VMEM)] * (rows - 1),
        cost_estimate=cost(0, blocks * domain * domain * 4),
        compiler_params=limits(8),
        name="gather_first",
    )(place, *requests, amplitudes)


def gather_again(asked, where, stores, rows, cap):
    domain = stores[0].shape[1]
    blocks = (rows - 1) * cap

    def body(asked_ref, where_ref, *refs):
        sources = laid(refs[: len(stores)])
        outs = refs[len(stores) :]
        for b in range(blocks):
            spot = where_ref[asked_ref[b // cap * (cap + 1) + b % cap]]
            fetch(sources, spot, outs[b // cap].at[b % cap])

    return pl.pallas_call(
        body,
        out_shape=[VMEM((cap, domain, domain), jnp.bfloat16)] * (rows - 1),
        in_specs=[pl.BlockSpec(memory_space=SMEM)] * 2
        + [pl.BlockSpec(memory_space=VMEM)] * len(stores),
        out_specs=[pl.BlockSpec(memory_space=VMEM)] * (rows - 1),
        cost_estimate=cost(0, blocks * domain * domain * 4),
        compiler_params=limits(8),
        name="gather_again",
    )(asked, where, *stores)


def prepare(own, at, shift, spread, stores, integrals, fock_matrix, intersection):
    half = own.shape[0]
    domain = integrals.shape[1]
    total = spread.shape[1] // LANES
    groups = domain // LANES // half
    strip = groups * LANES

    def body(own_ref, at_ref, shift_ref, spread_ref, *refs):
        sources = refs[: len(stores)]
        integ_ref, fock_ref, over_ref, local_ref, rest_ref, recip_ref, keep_ref = refs[len(stores) :]
        i = pl.program_id(0)
        for g in range(groups):
            rows = pl.ds(pl.multiple_of(i * strip + g * LANES, LANES), LANES)
            part = [s[:, rows, :].reshape(s.shape[0] * LANES, domain) for s in sources]
            part = part[0] if len(part) == 1 else jnp.concatenate(part, axis=0)
            sums = jnp.dot(spread_ref[...], part, preferred_element_type=jnp.float32)
            local_ref[:, g * LANES : (g + 1) * LANES, :] = sums.reshape(half, LANES, domain)
        amps = sources[0][at_ref[i]]
        fock = fock_ref[0]
        wide = amps.astype(jnp.float32)
        left = jnp.dot(fock, amps, preferred_element_type=jnp.float32)
        right = jnp.dot(amps, fock, preferred_element_type=jnp.float32)
        row_id = lax.broadcasted_iota(jnp.int32, (domain, domain), 0)
        col_id = lax.broadcasted_iota(jnp.int32, (domain, domain), 1)
        diagonal = jnp.where(row_id == col_id, fock.astype(jnp.float32), 0.0)
        across = jnp.sum(diagonal, axis=0, keepdims=True)
        down = jnp.sum(diagonal, axis=1, keepdims=True)
        residual = integ_ref[0].astype(jnp.float32) + left + right - shift_ref[i] * wide
        recip = 1.0 / (down + across - shift_ref[i])
        recip_ref[0] = recip
        rest_ref[0] = wide - residual * recip
        keep_ref[0] = over_ref[0]

    block = (1, domain, domain)
    mine = pl.BlockSpec(block, lambda i, own, *_: (own[i], 0, 0))
    in_turn = pl.BlockSpec(block, lambda i, *_: (i, 0, 0))
    wide_shape = jax.ShapeDtypeStruct((half, domain, domain), jnp.float32)
    return pl.pallas_call(
        body,
        grid_spec=pltpu.PrefetchScalarGridSpec(
            num_scalar_prefetch=3,
            grid=(half,),
            in_specs=[pl.BlockSpec(spread.shape, lambda i, *_: (0, 0))]
            + [pl.BlockSpec(s.shape, lambda i, *_: (0, 0, 0)) for s in stores]
            + [mine, mine, mine],
            out_specs=[
                pl.BlockSpec((half, strip, domain), lambda i, *_: (0, i, 0)),
                in_turn,
                in_turn,
                in_turn,
            ],
        ),
        out_shape=[
            wide_shape,
            wide_shape,
            wide_shape,
            jax.ShapeDtypeStruct((half, domain, domain), jnp.bfloat16),
        ],
        cost_estimate=cost(
            2 * half * domain**3 * 3,
            (total + 4 * half) * domain * domain * 2 + half * domain * domain * 12,
        ),
        compiler_params=limits(20),
        name="prepare",
    )(own, at, shift, spread, *stores, integrals, fock_matrix, intersection)


def finish(start, count, numbers, scale, prepared, arrived, stores, occ_count, last):
    half, domain = prepared[0].shape[:2]

    def body(number_ref, scale_ref, local_ref, rest_ref, recip_ref, over_ref, *refs):
        candidates = [
            (offset, ref) for offset, ref in zip([o for o, _ in arrived + stores], refs)
        ]
        outs = refs[len(candidates) : -1]
        hold = refs[-1]
        for n in range(count):
            fetch(candidates, number_ref[start + n], hold.at[n])
        if last:
            row_id = lax.broadcasted_iota(jnp.int32, (domain, domain), 0)
            col_id = lax.broadcasted_iota(jnp.int32, (domain, domain), 1)
            on_diagonal = row_id == col_id
            orbital = lax.broadcasted_iota(jnp.int32, (1, occ_count), 1)
            density = jnp.zeros((1, occ_count), jnp.float32)
        for n in range(count):
            i = start + n
            coupled = local_ref[i] + scale_ref[i] * hold[n].astype(jnp.float32)
            over = over_ref[i]
            projected = jnp.dot(
                over, coupled.astype(jnp.bfloat16), preferred_element_type=jnp.float32
            )
            back = lax.dot_general(
                projected.astype(jnp.bfloat16),
                over,
                (((1,), (1,)), ((), ())),
                preferred_element_type=jnp.float32,
            )
            fresh = (rest_ref[i] + back * recip_ref[i]).astype(jnp.bfloat16)
            outs[0][n] = fresh
            if last:
                wide = fresh.astype(jnp.float32)
                square = jnp.dot(fresh, fresh, preferred_element_type=jnp.float32)
                terms = 2.0 * wide * wide - jnp.where(on_diagonal, square, 0.0)
                norm = jnp.sum(jnp.sum(terms, axis=0, keepdims=True), axis=1, keepdims=True)
                picks = (orbital == number_ref[half + i]).astype(jnp.float32)
                picks = picks + (orbital == number_ref[2 * half + i]).astype(jnp.float32)
                density = density + norm * picks
        if last:
            outs[1][...] = density

    out_shape = [VMEM((count, domain, domain), jnp.bfloat16)]
    if last:
        out_shape.append(VMEM((1, occ_count), jnp.float32))
    return pl.pallas_call(
        body,
        out_shape=out_shape,
        in_specs=[pl.BlockSpec(memory_space=SMEM)] * 2
        + [pl.BlockSpec(memory_space=VMEM)] * 4
        + [pl.BlockSpec(memory_space=VMEM)] * len(arrived + stores),
        out_specs=[pl.BlockSpec(memory_space=VMEM)] * len(out_shape),
        scratch_shapes=[VMEM((count, domain, domain), jnp.bfloat16)],
        cost_estimate=cost(2 * count * domain**3 * 2, count * domain * domain * 18),
        compiler_params=limits(16),
        name="finish",
    )(numbers, scale, *prepared, *[a for _, a in arrived + stores])


def put_in_slots(slots, stores):
    domain = stores[0].shape[1]
    total = slots.shape[0]

    def body(slot_ref, *refs):
        sources = refs[: len(stores)]
        out_ref, sem = refs[-2:]
        copies = []
        for source in sources:
            for n in range(source.shape[0]):
                at = len(copies)
                copies.append(
                    pltpu.make_async_copy(source.at[n], out_ref.at[slot_ref[at]], sem.at[at])
                )
        for copy in copies:
            copy.start()
        for copy in copies:
            copy.wait()

    return pl.pallas_call(
        body,
        out_shape=jax.ShapeDtypeStruct((total, domain, domain), jnp.bfloat16),
        in_specs=[pl.BlockSpec(memory_space=SMEM)]
        + [pl.BlockSpec(memory_space=VMEM)] * len(stores),
        out_specs=pl.BlockSpec(memory_space=ANY),
        scratch_shapes=[pltpu.SemaphoreType.DMA((total,))],
        cost_estimate=cost(0, total * domain * domain * 4),
        compiler_params=limits(8),
        name="put_in_slots",
    )(slots, *stores)


def add_over(values, name):
    size = lax.axis_size(name)
    if size & (size - 1):
        return lax.psum(values, name)
    step = 1
    while step < size:
        values = values + lax.ppermute(values, name, [(r, r ^ step) for r in range(size)])
        step *= 2
    return values


def per_device(
    amplitudes,
    integrals,
    fock_matrix,
    intersection,
    occ_energy,
    first_occ,
    second_occ,
    near_slot,
    near_count,
    near_weight,
    far_chip,
    far_slot,
    far_weight,
):
    pairs, domain = amplitudes.shape[:2]
    rows = lax.axis_size("row")
    half = pairs // 2
    cap = pairs // rows
    row = lax.axis_index("row")
    core = lax.axis_index("rep")
    occ_count = occ_energy.shape[0]
    slot_ids = jnp.arange(pairs, dtype=jnp.int32)
    source = far_chip[:, 0]
    packed = source * pairs + far_slot[:, 0]
    requests = [lax.ppermute(packed, "row", exchanges(rows, d)) for d in range(1, rows)]
    here = jnp.stack([row, core]).astype(jnp.int32)
    asked, *sends = gather_first(requests, here, amplitudes, rows, cap)
    source, far_slot, near_slot, near_count, near_weight, far_weight, *_ = lax.optimization_barrier(
        (source, far_slot, near_slot, near_count, near_weight, far_weight, asked)
    )

    step = apart(rows, source, row)
    same = step[:, None] == step[None, :]
    before = (step[None, :] < step[:, None]) | (same & (slot_ids[None, :] < slot_ids[:, None]))
    turn = jnp.sum(before.astype(jnp.int32), axis=1)
    like = same & (turn[:, None] % 2 == turn[None, :] % 2) & (turn[None, :] < turn[:, None])
    place = jnp.sum(like.astype(jnp.int32), axis=1)
    mine = jnp.arange(half, dtype=jnp.int32) * 2 + core
    own_pick = mine[:, None] == turn[None, :]
    other_pick = (mine ^ 1)[:, None] == turn[None, :]

    def pick(chosen, values):
        return jnp.sum(jnp.where(chosen, values[None, :], jnp.zeros((), values.dtype)), axis=1)

    own = pick(own_pick, slot_ids)
    other = pick(other_pick, slot_ids)
    far_step = pick(own_pick, step)
    own_far = pick(own_pick, far_slot[:, 0])
    own_place = pick(own_pick, place)
    far_scale = pick(own_pick, far_weight[:, 0].astype(jnp.float32))
    first = pick(own_pick, first_occ)
    second = pick(own_pick, second_occ)
    orbitals = jnp.arange(occ_count, dtype=jnp.int32)

    def energy_of(index):
        found = index[:, None] == orbitals[None, :]
        return jnp.sum(jnp.where(found, occ_energy[None, :], jnp.float32(0.0)), axis=1)

    shift = energy_of(first) + energy_of(second)

    near_pos = jnp.arange(near_slot.shape[1], dtype=jnp.int32)
    alive = near_pos[None, :] < near_count[:, None]
    matches = (near_slot[:, :, None] == slot_ids[None, None, :]) & alive[:, :, None]
    weights = jnp.sum(
        jnp.where(matches, near_weight.astype(jnp.float32)[:, :, None], jnp.float32(0.0)), axis=1
    ).astype(jnp.bfloat16)

    def choose(chosen, table):
        spread = jnp.where(chosen[:, :, None], table[None], jnp.zeros((), table.dtype))
        return jnp.sum(spread.astype(jnp.float32), axis=1).astype(table.dtype)

    own_weights = choose(own_pick, weights)
    by_core = jnp.concatenate(
        [choose(own_pick, own_weights.T).T, choose(other_pick, own_weights.T).T], axis=1
    )
    lane = jnp.arange(LANES)
    unit = lane[:, None] == lane[None, :]

    def spread_of(table):
        grid = jnp.where(
            unit[None, :, None, :], table[:, None, :, None], jnp.zeros((), table.dtype)
        )
        return grid.reshape(half * LANES, pairs * LANES)

    by_slot = turn // 2 + jnp.where(turn % 2 == core, 0, half)
    early = half - cap
    swap = [(0, 1), (1, 0)]
    remote = (rows - 1) * cap
    local_spots = [
        slot_ids,
        jnp.where(
            by_slot < half,
            by_slot + jnp.where(by_slot % half < early, 0, early),
            by_slot - half + jnp.where(by_slot % half < early, early, half),
        ),
    ]
    tables = []
    for where in (slot_ids, by_slot):
        at_home = remote + jnp.sum(
            jnp.where(own_far[:, None] == slot_ids[None, :], where[None, :], 0), axis=1
        )
        spot = jnp.where(far_step == 0, at_home, (far_step - 1) * cap + own_place)
        tables.append(jnp.concatenate([spot, first, second]))
    spreads = [spread_of(own_weights), spread_of(by_core)]
    ats = [own, jnp.arange(half, dtype=jnp.int32)]
    slots = jnp.concatenate([own[:early], other[:early], own[early:], other[early:]])
    stores = [amplitudes]
    whole = [amplitudes]
    for sweep in range(ITERS):
        last = sweep == ITERS - 1
        again = min(sweep, 1)
        if sweep > 0:
            sends = gather_again(asked, local_spots[again], stores, rows, cap)
        arrived = []
        for d in range(1, rows):
            arrived.append(lax.ppermute(sends[d - 1], "row", returns(rows, d)))
        prepared = prepare(
            own, ats[again], shift, spreads[again], whole,
            integrals, fock_matrix, intersection,
        )
        spots = laid(arrived)
        homes = laid(whole, remote)
        done_early = finish(
            0, early, tables[again], far_scale, prepared, spots[:-1], homes, occ_count,
            last,
        )
        given_early = lax.ppermute(done_early[0], "rep", swap)
        done_late = finish(
            early, cap, tables[again], far_scale, prepared, spots, homes, occ_count, last
        )
        given_late = lax.ppermute(done_late[0], "rep", swap)
        stores = [done_early[0], given_early, done_late[0], given_late]
        whole = [
            jnp.concatenate([done_early[0], done_late[0]], axis=0),
            jnp.concatenate([given_early, given_late], axis=0),
        ]
    final = put_in_slots(slots, stores)
    occ_sum = (done_early[1] + done_late[1])[0]
    occ_sum = add_over(occ_sum, "rep")
    occ_sum = add_over(occ_sum, "col")
    occ_sum = add_over(occ_sum, "row")
    total_pairs = pairs * rows * lax.axis_size("col")
    occ_density = occ_sum * (occ_count / (2.0 * total_pairs * domain * domain))
    return (final, occ_density)


def solution(mesh):
    pair_spec = P(("groups", "row", "col"), None, None)
    flat = P(("groups", "row", "col"))
    table = P(("groups", "row", "col"), None)
    return jax.shard_map(
        per_device,
        mesh=mesh,
        in_specs=(
            pair_spec, pair_spec, pair_spec, pair_spec,
            P("groups"), flat, flat, table, flat, table, table, table, table,
        ),
        out_specs=(pair_spec, P("groups")),
        check_vma=False,
    )
```

```python
import jax
import jax.numpy as jnp
from jax import lax
from jax.experimental import pallas as pl
from jax.experimental.pallas import tpu as pltpu
from jax.sharding import PartitionSpec as P


ITERS = 2
ANY = pl.ANY
SMEM = pltpu.SMEM
VMEM = pltpu.VMEM
LANES = 16
MIB = 1 << 20


def exchanges(rows, shift):
    if rows & (rows - 1):
        return [(r, (r - shift) % rows) for r in range(rows)]
    return [(r, r ^ shift) for r in range(rows)]


def returns(rows, shift):
    return [(b, a) for a, b in exchanges(rows, shift)]


def apart(rows, source, row):
    if rows & (rows - 1):
        return (row - source) % rows
    return source ^ row


def limits(mib):
    return pltpu.CompilerParams(vmem_limit_bytes=mib * MIB)


def cost(flops, size):
    return pl.CostEstimate(flops=flops, transcendentals=0, bytes_accessed=size)


def fetch(candidates, spot, target):
    for offset, ref in candidates:

        @pl.when((spot >= offset) & (spot < offset + ref.shape[0]))
        def _(offset=offset, ref=ref):
            target[...] = ref[spot - offset]


def laid(refs, offset=0):
    placed = []
    for ref in refs:
        placed.append((offset, ref))
        offset += ref.shape[0]
    return placed


def gather_first(requests, place, amplitudes, rows, cap):
    pairs, domain = amplitudes.shape[:2]
    blocks = (rows - 1) * cap

    def body(place_ref, *refs):
        lists = refs[: rows - 1]
        store = refs[rows - 1]
        asked = refs[rows]
        outs = refs[rows + 1 : -1]
        sem = refs[-1]
        me = place_ref[0]
        core = place_ref[1]
        for shift in range(1, rows):
            base = (shift - 1) * (cap + 1)
            asker = apart(rows, me, shift) if rows & (rows - 1) == 0 else (me + shift) % rows
            for k in range(cap):
                asked[base + k] = 0
            sources = [lists[shift - 1][p] // pairs for p in range(pairs)]
            count = jnp.int32(0)
            for p in range(pairs):
                count = count + (apart(rows, sources[p], asker) < shift).astype(jnp.int32)
            filled = jnp.int32(0)
            for p in range(pairs):
                mine = sources[p] == me
                taken = mine & (count % 2 == core)
                asked[base + jnp.minimum(filled, cap)] = lists[shift - 1][p] % pairs
                count = count + mine.astype(jnp.int32)
                filled = filled + taken.astype(jnp.int32)
            for k in range(cap):
                pltpu.make_async_copy(
                    store.at[asked[base + k]], outs[shift - 1].at[k], sem.at[shift - 1, k]
                ).start()
        for shift in range(rows - 1):
            for k in range(cap):
                pltpu.make_async_copy(store.at[0], outs[shift].at[k], sem.at[shift, k]).wait()

    shape = (cap, domain, domain)
    return pl.pallas_call(
        body,
        out_shape=[jax.ShapeDtypeStruct(((rows - 1) * (cap + 1),), jnp.int32)]
        + [VMEM(shape, jnp.bfloat16)] * (rows - 1),
        in_specs=[pl.BlockSpec(memory_space=SMEM)] * rows
        + [pl.BlockSpec(memory_space=pltpu.HBM)],
        out_specs=[pl.BlockSpec(memory_space=SMEM)]
        + [pl.BlockSpec(memory_space=VMEM)] * (rows - 1),
        scratch_shapes=[pltpu.SemaphoreType.DMA((rows - 1, cap))],
        cost_estimate=cost(0, blocks * domain * domain * 4),
        compiler_params=limits(8),
        name="gather_first",
    )(place, *requests, pltpu.with_memory_space_constraint(amplitudes, pltpu.HBM))


def gather_again(asked, where, stores, rows, cap):
    domain = stores[0].shape[1]
    blocks = (rows - 1) * cap

    def body(asked_ref, where_ref, *refs):
        sources = laid(refs[: len(stores)])
        outs = refs[len(stores) :]
        for b in range(blocks):
            spot = where_ref[asked_ref[b // cap * (cap + 1) + b % cap]]
            fetch(sources, spot, outs[b // cap].at[b % cap])

    return pl.pallas_call(
        body,
        out_shape=[VMEM((cap, domain, domain), jnp.bfloat16)] * (rows - 1),
        in_specs=[pl.BlockSpec(memory_space=SMEM)] * 2
        + [pl.BlockSpec(memory_space=VMEM)] * len(stores),
        out_specs=[pl.BlockSpec(memory_space=VMEM)] * (rows - 1),
        cost_estimate=cost(0, blocks * domain * domain * 4),
        compiler_params=limits(8),
        name="gather_again",
    )(asked, where, *stores)


def prepare(own, at, shift, spread, stores, integrals, fock_matrix, intersection):
    half = own.shape[0]
    domain = integrals.shape[1]
    total = spread.shape[1] // LANES
    groups = domain // LANES // half
    strip = groups * LANES

    def body(own_ref, at_ref, shift_ref, spread_ref, *refs):
        sources = refs[: len(stores)]
        integ_ref, fock_ref, over_ref, local_ref, rest_ref, recip_ref, keep_ref = refs[len(stores) :]
        i = pl.program_id(0)
        for g in range(groups):
            rows = pl.ds(pl.multiple_of(i * strip + g * LANES, LANES), LANES)
            part = [s[:, rows, :].reshape(s.shape[0] * LANES, domain) for s in sources]
            part = part[0] if len(part) == 1 else jnp.concatenate(part, axis=0)
            sums = jnp.dot(spread_ref[...], part, preferred_element_type=jnp.float32)
            local_ref[:, g * LANES : (g + 1) * LANES, :] = sums.reshape(half, LANES, domain)
        amps = sources[0][at_ref[i]]
        fock = fock_ref[0]
        wide = amps.astype(jnp.float32)
        left = jnp.dot(fock, amps, preferred_element_type=jnp.float32)
        right = jnp.dot(amps, fock, preferred_element_type=jnp.float32)
        row_id = lax.broadcasted_iota(jnp.int32, (domain, domain), 0)
        col_id = lax.broadcasted_iota(jnp.int32, (domain, domain), 1)
        diagonal = jnp.where(row_id == col_id, fock.astype(jnp.float32), 0.0)
        across = jnp.sum(diagonal, axis=0, keepdims=True)
        down = jnp.sum(diagonal, axis=1, keepdims=True)
        residual = integ_ref[0].astype(jnp.float32) + left + right - shift_ref[i] * wide
        recip = 1.0 / (down + across - shift_ref[i])
        recip_ref[0] = recip
        rest_ref[0] = wide - residual * recip
        keep_ref[0] = over_ref[0]

    block = (1, domain, domain)
    mine = pl.BlockSpec(block, lambda i, own, *_: (own[i], 0, 0))
    in_turn = pl.BlockSpec(block, lambda i, *_: (i, 0, 0))
    wide_shape = jax.ShapeDtypeStruct((half, domain, domain), jnp.float32)
    return pl.pallas_call(
        body,
        grid_spec=pltpu.PrefetchScalarGridSpec(
            num_scalar_prefetch=3,
            grid=(half,),
            in_specs=[pl.BlockSpec(spread.shape, lambda i, *_: (0, 0))]
            + [pl.BlockSpec(s.shape, lambda i, *_: (0, 0, 0)) for s in stores]
            + [mine, mine, mine],
            out_specs=[
                pl.BlockSpec((half, strip, domain), lambda i, *_: (0, i, 0)),
                in_turn,
                in_turn,
                in_turn,
            ],
        ),
        out_shape=[
            wide_shape,
            wide_shape,
            wide_shape,
            jax.ShapeDtypeStruct((half, domain, domain), jnp.bfloat16),
        ],
        cost_estimate=cost(
            2 * half * domain**3 * 3,
            (total + 4 * half) * domain * domain * 2 + half * domain * domain * 12,
        ),
        compiler_params=limits(20),
        name="prepare",
    )(own, at, shift, spread, *stores, integrals, fock_matrix, intersection)


def finish(start, count, numbers, scale, prepared, arrived, stores, occ_count, last):
    half, domain = prepared[0].shape[:2]

    def body(number_ref, scale_ref, local_ref, rest_ref, recip_ref, over_ref, *refs):
        candidates = [
            (offset, ref) for offset, ref in zip([o for o, _ in arrived + stores], refs)
        ]
        outs = refs[len(candidates) : -1]
        hold = refs[-1]
        for n in range(count):
            fetch(candidates, number_ref[start + n], hold.at[n])
        if last:
            row_id = lax.broadcasted_iota(jnp.int32, (domain, domain), 0)
            col_id = lax.broadcasted_iota(jnp.int32, (domain, domain), 1)
            on_diagonal = row_id == col_id
            orbital = lax.broadcasted_iota(jnp.int32, (1, occ_count), 1)
            density = jnp.zeros((1, occ_count), jnp.float32)
        for n in range(count):
            i = start + n
            coupled = local_ref[i] + scale_ref[i] * hold[n].astype(jnp.float32)
            over = over_ref[i]
            projected = jnp.dot(
                over, coupled.astype(jnp.bfloat16), preferred_element_type=jnp.float32
            )
            back = lax.dot_general(
                projected.astype(jnp.bfloat16),
                over,
                (((1,), (1,)), ((), ())),
                preferred_element_type=jnp.float32,
            )
            fresh = (rest_ref[i] + back * recip_ref[i]).astype(jnp.bfloat16)
            outs[0][n] = fresh
            if last:
                wide = fresh.astype(jnp.float32)
                square = jnp.dot(fresh, fresh, preferred_element_type=jnp.float32)
                terms = 2.0 * wide * wide - jnp.where(on_diagonal, square, 0.0)
                norm = jnp.sum(jnp.sum(terms, axis=0, keepdims=True), axis=1, keepdims=True)
                picks = (orbital == number_ref[half + i]).astype(jnp.float32)
                picks = picks + (orbital == number_ref[2 * half + i]).astype(jnp.float32)
                density = density + norm * picks
        if last:
            outs[1][...] = density

    out_shape = [VMEM((count, domain, domain), jnp.bfloat16)]
    if last:
        out_shape.append(VMEM((1, occ_count), jnp.float32))
    return pl.pallas_call(
        body,
        out_shape=out_shape,
        in_specs=[pl.BlockSpec(memory_space=SMEM)] * 2
        + [pl.BlockSpec(memory_space=VMEM)] * 4
        + [pl.BlockSpec(memory_space=VMEM)] * len(arrived + stores),
        out_specs=[pl.BlockSpec(memory_space=VMEM)] * len(out_shape),
        scratch_shapes=[VMEM((count, domain, domain), jnp.bfloat16)],
        cost_estimate=cost(2 * count * domain**3 * 2, count * domain * domain * 18),
        compiler_params=limits(16),
        name="finish",
    )(numbers, scale, *prepared, *[a for _, a in arrived + stores])


def put_in_slots(slots, stores):
    domain = stores[0].shape[1]
    total = slots.shape[0]

    def body(slot_ref, *refs):
        sources = refs[: len(stores)]
        out_ref, sem = refs[-2:]
        copies = []
        for source in sources:
            for n in range(source.shape[0]):
                at = len(copies)
                copies.append(
                    pltpu.make_async_copy(source.at[n], out_ref.at[slot_ref[at]], sem.at[at])
                )
        for copy in copies:
            copy.start()
        for copy in copies:
            copy.wait()

    return pl.pallas_call(
        body,
        out_shape=jax.ShapeDtypeStruct((total, domain, domain), jnp.bfloat16),
        in_specs=[pl.BlockSpec(memory_space=SMEM)]
        + [pl.BlockSpec(memory_space=VMEM)] * len(stores),
        out_specs=pl.BlockSpec(memory_space=ANY),
        scratch_shapes=[pltpu.SemaphoreType.DMA((total,))],
        cost_estimate=cost(0, total * domain * domain * 4),
        compiler_params=limits(8),
        name="put_in_slots",
    )(slots, *stores)


def add_over(values, name):
    size = lax.axis_size(name)
    if size & (size - 1):
        return lax.psum(values, name)
    step = 1
    while step < size:
        values = values + lax.ppermute(values, name, [(r, r ^ step) for r in range(size)])
        step *= 2
    return values


def per_device(
    amplitudes,
    integrals,
    fock_matrix,
    intersection,
    occ_energy,
    first_occ,
    second_occ,
    near_slot,
    near_count,
    near_weight,
    far_chip,
    far_slot,
    far_weight,
):
    pairs, domain = amplitudes.shape[:2]
    rows = lax.axis_size("row")
    half = pairs // 2
    cap = pairs // rows
    row = lax.axis_index("row")
    core = lax.axis_index("rep")
    occ_count = occ_energy.shape[0]
    slot_ids = jnp.arange(pairs, dtype=jnp.int32)
    source = far_chip[:, 0]
    packed = source * pairs + far_slot[:, 0]
    requests = [lax.ppermute(packed, "row", exchanges(rows, d)) for d in range(1, rows)]
    here = jnp.stack([row, core]).astype(jnp.int32)
    asked, *sends = gather_first(requests, here, amplitudes, rows, cap)

    step = apart(rows, source, row)
    same = step[:, None] == step[None, :]
    before = (step[None, :] < step[:, None]) | (same & (slot_ids[None, :] < slot_ids[:, None]))
    turn = jnp.sum(before.astype(jnp.int32), axis=1)
    like = same & (turn[:, None] % 2 == turn[None, :] % 2) & (turn[None, :] < turn[:, None])
    place = jnp.sum(like.astype(jnp.int32), axis=1)
    mine = jnp.arange(half, dtype=jnp.int32) * 2 + core
    own_pick = mine[:, None] == turn[None, :]
    other_pick = (mine ^ 1)[:, None] == turn[None, :]

    def pick(chosen, values):
        return jnp.sum(jnp.where(chosen, values[None, :], jnp.zeros((), values.dtype)), axis=1)

    own = pick(own_pick, slot_ids)
    other = pick(other_pick, slot_ids)
    far_step = pick(own_pick, step)
    own_far = pick(own_pick, far_slot[:, 0])
    own_place = pick(own_pick, place)
    far_scale = pick(own_pick, far_weight[:, 0].astype(jnp.float32))
    first = pick(own_pick, first_occ)
    second = pick(own_pick, second_occ)
    orbitals = jnp.arange(occ_count, dtype=jnp.int32)

    def energy_of(index):
        found = index[:, None] == orbitals[None, :]
        return jnp.sum(jnp.where(found, occ_energy[None, :], jnp.float32(0.0)), axis=1)

    shift = energy_of(first) + energy_of(second)

    near_wide = near_weight.astype(jnp.float32)
    weights = jnp.zeros((pairs, pairs), jnp.float32)
    for k in range(near_slot.shape[1]):
        used = (near_slot[:, k : k + 1] == slot_ids[None, :]) & (k < near_count[:, None])
        weights = weights + jnp.where(used, near_wide[:, k : k + 1], jnp.float32(0.0))
    weights = weights.astype(jnp.bfloat16)

    def choose(chosen, table):
        spread = jnp.where(chosen[:, :, None], table[None], jnp.zeros((), table.dtype))
        return jnp.sum(spread.astype(jnp.float32), axis=1).astype(table.dtype)

    own_weights = choose(own_pick, weights)
    by_core = jnp.concatenate(
        [choose(own_pick, own_weights.T).T, choose(other_pick, own_weights.T).T], axis=1
    )
    lane = jnp.arange(LANES)
    unit = lane[:, None] == lane[None, :]

    def spread_of(table):
        grid = jnp.where(
            unit[None, :, None, :], table[:, None, :, None], jnp.zeros((), table.dtype)
        )
        return grid.reshape(half * LANES, pairs * LANES)

    by_slot = turn // 2 + jnp.where(turn % 2 == core, 0, half)
    early = half - cap
    swap = [(0, 1), (1, 0)]
    remote = (rows - 1) * cap
    local_spots = [
        slot_ids,
        jnp.where(
            by_slot < half,
            by_slot + jnp.where(by_slot % half < early, 0, early),
            by_slot - half + jnp.where(by_slot % half < early, early, half),
        ),
    ]
    tables = []
    for where in (slot_ids, by_slot):
        at_home = remote + jnp.sum(
            jnp.where(own_far[:, None] == slot_ids[None, :], where[None, :], 0), axis=1
        )
        spot = jnp.where(far_step == 0, at_home, (far_step - 1) * cap + own_place)
        tables.append(jnp.concatenate([spot, first, second]))
    spreads = [spread_of(own_weights), spread_of(by_core)]
    ats = [own, jnp.arange(half, dtype=jnp.int32)]
    slots = jnp.concatenate([own[:early], other[:early], own[early:], other[early:]])
    (own, shift, far_scale, *moved) = lax.optimization_barrier(
        (own, shift, far_scale, *tables, *spreads, *ats, slots, *sends)
    )
    tables, spreads, ats, slots = moved[:2], moved[2:4], moved[4:6], moved[6]
    stores = [amplitudes]
    whole = [amplitudes]
    for sweep in range(ITERS):
        last = sweep == ITERS - 1
        again = min(sweep, 1)
        if sweep > 0:
            sends = gather_again(asked, local_spots[again], stores, rows, cap)
        arrived = []
        for d in range(1, rows):
            arrived.append(lax.ppermute(sends[d - 1], "row", returns(rows, d)))
        prepared = prepare(
            own, ats[again], shift, spreads[again], whole,
            integrals, fock_matrix, intersection,
        )
        spots = laid(arrived)
        homes = laid(whole, remote)
        done_early = finish(
            0, early, tables[again], far_scale, prepared, spots[:-1], homes, occ_count,
            last,
        )
        given_early = lax.ppermute(done_early[0], "rep", swap)
        done_late = finish(
            early, cap, tables[again], far_scale, prepared, spots, homes, occ_count, last
        )
        given_late = lax.ppermute(done_late[0], "rep", swap)
        stores = [done_early[0], given_early, done_late[0], given_late]
        whole = [
            jnp.concatenate([done_early[0], done_late[0]], axis=0),
            jnp.concatenate([given_early, given_late], axis=0),
        ]
    final = put_in_slots(slots, stores)
    occ_sum = (done_early[1] + done_late[1])[0]
    occ_sum = add_over(occ_sum, "rep")
    occ_sum = add_over(occ_sum, "col")
    occ_sum = add_over(occ_sum, "row")
    total_pairs = pairs * rows * lax.axis_size("col")
    occ_density = occ_sum * (occ_count / (2.0 * total_pairs * domain * domain))
    return (final, occ_density)


def solution(mesh):
    pair_spec = P(("groups", "row", "col"), None, None)
    flat = P(("groups", "row", "col"))
    table = P(("groups", "row", "col"), None)
    return jax.shard_map(
        per_device,
        mesh=mesh,
        in_specs=(
            pair_spec, pair_spec, pair_spec, pair_spec,
            P("groups"), flat, flat, table, flat, table, table, table, table,
        ),
        out_specs=(pair_spec, P("groups")),
        check_vma=False,
    )
```

```python
import jax
import jax.numpy as jnp
from jax import lax
from jax.experimental import pallas as pl
from jax.experimental.pallas import tpu as pltpu
from jax.sharding import PartitionSpec as P


ITERS = 2
ANY = pl.ANY
SMEM = pltpu.SMEM
VMEM = pltpu.VMEM
LANES = 16
MIB = 1 << 20


def exchanges(rows, shift):
    if rows & (rows - 1):
        return [(r, (r - shift) % rows) for r in range(rows)]
    return [(r, r ^ shift) for r in range(rows)]


def returns(rows, shift):
    return [(b, a) for a, b in exchanges(rows, shift)]


def apart(rows, source, row):
    if rows & (rows - 1):
        return (row - source) % rows
    return source ^ row


def limits(mib):
    return pltpu.CompilerParams(vmem_limit_bytes=mib * MIB)


def cost(flops, size):
    return pl.CostEstimate(flops=flops, transcendentals=0, bytes_accessed=size)


def fetch(candidates, spot, target):
    for offset, ref in candidates:

        @pl.when((spot >= offset) & (spot < offset + ref.shape[0]))
        def _(offset=offset, ref=ref):
            target[...] = ref[spot - offset]


def laid(refs, offset=0):
    placed = []
    for ref in refs:
        placed.append((offset, ref))
        offset += ref.shape[0]
    return placed


def gather_first(requests, shifts, place, amplitudes, rows, cap):
    pairs, domain = amplitudes.shape[:2]
    count_of = len(shifts)
    blocks = count_of * cap

    def body(place_ref, *refs):
        lists = refs[:count_of]
        store = refs[count_of]
        asked = refs[count_of + 1]
        outs = refs[count_of + 2 : -1]
        sem = refs[-1]
        me = place_ref[0]
        core = place_ref[1]
        for n, shift in enumerate(shifts):
            base = n * (cap + 1)
            asker = apart(rows, me, shift) if rows & (rows - 1) == 0 else (me + shift) % rows
            for k in range(cap):
                asked[base + k] = 0
            sources = [lists[n][p] // pairs for p in range(pairs)]
            count = jnp.int32(0)
            for p in range(pairs):
                count = count + (apart(rows, sources[p], asker) < shift).astype(jnp.int32)
            filled = jnp.int32(0)
            for p in range(pairs):
                mine = sources[p] == me
                taken = mine & (count % 2 == core)
                asked[base + jnp.minimum(filled, cap)] = lists[n][p] % pairs
                count = count + mine.astype(jnp.int32)
                filled = filled + taken.astype(jnp.int32)
            for k in range(cap):
                pltpu.make_async_copy(
                    store.at[asked[base + k]], outs[n].at[k], sem.at[n, k]
                ).start()
        for n in range(count_of):
            for k in range(cap):
                pltpu.make_async_copy(store.at[0], outs[n].at[k], sem.at[n, k]).wait()

    shape = (cap, domain, domain)
    return pl.pallas_call(
        body,
        out_shape=[jax.ShapeDtypeStruct((count_of * (cap + 1),), jnp.int32)]
        + [VMEM(shape, jnp.bfloat16)] * count_of,
        in_specs=[pl.BlockSpec(memory_space=SMEM)] * (count_of + 1)
        + [pl.BlockSpec(memory_space=pltpu.HBM)],
        out_specs=[pl.BlockSpec(memory_space=SMEM)]
        + [pl.BlockSpec(memory_space=VMEM)] * count_of,
        scratch_shapes=[pltpu.SemaphoreType.DMA((count_of, cap))],
        cost_estimate=cost(0, blocks * domain * domain * 4),
        compiler_params=limits(8),
        name="gather_first",
    )(place, *requests, pltpu.with_memory_space_constraint(amplitudes, pltpu.HBM))


def gather_again(asked, where, stores, cap):
    domain = stores[0].shape[1]
    lists = asked.shape[0] // (cap + 1)
    blocks = lists * cap

    def body(asked_ref, where_ref, *refs):
        sources = laid(refs[: len(stores)])
        outs = refs[len(stores) :]
        for b in range(blocks):
            spot = where_ref[asked_ref[b // cap * (cap + 1) + b % cap]]
            fetch(sources, spot, outs[b // cap].at[b % cap])

    return pl.pallas_call(
        body,
        out_shape=[VMEM((cap, domain, domain), jnp.bfloat16)] * lists,
        in_specs=[pl.BlockSpec(memory_space=SMEM)] * 2
        + [pl.BlockSpec(memory_space=VMEM)] * len(stores),
        out_specs=[pl.BlockSpec(memory_space=VMEM)] * lists,
        cost_estimate=cost(0, blocks * domain * domain * 4),
        compiler_params=limits(8),
        name="gather_again",
    )(asked, where, *stores)


def prepare(own, at, columns, shift, near, stores, integrals, fock_matrix, intersection):
    half = own.shape[0]
    domain = integrals.shape[1]
    total = columns.shape[0]
    entries = near[0].shape[1]
    groups = domain // LANES // half
    strip = groups * LANES

    def spread_weights(own_ref, column_ref, slot_ref, count_ref, weight_ref, spread_ref):
        lane = lax.broadcasted_iota(jnp.int32, (total, total), 1)
        weights = jnp.zeros((total, total), jnp.float32)
        for k in range(entries):
            used = (slot_ref[:, k : k + 1] == lane) & (k < count_ref[...])
            wide = weight_ref[:, k : k + 1].astype(jnp.float32)
            weights = weights + jnp.where(used, wide, jnp.float32(0.0))
        weights = weights.astype(jnp.bfloat16)
        shape = (half * LANES, total)
        row = lax.broadcasted_iota(jnp.int32, shape, 0) // LANES
        wanted = jnp.zeros(shape, jnp.int32)
        for n in range(half):
            wanted = jnp.where(row == n, own_ref[n], wanted)
        pick = lax.broadcasted_iota(jnp.int32, shape, 1) == wanted
        mine = jnp.dot(
            pick.astype(jnp.float32).astype(jnp.bfloat16),
            weights,
            preferred_element_type=jnp.float32,
        ).astype(jnp.bfloat16)
        shape = (total, total * LANES)
        column = lax.broadcasted_iota(jnp.int32, shape, 1) // LANES
        wanted = jnp.zeros(shape, jnp.int32)
        for n in range(total):
            wanted = jnp.where(column == n, column_ref[n], wanted)
        pick = lax.broadcasted_iota(jnp.int32, shape, 0) == wanted
        full = jnp.dot(
            mine,
            pick.astype(jnp.float32).astype(jnp.bfloat16),
            preferred_element_type=jnp.float32,
        )
        shape = (half * LANES, total * LANES)
        down = lax.broadcasted_iota(jnp.int32, shape, 0) % LANES
        along = lax.broadcasted_iota(jnp.int32, shape, 1) % LANES
        spread_ref[...] = jnp.where(down == along, full, 0.0).astype(jnp.bfloat16)

    def body(own_ref, at_ref, column_ref, shift_ref, slot_ref, count_ref, weight_ref, *refs):
        sources = refs[: len(stores)]
        (integ_ref, fock_ref, over_ref, local_ref, rest_ref, recip_ref, keep_ref, spread_ref) = (
            refs[len(stores) :]
        )
        i = pl.program_id(0)

        @pl.when(i == 0)
        def _():
            spread_weights(own_ref, column_ref, slot_ref, count_ref, weight_ref, spread_ref)

        for g in range(groups):
            rows = pl.ds(pl.multiple_of(i * strip + g * LANES, LANES), LANES)
            part = [s[:, rows, :].reshape(s.shape[0] * LANES, domain) for s in sources]
            part = part[0] if len(part) == 1 else jnp.concatenate(part, axis=0)
            sums = jnp.dot(spread_ref[...], part, preferred_element_type=jnp.float32)
            local_ref[:, g * LANES : (g + 1) * LANES, :] = sums.reshape(half, LANES, domain)
        amps = sources[0][at_ref[i]]
        fock = fock_ref[0]
        wide = amps.astype(jnp.float32)
        left = jnp.dot(fock, amps, preferred_element_type=jnp.float32)
        right = jnp.dot(amps, fock, preferred_element_type=jnp.float32)
        row_id = lax.broadcasted_iota(jnp.int32, (domain, domain), 0)
        col_id = lax.broadcasted_iota(jnp.int32, (domain, domain), 1)
        diagonal = jnp.where(row_id == col_id, fock.astype(jnp.float32), 0.0)
        across = jnp.sum(diagonal, axis=0, keepdims=True)
        down = jnp.sum(diagonal, axis=1, keepdims=True)
        residual = integ_ref[0].astype(jnp.float32) + left + right - shift_ref[i] * wide
        recip = 1.0 / (down + across - shift_ref[i])
        recip_ref[0] = recip
        rest_ref[0] = wide - residual * recip
        keep_ref[0] = over_ref[0]

    block = (1, domain, domain)
    mine = pl.BlockSpec(block, lambda i, own, *_: (own[i], 0, 0))
    in_turn = pl.BlockSpec(block, lambda i, *_: (i, 0, 0))
    wide_shape = jax.ShapeDtypeStruct((half, domain, domain), jnp.float32)
    return pl.pallas_call(
        body,
        grid_spec=pltpu.PrefetchScalarGridSpec(
            num_scalar_prefetch=4,
            grid=(half,),
            in_specs=[pl.BlockSpec(n.shape, lambda i, *_: (0, 0)) for n in near]
            + [pl.BlockSpec(s.shape, lambda i, *_: (0, 0, 0)) for s in stores]
            + [mine, mine, mine],
            out_specs=[
                pl.BlockSpec((half, strip, domain), lambda i, *_: (0, i, 0)),
                in_turn,
                in_turn,
                in_turn,
            ],
            scratch_shapes=[VMEM((half * LANES, total * LANES), jnp.bfloat16)],
        ),
        out_shape=[
            wide_shape,
            wide_shape,
            wide_shape,
            jax.ShapeDtypeStruct((half, domain, domain), jnp.bfloat16),
        ],
        cost_estimate=cost(
            2 * half * domain**3 * 3,
            (total + 4 * half) * domain * domain * 2 + half * domain * domain * 12,
        ),
        compiler_params=limits(20),
        name="prepare",
    )(own, at, columns, shift, *near, *stores, integrals, fock_matrix, intersection)


def finish(start, count, numbers, scale, prepared, arrived, stores, occ_count, last):
    half, domain = prepared[0].shape[:2]

    def body(number_ref, scale_ref, local_ref, rest_ref, recip_ref, over_ref, *refs):
        candidates = [
            (offset, ref) for offset, ref in zip([o for o, _ in arrived + stores], refs)
        ]
        outs = refs[len(candidates) : -1]
        hold = refs[-1]
        for n in range(count):
            fetch(candidates, number_ref[start + n], hold.at[n])
        if last:
            row_id = lax.broadcasted_iota(jnp.int32, (domain, domain), 0)
            col_id = lax.broadcasted_iota(jnp.int32, (domain, domain), 1)
            on_diagonal = row_id == col_id
            orbital = lax.broadcasted_iota(jnp.int32, (1, occ_count), 1)
            density = jnp.zeros((1, occ_count), jnp.float32)
        for n in range(count):
            i = start + n
            coupled = local_ref[i] + scale_ref[i] * hold[n].astype(jnp.float32)
            over = over_ref[i]
            projected = jnp.dot(
                over, coupled.astype(jnp.bfloat16), preferred_element_type=jnp.float32
            )
            back = lax.dot_general(
                projected.astype(jnp.bfloat16),
                over,
                (((1,), (1,)), ((), ())),
                preferred_element_type=jnp.float32,
            )
            fresh = (rest_ref[i] + back * recip_ref[i]).astype(jnp.bfloat16)
            outs[0][n] = fresh
            if last:
                wide = fresh.astype(jnp.float32)
                square = jnp.dot(fresh, fresh, preferred_element_type=jnp.float32)
                terms = 2.0 * wide * wide - jnp.where(on_diagonal, square, 0.0)
                norm = jnp.sum(jnp.sum(terms, axis=0, keepdims=True), axis=1, keepdims=True)
                picks = (orbital == number_ref[half + i]).astype(jnp.float32)
                picks = picks + (orbital == number_ref[2 * half + i]).astype(jnp.float32)
                density = density + norm * picks
        if last:
            outs[1][...] = density

    out_shape = [VMEM((count, domain, domain), jnp.bfloat16)]
    if last:
        out_shape.append(VMEM((1, occ_count), jnp.float32))
    return pl.pallas_call(
        body,
        out_shape=out_shape,
        in_specs=[pl.BlockSpec(memory_space=SMEM)] * 2
        + [pl.BlockSpec(memory_space=VMEM)] * 4
        + [pl.BlockSpec(memory_space=VMEM)] * len(arrived + stores),
        out_specs=[pl.BlockSpec(memory_space=VMEM)] * len(out_shape),
        scratch_shapes=[VMEM((count, domain, domain), jnp.bfloat16)],
        cost_estimate=cost(2 * count * domain**3 * 2, count * domain * domain * 18),
        compiler_params=limits(16),
        name="finish",
    )(numbers, scale, *prepared, *[a for _, a in arrived + stores])


def put_in_slots(slots, stores):
    domain = stores[0].shape[1]
    total = slots.shape[0]

    def body(slot_ref, *refs):
        sources = refs[: len(stores)]
        out_ref, sem = refs[-2:]
        copies = []
        for source in sources:
            for n in range(source.shape[0]):
                at = len(copies)
                copies.append(
                    pltpu.make_async_copy(source.at[n], out_ref.at[slot_ref[at]], sem.at[at])
                )
        for copy in copies:
            copy.start()
        for copy in copies:
            copy.wait()

    return pl.pallas_call(
        body,
        out_shape=jax.ShapeDtypeStruct((total, domain, domain), jnp.bfloat16),
        in_specs=[pl.BlockSpec(memory_space=SMEM)]
        + [pl.BlockSpec(memory_space=VMEM)] * len(stores),
        out_specs=pl.BlockSpec(memory_space=ANY),
        scratch_shapes=[pltpu.SemaphoreType.DMA((total,))],
        cost_estimate=cost(0, total * domain * domain * 4),
        compiler_params=limits(8),
        name="put_in_slots",
    )(slots, *stores)


def add_over(values, name):
    size = lax.axis_size(name)
    if size & (size - 1):
        return lax.psum(values, name)
    step = 1
    while step < size:
        values = values + lax.ppermute(values, name, [(r, r ^ step) for r in range(size)])
        step *= 2
    return values


def per_device(
    amplitudes,
    integrals,
    fock_matrix,
    intersection,
    occ_energy,
    first_occ,
    second_occ,
    near_slot,
    near_count,
    near_weight,
    far_chip,
    far_slot,
    far_weight,
):
    pairs, domain = amplitudes.shape[:2]
    rows = lax.axis_size("row")
    half = pairs // 2
    cap = pairs // rows
    row = lax.axis_index("row")
    core = lax.axis_index("rep")
    occ_count = occ_energy.shape[0]
    slot_ids = jnp.arange(pairs, dtype=jnp.int32)
    source = far_chip[:, 0]
    packed = source * pairs + far_slot[:, 0]
    here = jnp.stack([row, core]).astype(jnp.int32)
    groups = [[rows // 2], [d for d in range(1, rows) if d != rows // 2]]
    request = lax.ppermute(packed, "row", exchanges(rows, rows // 2))
    asked_mid, send_mid = gather_first([request], groups[0], here, amplitudes, rows, cap)

    step = apart(rows, source, row)
    same = step[:, None] == step[None, :]
    before = (step[None, :] < step[:, None]) | (same & (slot_ids[None, :] < slot_ids[:, None]))
    turn = jnp.sum(before.astype(jnp.int32), axis=1)
    like = same & (turn[:, None] % 2 == turn[None, :] % 2) & (turn[None, :] < turn[:, None])
    place = jnp.sum(like.astype(jnp.int32), axis=1)
    mine = jnp.arange(half, dtype=jnp.int32) * 2 + core
    own_pick = mine[:, None] == turn[None, :]
    other_pick = (mine ^ 1)[:, None] == turn[None, :]

    def pick(chosen, values):
        return jnp.sum(jnp.where(chosen, values[None, :], jnp.zeros((), values.dtype)), axis=1)

    own = pick(own_pick, slot_ids)
    other = pick(other_pick, slot_ids)
    far_step = pick(own_pick, step)
    own_far = pick(own_pick, far_slot[:, 0])
    own_place = pick(own_pick, place)
    far_scale = pick(own_pick, far_weight[:, 0].astype(jnp.float32))
    first = pick(own_pick, first_occ)
    second = pick(own_pick, second_occ)
    orbitals = jnp.arange(occ_count, dtype=jnp.int32)

    def energy_of(index):
        found = index[:, None] == orbitals[None, :]
        return jnp.sum(jnp.where(found, occ_energy[None, :], jnp.float32(0.0)), axis=1)

    shift = energy_of(first) + energy_of(second)

    by_slot = turn // 2 + jnp.where(turn % 2 == core, 0, half)
    early = half - cap
    swap = [(0, 1), (1, 0)]
    remote = (rows - 1) * cap
    local_spots = [
        slot_ids,
        jnp.where(
            by_slot < half,
            by_slot + jnp.where(by_slot % half < early, 0, early),
            by_slot - half + jnp.where(by_slot % half < early, early, half),
        ),
    ]
    tables = []
    for where in (slot_ids, by_slot):
        at_home = remote + jnp.sum(
            jnp.where(own_far[:, None] == slot_ids[None, :], where[None, :], 0), axis=1
        )
        spot = jnp.where(far_step == 0, at_home, (far_step - 1) * cap + own_place)
        tables.append(jnp.concatenate([spot, first, second]))
    near = [near_slot, near_count[:, None], near_weight]
    columns = [slot_ids, jnp.concatenate([own, other])]
    ats = [own, jnp.arange(half, dtype=jnp.int32)]
    slots = jnp.concatenate([own[:early], other[:early], own[early:], other[early:]])
    (own, shift, far_scale, *moved, send_mid) = lax.optimization_barrier(
        (own, shift, far_scale, *tables, *columns, *ats, slots, send_mid)
    )
    tables, columns, ats, slots = moved[:2], moved[2:4], moved[4:6], moved[6]
    stores = [amplitudes]
    whole = [amplitudes]
    for sweep in range(ITERS):
        last = sweep == ITERS - 1
        again = min(sweep, 1)
        if sweep > 0:
            (send_mid,) = gather_again(asked_mid, local_spots[1], stores, cap)
        arrived = {}
        arrived[rows // 2] = lax.ppermute(send_mid, "row", returns(rows, rows // 2))
        if sweep == 0:
            packed, _ = lax.optimization_barrier((packed, send_mid))
            requests = [
                lax.ppermute(packed, "row", exchanges(rows, d)) for d in groups[1]
            ]
            asked, *sends = gather_first(
                requests, groups[1], here, amplitudes, rows, cap
            )
        else:
            sends = gather_again(asked, local_spots[1], stores, cap)
        for d, send in zip(groups[1], sends):
            arrived[d] = lax.ppermute(send, "row", returns(rows, d))
        arrived = [arrived[d] for d in range(1, rows)]
        prepared = prepare(
            own, ats[again], columns[again], shift, near, whole,
            integrals, fock_matrix, intersection,
        )
        spots = laid(arrived)
        homes = laid(whole, remote)
        done_early = finish(
            0, early, tables[again], far_scale, prepared, spots[:-1], homes, occ_count,
            last,
        )
        given_early = lax.ppermute(done_early[0], "rep", swap)
        done_late = finish(
            early, cap, tables[again], far_scale, prepared, spots, homes, occ_count, last
        )
        given_late = lax.ppermute(done_late[0], "rep", swap)
        stores = [done_early[0], given_early, done_late[0], given_late]
        whole = [
            jnp.concatenate([done_early[0], done_late[0]], axis=0),
            jnp.concatenate([given_early, given_late], axis=0),
        ]
    final = put_in_slots(slots, stores)
    occ_sum = (done_early[1] + done_late[1])[0]
    occ_sum = add_over(occ_sum, "rep")
    occ_sum = add_over(occ_sum, "col")
    occ_sum = add_over(occ_sum, "row")
    total_pairs = pairs * rows * lax.axis_size("col")
    occ_density = occ_sum * (occ_count / (2.0 * total_pairs * domain * domain))
    return (final, occ_density)


def solution(mesh):
    pair_spec = P(("groups", "row", "col"), None, None)
    flat = P(("groups", "row", "col"))
    table = P(("groups", "row", "col"), None)
    return jax.shard_map(
        per_device,
        mesh=mesh,
        in_specs=(
            pair_spec, pair_spec, pair_spec, pair_spec,
            P("groups"), flat, flat, table, flat, table, table, table, table,
        ),
        out_specs=(pair_spec, P("groups")),
        check_vma=False,
    )
```

```python
import jax
import jax.numpy as jnp
from jax import lax
from jax.experimental import pallas as pl
from jax.experimental.pallas import tpu as pltpu
from jax.sharding import PartitionSpec as P


ITERS = 2
ANY = pl.ANY
SMEM = pltpu.SMEM
VMEM = pltpu.VMEM
LANES = 16
MIB = 1 << 20


def exchanges(rows, shift):
    if rows & (rows - 1):
        return [(r, (r - shift) % rows) for r in range(rows)]
    return [(r, r ^ shift) for r in range(rows)]


def returns(rows, shift):
    return [(b, a) for a, b in exchanges(rows, shift)]


def apart(rows, source, row):
    if rows & (rows - 1):
        return (row - source) % rows
    return source ^ row


def limits(mib):
    return pltpu.CompilerParams(vmem_limit_bytes=mib * MIB)


def cost(flops, size):
    return pl.CostEstimate(flops=flops, transcendentals=0, bytes_accessed=size)


def fetch(candidates, spot, target):
    for offset, ref in candidates:

        @pl.when((spot >= offset) & (spot < offset + ref.shape[0]))
        def _(offset=offset, ref=ref):
            target[...] = ref[spot - offset]


def laid(refs, offset=0):
    placed = []
    for ref in refs:
        placed.append((offset, ref))
        offset += ref.shape[0]
    return placed


def gather_first(requests, shifts, place, amplitudes, rows, cap):
    pairs, domain = amplitudes.shape[:2]
    count_of = len(shifts)
    blocks = count_of * cap

    def body(place_ref, *refs):
        lists = refs[:count_of]
        store = refs[count_of]
        asked = refs[count_of + 1]
        outs = refs[count_of + 2 : -1]
        sem = refs[-1]
        me = place_ref[0]
        core = place_ref[1]
        for n, shift in enumerate(shifts):
            base = n * (cap + 1)
            asker = apart(rows, me, shift) if rows & (rows - 1) == 0 else (me + shift) % rows
            for k in range(cap):
                asked[base + k] = 0
            sources = [lists[n][p] // pairs for p in range(pairs)]
            count = jnp.int32(0)
            for p in range(pairs):
                count = count + (apart(rows, sources[p], asker) < shift).astype(jnp.int32)
            filled = jnp.int32(0)
            for p in range(pairs):
                mine = sources[p] == me
                taken = mine & (count % 2 == core)
                asked[base + jnp.minimum(filled, cap)] = lists[n][p] % pairs
                count = count + mine.astype(jnp.int32)
                filled = filled + taken.astype(jnp.int32)
            for k in range(cap):
                pltpu.make_async_copy(
                    store.at[asked[base + k]], outs[n].at[k], sem.at[n, k]
                ).start()
        for n in range(count_of):
            for k in range(cap):
                pltpu.make_async_copy(store.at[0], outs[n].at[k], sem.at[n, k]).wait()

    shape = (cap, domain, domain)
    return pl.pallas_call(
        body,
        out_shape=[jax.ShapeDtypeStruct((count_of * (cap + 1),), jnp.int32)]
        + [VMEM(shape, jnp.bfloat16)] * count_of,
        in_specs=[pl.BlockSpec(memory_space=SMEM)] * (count_of + 1)
        + [pl.BlockSpec(memory_space=pltpu.HBM)],
        out_specs=[pl.BlockSpec(memory_space=SMEM)]
        + [pl.BlockSpec(memory_space=VMEM)] * count_of,
        scratch_shapes=[pltpu.SemaphoreType.DMA((count_of, cap))],
        cost_estimate=cost(0, blocks * domain * domain * 4),
        compiler_params=limits(8),
        name="gather_first",
    )(place, *requests, pltpu.with_memory_space_constraint(amplitudes, pltpu.HBM))


def gather_again(asked, where, stores, cap):
    domain = stores[0].shape[1]
    lists = asked.shape[0] // (cap + 1)
    blocks = lists * cap

    def body(asked_ref, where_ref, *refs):
        sources = laid(refs[: len(stores)])
        outs = refs[len(stores) :]
        for b in range(blocks):
            spot = where_ref[asked_ref[b // cap * (cap + 1) + b % cap]]
            fetch(sources, spot, outs[b // cap].at[b % cap])

    return pl.pallas_call(
        body,
        out_shape=[VMEM((cap, domain, domain), jnp.bfloat16)] * lists,
        in_specs=[pl.BlockSpec(memory_space=SMEM)] * 2
        + [pl.BlockSpec(memory_space=VMEM)] * len(stores),
        out_specs=[pl.BlockSpec(memory_space=VMEM)] * lists,
        cost_estimate=cost(0, blocks * domain * domain * 4),
        compiler_params=limits(8),
        name="gather_again",
    )(asked, where, *stores)


def prepare(own, at, columns, shift, near, stores, integrals, fock_matrix, intersection):
    half = own.shape[0]
    domain = integrals.shape[1]
    total = columns.shape[0]
    entries = near[0].shape[1]
    groups = domain // LANES // half
    strip = groups * LANES

    def spread_weights(own_ref, column_ref, slot_ref, count_ref, weight_ref, spread_ref):
        lane = lax.broadcasted_iota(jnp.int32, (total, total), 1)
        weights = jnp.zeros((total, total), jnp.float32)
        for k in range(entries):
            used = (slot_ref[:, k : k + 1] == lane) & (k < count_ref[...])
            wide = weight_ref[:, k : k + 1].astype(jnp.float32)
            weights = weights + jnp.where(used, wide, jnp.float32(0.0))
        weights = weights.astype(jnp.bfloat16)
        shape = (half * LANES, total)
        row = lax.broadcasted_iota(jnp.int32, shape, 0) // LANES
        wanted = jnp.zeros(shape, jnp.int32)
        for n in range(half):
            wanted = jnp.where(row == n, own_ref[n], wanted)
        pick = lax.broadcasted_iota(jnp.int32, shape, 1) == wanted
        mine = jnp.dot(
            pick.astype(jnp.float32).astype(jnp.bfloat16),
            weights,
            preferred_element_type=jnp.float32,
        ).astype(jnp.bfloat16)
        shape = (total, total * LANES)
        column = lax.broadcasted_iota(jnp.int32, shape, 1) // LANES
        wanted = jnp.zeros(shape, jnp.int32)
        for n in range(total):
            wanted = jnp.where(column == n, column_ref[n], wanted)
        pick = lax.broadcasted_iota(jnp.int32, shape, 0) == wanted
        full = jnp.dot(
            mine,
            pick.astype(jnp.float32).astype(jnp.bfloat16),
            preferred_element_type=jnp.float32,
        )
        shape = (half * LANES, total * LANES)
        down = lax.broadcasted_iota(jnp.int32, shape, 0) % LANES
        along = lax.broadcasted_iota(jnp.int32, shape, 1) % LANES
        spread_ref[...] = jnp.where(down == along, full, 0.0).astype(jnp.bfloat16)

    def body(own_ref, at_ref, column_ref, shift_ref, slot_ref, count_ref, weight_ref, *refs):
        sources = refs[: len(stores)]
        (integ_ref, fock_ref, over_ref, local_ref, rest_ref, recip_ref, keep_ref, spread_ref) = (
            refs[len(stores) :]
        )
        i = pl.program_id(0)

        @pl.when(i == 0)
        def _():
            spread_weights(own_ref, column_ref, slot_ref, count_ref, weight_ref, spread_ref)

        for g in range(groups):
            rows = pl.ds(pl.multiple_of(i * strip + g * LANES, LANES), LANES)
            part = [s[:, rows, :].reshape(s.shape[0] * LANES, domain) for s in sources]
            part = part[0] if len(part) == 1 else jnp.concatenate(part, axis=0)
            sums = jnp.dot(spread_ref[...], part, preferred_element_type=jnp.float32)
            local_ref[:, g * LANES : (g + 1) * LANES, :] = sums.reshape(half, LANES, domain)
        amps = sources[0][at_ref[i]]
        fock = fock_ref[0]
        wide = amps.astype(jnp.float32)
        left = jnp.dot(fock, amps, preferred_element_type=jnp.float32)
        right = jnp.dot(amps, fock, preferred_element_type=jnp.float32)
        row_id = lax.broadcasted_iota(jnp.int32, (domain, domain), 0)
        col_id = lax.broadcasted_iota(jnp.int32, (domain, domain), 1)
        diagonal = jnp.where(row_id == col_id, fock.astype(jnp.float32), 0.0)
        across = jnp.sum(diagonal, axis=0, keepdims=True)
        down = jnp.sum(diagonal, axis=1, keepdims=True)
        residual = integ_ref[0].astype(jnp.float32) + left + right - shift_ref[i] * wide
        recip = 1.0 / (down + across - shift_ref[i])
        recip_ref[0] = recip
        rest_ref[0] = wide - residual * recip
        keep_ref[0] = over_ref[0]

    block = (1, domain, domain)
    mine = pl.BlockSpec(block, lambda i, own, *_: (own[i], 0, 0))
    in_turn = pl.BlockSpec(block, lambda i, *_: (i, 0, 0))
    wide_shape = jax.ShapeDtypeStruct((half, domain, domain), jnp.float32)
    return pl.pallas_call(
        body,
        grid_spec=pltpu.PrefetchScalarGridSpec(
            num_scalar_prefetch=4,
            grid=(half,),
            in_specs=[pl.BlockSpec(n.shape, lambda i, *_: (0, 0)) for n in near]
            + [pl.BlockSpec(s.shape, lambda i, *_: (0, 0, 0)) for s in stores]
            + [mine, mine, mine],
            out_specs=[
                pl.BlockSpec((half, strip, domain), lambda i, *_: (0, i, 0)),
                in_turn,
                in_turn,
                in_turn,
            ],
            scratch_shapes=[VMEM((half * LANES, total * LANES), jnp.bfloat16)],
        ),
        out_shape=[
            wide_shape,
            wide_shape,
            wide_shape,
            jax.ShapeDtypeStruct((half, domain, domain), jnp.bfloat16),
        ],
        cost_estimate=cost(
            2 * half * domain**3 * 3,
            (total + 4 * half) * domain * domain * 2 + half * domain * domain * 12,
        ),
        compiler_params=limits(20),
        name="prepare",
    )(own, at, columns, shift, *near, *stores, integrals, fock_matrix, intersection)


def finish(start, count, numbers, scale, prepared, arrived, stores, occ_count, last):
    half, domain = prepared[0].shape[:2]

    def body(number_ref, scale_ref, local_ref, rest_ref, recip_ref, over_ref, *refs):
        candidates = [
            (offset, ref) for offset, ref in zip([o for o, _ in arrived + stores], refs)
        ]
        outs = refs[len(candidates) : -1]
        hold = refs[-1]
        for n in range(count):
            fetch(candidates, number_ref[start + n], hold.at[n])
        if last:
            row_id = lax.broadcasted_iota(jnp.int32, (domain, domain), 0)
            col_id = lax.broadcasted_iota(jnp.int32, (domain, domain), 1)
            on_diagonal = row_id == col_id
            orbital = lax.broadcasted_iota(jnp.int32, (1, occ_count), 1)
            density = jnp.zeros((1, occ_count), jnp.float32)
        for n in range(count):
            i = start + n
            coupled = local_ref[i] + scale_ref[i] * hold[n].astype(jnp.float32)
            over = over_ref[i]
            projected = jnp.dot(
                over, coupled.astype(jnp.bfloat16), preferred_element_type=jnp.float32
            )
            back = lax.dot_general(
                projected.astype(jnp.bfloat16),
                over,
                (((1,), (1,)), ((), ())),
                preferred_element_type=jnp.float32,
            )
            fresh = (rest_ref[i] + back * recip_ref[i]).astype(jnp.bfloat16)
            outs[0][n] = fresh
            if last:
                wide = fresh.astype(jnp.float32)
                square = jnp.dot(fresh, fresh, preferred_element_type=jnp.float32)
                terms = 2.0 * wide * wide - jnp.where(on_diagonal, square, 0.0)
                norm = jnp.sum(jnp.sum(terms, axis=0, keepdims=True), axis=1, keepdims=True)
                picks = (orbital == number_ref[half + i]).astype(jnp.float32)
                picks = picks + (orbital == number_ref[2 * half + i]).astype(jnp.float32)
                density = density + norm * picks
        if last:
            outs[1][...] = density

    out_shape = [VMEM((count, domain, domain), jnp.bfloat16)]
    if last:
        out_shape.append(VMEM((1, occ_count), jnp.float32))
    return pl.pallas_call(
        body,
        out_shape=out_shape,
        in_specs=[pl.BlockSpec(memory_space=SMEM)] * 2
        + [pl.BlockSpec(memory_space=VMEM)] * 4
        + [pl.BlockSpec(memory_space=VMEM)] * len(arrived + stores),
        out_specs=[pl.BlockSpec(memory_space=VMEM)] * len(out_shape),
        scratch_shapes=[VMEM((count, domain, domain), jnp.bfloat16)],
        cost_estimate=cost(2 * count * domain**3 * 2, count * domain * domain * 18),
        compiler_params=limits(16),
        name="finish",
    )(numbers, scale, *prepared, *[a for _, a in arrived + stores])


def put_in_slots(slots, stores):
    domain = stores[0].shape[1]
    total = slots.shape[0]

    def body(slot_ref, *refs):
        sources = refs[: len(stores)]
        out_ref, sem = refs[-2:]
        copies = []
        for source in sources:
            for n in range(source.shape[0]):
                at = len(copies)
                copies.append(
                    pltpu.make_async_copy(source.at[n], out_ref.at[slot_ref[at]], sem.at[at])
                )
        for copy in copies:
            copy.start()
        for copy in copies:
            copy.wait()

    return pl.pallas_call(
        body,
        out_shape=jax.ShapeDtypeStruct((total, domain, domain), jnp.bfloat16),
        in_specs=[pl.BlockSpec(memory_space=SMEM)]
        + [pl.BlockSpec(memory_space=VMEM)] * len(stores),
        out_specs=pl.BlockSpec(memory_space=ANY),
        scratch_shapes=[pltpu.SemaphoreType.DMA((total,))],
        cost_estimate=cost(0, total * domain * domain * 4),
        compiler_params=limits(8),
        name="put_in_slots",
    )(slots, *stores)


def add_over(values, name):
    size = lax.axis_size(name)
    if size & (size - 1):
        return lax.psum(values, name)
    step = 1
    while step < size:
        values = values + lax.ppermute(values, name, [(r, r ^ step) for r in range(size)])
        step *= 2
    return values


def per_device(
    amplitudes,
    integrals,
    fock_matrix,
    intersection,
    occ_energy,
    first_occ,
    second_occ,
    near_slot,
    near_count,
    near_weight,
    far_chip,
    far_slot,
    far_weight,
):
    pairs, domain = amplitudes.shape[:2]
    rows = lax.axis_size("row")
    half = pairs // 2
    cap = pairs // rows
    row = lax.axis_index("row")
    core = lax.axis_index("rep")
    occ_count = occ_energy.shape[0]
    slot_ids = jnp.arange(pairs, dtype=jnp.int32)
    source = far_chip[:, 0]
    packed = source * pairs + far_slot[:, 0]
    here = jnp.stack([row, core]).astype(jnp.int32)
    groups = [[rows // 2], [d for d in range(1, rows) if d != rows // 2]]
    request = lax.ppermute(packed, "row", exchanges(rows, rows // 2))
    requests = [lax.ppermute(packed, "row", exchanges(rows, d)) for d in groups[1]]
    asked_mid, send_mid = gather_first([request], groups[0], here, amplitudes, rows, cap)

    step = apart(rows, source, row)
    same = step[:, None] == step[None, :]
    before = (step[None, :] < step[:, None]) | (same & (slot_ids[None, :] < slot_ids[:, None]))
    turn = jnp.sum(before.astype(jnp.int32), axis=1)
    like = same & (turn[:, None] % 2 == turn[None, :] % 2) & (turn[None, :] < turn[:, None])
    place = jnp.sum(like.astype(jnp.int32), axis=1)
    mine = jnp.arange(half, dtype=jnp.int32) * 2 + core
    own_pick = mine[:, None] == turn[None, :]
    other_pick = (mine ^ 1)[:, None] == turn[None, :]

    def pick(chosen, values):
        return jnp.sum(jnp.where(chosen, values[None, :], jnp.zeros((), values.dtype)), axis=1)

    own = pick(own_pick, slot_ids)
    other = pick(other_pick, slot_ids)
    far_step = pick(own_pick, step)
    own_far = pick(own_pick, far_slot[:, 0])
    own_place = pick(own_pick, place)
    far_scale = pick(own_pick, far_weight[:, 0].astype(jnp.float32))
    first = pick(own_pick, first_occ)
    second = pick(own_pick, second_occ)
    orbitals = jnp.arange(occ_count, dtype=jnp.int32)

    def energy_of(index):
        found = index[:, None] == orbitals[None, :]
        return jnp.sum(jnp.where(found, occ_energy[None, :], jnp.float32(0.0)), axis=1)

    shift = energy_of(first) + energy_of(second)

    by_slot = turn // 2 + jnp.where(turn % 2 == core, 0, half)
    early = half - cap
    swap = [(0, 1), (1, 0)]
    remote = (rows - 1) * cap
    local_spots = [
        slot_ids,
        jnp.where(
            by_slot < half,
            by_slot + jnp.where(by_slot % half < early, 0, early),
            by_slot - half + jnp.where(by_slot % half < early, early, half),
        ),
    ]
    tables = []
    for where in (slot_ids, by_slot):
        at_home = remote + jnp.sum(
            jnp.where(own_far[:, None] == slot_ids[None, :], where[None, :], 0), axis=1
        )
        spot = jnp.where(far_step == 0, at_home, (far_step - 1) * cap + own_place)
        tables.append(jnp.concatenate([spot, first, second]))
    near = [near_slot, near_count[:, None], near_weight]
    columns = [slot_ids, jnp.concatenate([own, other])]
    ats = [own, jnp.arange(half, dtype=jnp.int32)]
    slots = jnp.concatenate([own[:early], other[:early], own[early:], other[early:]])
    (own, *moved, send_mid) = lax.optimization_barrier(
        (own, *tables, *columns, *ats, slots, send_mid)
    )
    tables, columns, ats, slots = moved[:2], moved[2:4], moved[4:6], moved[6]
    stores = [amplitudes]
    whole = [amplitudes]
    for sweep in range(ITERS):
        last = sweep == ITERS - 1
        again = min(sweep, 1)
        if sweep > 0:
            (send_mid,) = gather_again(asked_mid, local_spots[1], stores, cap)
        arrived = {}
        arrived[rows // 2] = lax.ppermute(send_mid, "row", returns(rows, rows // 2))
        if sweep == 0:
            (*requests, _) = lax.optimization_barrier((*requests, send_mid))
            asked, *sends = gather_first(
                requests, groups[1], here, amplitudes, rows, cap
            )
        else:
            sends = gather_again(asked, local_spots[1], stores, cap)
        for d, send in zip(groups[1], sends):
            arrived[d] = lax.ppermute(send, "row", returns(rows, d))
        arrived = [arrived[d] for d in range(1, rows)]
        prepared = prepare(
            own, ats[again], columns[again], shift, near, whole,
            integrals, fock_matrix, intersection,
        )
        spots = laid(arrived)
        homes = laid(whole, remote)
        done_early = finish(
            0, early, tables[again], far_scale, prepared, spots[:-1], homes, occ_count,
            last,
        )
        given_early = lax.ppermute(done_early[0], "rep", swap)
        done_late = finish(
            early, cap, tables[again], far_scale, prepared, spots, homes, occ_count, last
        )
        given_late = lax.ppermute(done_late[0], "rep", swap)
        stores = [done_early[0], given_early, done_late[0], given_late]
        whole = [
            jnp.concatenate([done_early[0], done_late[0]], axis=0),
            jnp.concatenate([given_early, given_late], axis=0),
        ]
    final = put_in_slots(slots, stores)
    occ_sum = (done_early[1] + done_late[1])[0]
    occ_sum = add_over(occ_sum, "rep")
    occ_sum = add_over(occ_sum, "col")
    occ_sum = add_over(occ_sum, "row")
    total_pairs = pairs * rows * lax.axis_size("col")
    occ_density = occ_sum * (occ_count / (2.0 * total_pairs * domain * domain))
    return (final, occ_density)


def solution(mesh):
    pair_spec = P(("groups", "row", "col"), None, None)
    flat = P(("groups", "row", "col"))
    table = P(("groups", "row", "col"), None)
    return jax.shard_map(
        per_device,
        mesh=mesh,
        in_specs=(
            pair_spec, pair_spec, pair_spec, pair_spec,
            P("groups"), flat, flat, table, flat, table, table, table, table,
        ),
        out_specs=(pair_spec, P("groups")),
        check_vma=False,
    )
```

```python
import jax
import jax.numpy as jnp
from jax import lax
from jax.experimental import pallas as pl
from jax.experimental.pallas import tpu as pltpu
from jax.sharding import PartitionSpec as P


ITERS = 2
ANY = pl.ANY
SMEM = pltpu.SMEM
VMEM = pltpu.VMEM
LANES = 16
MIB = 1 << 20


def ring(rows, row):
    return row if rows & (rows - 1) else row ^ (row >> 1)


def sent(rows, step):
    hop = (step + 1) // 2 if step % 2 else rows - step // 2
    where = {ring(rows, r): r for r in range(rows)}
    return [(r, where[(ring(rows, r) + hop) % rows]) for r in range(rows)]


def asked_of(rows, step):
    return [(b, a) for a, b in sent(rows, step)]


def step_of(rows, source, row):
    hop = ring(rows, row) - ring(rows, source)
    hop = jnp.where(hop < 0, hop + rows, hop)
    step = jnp.where(2 * hop <= rows, 2 * hop - 1, 2 * (rows - hop))
    return jnp.where(hop == 0, 0, step)


def limits(mib):
    return pltpu.CompilerParams(vmem_limit_bytes=mib * MIB)


def cost(flops, size):
    return pl.CostEstimate(flops=flops, transcendentals=0, bytes_accessed=size)


def fetch(candidates, spot, target):
    for offset, ref in candidates:

        @pl.when((spot >= offset) & (spot < offset + ref.shape[0]))
        def _(offset=offset, ref=ref):
            target[...] = ref[spot - offset]


def laid(refs, offset=0):
    placed = []
    for ref in refs:
        placed.append((offset, ref))
        offset += ref.shape[0]
    return placed


def gather_first(requests, shifts, place, amplitudes, rows, cap):
    pairs, domain = amplitudes.shape[:2]
    count_of = len(shifts)
    blocks = count_of * cap

    def body(place_ref, *refs):
        lists = refs[:count_of]
        store = refs[count_of]
        asked = refs[count_of + 1]
        outs = refs[count_of + 2 : -1]
        sem = refs[-1]
        me = place_ref[0]
        core = place_ref[1]
        for n, shift in enumerate(shifts):
            base = n * (cap + 1)
            asker = jnp.int32(0)
            for a, b in sent(rows, shift):
                asker = jnp.where(me == a, b, asker)
            for k in range(cap):
                asked[base + k] = 0
            sources = [lists[n][p] // pairs for p in range(pairs)]
            count = jnp.int32(0)
            for p in range(pairs):
                count = count + (step_of(rows, sources[p], asker) < shift).astype(jnp.int32)
            filled = jnp.int32(0)
            for p in range(pairs):
                mine = sources[p] == me
                taken = mine & (count % 2 == core)
                asked[base + jnp.minimum(filled, cap)] = lists[n][p] % pairs
                count = count + mine.astype(jnp.int32)
                filled = filled + taken.astype(jnp.int32)
            for k in range(cap):
                pltpu.make_async_copy(
                    store.at[asked[base + k]], outs[n].at[k], sem.at[n, k]
                ).start()
        for n in range(count_of):
            for k in range(cap):
                pltpu.make_async_copy(store.at[0], outs[n].at[k], sem.at[n, k]).wait()

    shape = (cap, domain, domain)
    return pl.pallas_call(
        body,
        out_shape=[jax.ShapeDtypeStruct((count_of * (cap + 1),), jnp.int32)]
        + [VMEM(shape, jnp.bfloat16)] * count_of,
        in_specs=[pl.BlockSpec(memory_space=SMEM)] * (count_of + 1)
        + [pl.BlockSpec(memory_space=pltpu.HBM)],
        out_specs=[pl.BlockSpec(memory_space=SMEM)]
        + [pl.BlockSpec(memory_space=VMEM)] * count_of,
        scratch_shapes=[pltpu.SemaphoreType.DMA((count_of, cap))],
        cost_estimate=cost(0, blocks * domain * domain * 4),
        compiler_params=limits(8),
        name="gather_first",
    )(place, *requests, pltpu.with_memory_space_constraint(amplitudes, pltpu.HBM))


def gather_again(asked, where, stores, cap):
    domain = stores[0].shape[1]
    lists = asked.shape[0] // (cap + 1)
    blocks = lists * cap

    def body(asked_ref, where_ref, *refs):
        sources = laid(refs[: len(stores)])
        outs = refs[len(stores) :]
        for b in range(blocks):
            spot = where_ref[asked_ref[b // cap * (cap + 1) + b % cap]]
            fetch(sources, spot, outs[b // cap].at[b % cap])

    return pl.pallas_call(
        body,
        out_shape=[VMEM((cap, domain, domain), jnp.bfloat16)] * lists,
        in_specs=[pl.BlockSpec(memory_space=SMEM)] * 2
        + [pl.BlockSpec(memory_space=VMEM)] * len(stores),
        out_specs=[pl.BlockSpec(memory_space=VMEM)] * lists,
        cost_estimate=cost(0, blocks * domain * domain * 4),
        compiler_params=limits(8),
        name="gather_again",
    )(asked, where, *stores)


def prepare(own, at, columns, shift, near, stores, integrals, fock_matrix, intersection):
    half = own.shape[0]
    domain = integrals.shape[1]
    total = columns.shape[0]
    entries = near[0].shape[1]
    groups = domain // LANES // half
    strip = groups * LANES

    def spread_weights(own_ref, column_ref, slot_ref, count_ref, weight_ref, spread_ref):
        lane = lax.broadcasted_iota(jnp.int32, (total, total), 1)
        weights = jnp.zeros((total, total), jnp.float32)
        for k in range(entries):
            used = (slot_ref[:, k : k + 1] == lane) & (k < count_ref[...])
            wide = weight_ref[:, k : k + 1].astype(jnp.float32)
            weights = weights + jnp.where(used, wide, jnp.float32(0.0))
        weights = weights.astype(jnp.bfloat16)
        shape = (half * LANES, total)
        row = lax.broadcasted_iota(jnp.int32, shape, 0) // LANES
        wanted = jnp.zeros(shape, jnp.int32)
        for n in range(half):
            wanted = jnp.where(row == n, own_ref[n], wanted)
        pick = lax.broadcasted_iota(jnp.int32, shape, 1) == wanted
        mine = jnp.dot(
            pick.astype(jnp.float32).astype(jnp.bfloat16),
            weights,
            preferred_element_type=jnp.float32,
        ).astype(jnp.bfloat16)
        shape = (total, total * LANES)
        column = lax.broadcasted_iota(jnp.int32, shape, 1) // LANES
        wanted = jnp.zeros(shape, jnp.int32)
        for n in range(total):
            wanted = jnp.where(column == n, column_ref[n], wanted)
        pick = lax.broadcasted_iota(jnp.int32, shape, 0) == wanted
        full = jnp.dot(
            mine,
            pick.astype(jnp.float32).astype(jnp.bfloat16),
            preferred_element_type=jnp.float32,
        )
        shape = (half * LANES, total * LANES)
        down = lax.broadcasted_iota(jnp.int32, shape, 0) % LANES
        along = lax.broadcasted_iota(jnp.int32, shape, 1) % LANES
        spread_ref[...] = jnp.where(down == along, full, 0.0).astype(jnp.bfloat16)

    def body(own_ref, at_ref, column_ref, shift_ref, slot_ref, count_ref, weight_ref, *refs):
        sources = refs[: len(stores)]
        (integ_ref, fock_ref, over_ref, local_ref, rest_ref, recip_ref, keep_ref, spread_ref) = (
            refs[len(stores) :]
        )
        i = pl.program_id(0)

        @pl.when(i == 0)
        def _():
            spread_weights(own_ref, column_ref, slot_ref, count_ref, weight_ref, spread_ref)

        for g in range(groups):
            rows = pl.ds(pl.multiple_of(i * strip + g * LANES, LANES), LANES)
            part = [s[:, rows, :].reshape(s.shape[0] * LANES, domain) for s in sources]
            part = part[0] if len(part) == 1 else jnp.concatenate(part, axis=0)
            sums = jnp.dot(spread_ref[...], part, preferred_element_type=jnp.float32)
            local_ref[:, g * LANES : (g + 1) * LANES, :] = sums.reshape(half, LANES, domain)
        amps = sources[0][at_ref[i]]
        fock = fock_ref[0]
        wide = amps.astype(jnp.float32)
        left = jnp.dot(fock, amps, preferred_element_type=jnp.float32)
        right = jnp.dot(amps, fock, preferred_element_type=jnp.float32)
        row_id = lax.broadcasted_iota(jnp.int32, (domain, domain), 0)
        col_id = lax.broadcasted_iota(jnp.int32, (domain, domain), 1)
        diagonal = jnp.where(row_id == col_id, fock.astype(jnp.float32), 0.0)
        across = jnp.sum(diagonal, axis=0, keepdims=True)
        down = jnp.sum(diagonal, axis=1, keepdims=True)
        residual = integ_ref[0].astype(jnp.float32) + left + right - shift_ref[i] * wide
        recip = 1.0 / (down + across - shift_ref[i])
        recip_ref[0] = recip
        rest_ref[0] = wide - residual * recip
        keep_ref[0] = over_ref[0]

    block = (1, domain, domain)
    mine = pl.BlockSpec(block, lambda i, own, *_: (own[i], 0, 0))
    in_turn = pl.BlockSpec(block, lambda i, *_: (i, 0, 0))
    wide_shape = jax.ShapeDtypeStruct((half, domain, domain), jnp.float32)
    return pl.pallas_call(
        body,
        grid_spec=pltpu.PrefetchScalarGridSpec(
            num_scalar_prefetch=4,
            grid=(half,),
            in_specs=[pl.BlockSpec(n.shape, lambda i, *_: (0, 0)) for n in near]
            + [pl.BlockSpec(s.shape, lambda i, *_: (0, 0, 0)) for s in stores]
            + [mine, mine, mine],
            out_specs=[
                pl.BlockSpec((half, strip, domain), lambda i, *_: (0, i, 0)),
                in_turn,
                in_turn,
                in_turn,
            ],
            scratch_shapes=[VMEM((half * LANES, total * LANES), jnp.bfloat16)],
        ),
        out_shape=[
            wide_shape,
            wide_shape,
            wide_shape,
            jax.ShapeDtypeStruct((half, domain, domain), jnp.bfloat16),
        ],
        cost_estimate=cost(
            2 * half * domain**3 * 3,
            (total + 4 * half) * domain * domain * 2 + half * domain * domain * 12,
        ),
        compiler_params=limits(20),
        name="prepare",
    )(own, at, columns, shift, *near, *stores, integrals, fock_matrix, intersection)


def finish(start, count, numbers, scale, prepared, arrived, stores, occ_count, last):
    half, domain = prepared[0].shape[:2]

    def body(number_ref, scale_ref, local_ref, rest_ref, recip_ref, over_ref, *refs):
        candidates = [
            (offset, ref) for offset, ref in zip([o for o, _ in arrived + stores], refs)
        ]
        outs = refs[len(candidates) : -1]
        hold = refs[-1]
        for n in range(count):
            fetch(candidates, number_ref[start + n], hold.at[n])
        if last:
            row_id = lax.broadcasted_iota(jnp.int32, (domain, domain), 0)
            col_id = lax.broadcasted_iota(jnp.int32, (domain, domain), 1)
            on_diagonal = row_id == col_id
            orbital = lax.broadcasted_iota(jnp.int32, (1, occ_count), 1)
            density = jnp.zeros((1, occ_count), jnp.float32)
        for n in range(count):
            i = start + n
            coupled = local_ref[i] + scale_ref[i] * hold[n].astype(jnp.float32)
            over = over_ref[i]
            projected = jnp.dot(
                over, coupled.astype(jnp.bfloat16), preferred_element_type=jnp.float32
            )
            back = lax.dot_general(
                projected.astype(jnp.bfloat16),
                over,
                (((1,), (1,)), ((), ())),
                preferred_element_type=jnp.float32,
            )
            fresh = (rest_ref[i] + back * recip_ref[i]).astype(jnp.bfloat16)
            outs[0][n] = fresh
            if last:
                wide = fresh.astype(jnp.float32)
                square = jnp.dot(fresh, fresh, preferred_element_type=jnp.float32)
                terms = 2.0 * wide * wide - jnp.where(on_diagonal, square, 0.0)
                norm = jnp.sum(jnp.sum(terms, axis=0, keepdims=True), axis=1, keepdims=True)
                picks = (orbital == number_ref[half + i]).astype(jnp.float32)
                picks = picks + (orbital == number_ref[2 * half + i]).astype(jnp.float32)
                density = density + norm * picks
        if last:
            outs[1][...] = density

    out_shape = [VMEM((count, domain, domain), jnp.bfloat16)]
    if last:
        out_shape.append(VMEM((1, occ_count), jnp.float32))
    return pl.pallas_call(
        body,
        out_shape=out_shape,
        in_specs=[pl.BlockSpec(memory_space=SMEM)] * 2
        + [pl.BlockSpec(memory_space=VMEM)] * 4
        + [pl.BlockSpec(memory_space=VMEM)] * len(arrived + stores),
        out_specs=[pl.BlockSpec(memory_space=VMEM)] * len(out_shape),
        scratch_shapes=[VMEM((count, domain, domain), jnp.bfloat16)],
        cost_estimate=cost(2 * count * domain**3 * 2, count * domain * domain * 18),
        compiler_params=limits(16),
        name="finish",
    )(numbers, scale, *prepared, *[a for _, a in arrived + stores])


def put_in_slots(slots, stores):
    domain = stores[0].shape[1]
    total = slots.shape[0]

    def body(slot_ref, *refs):
        sources = refs[: len(stores)]
        out_ref, sem = refs[-2:]
        copies = []
        for source in sources:
            for n in range(source.shape[0]):
                at = len(copies)
                copies.append(
                    pltpu.make_async_copy(source.at[n], out_ref.at[slot_ref[at]], sem.at[at])
                )
        for copy in copies:
            copy.start()
        for copy in copies:
            copy.wait()

    return pl.pallas_call(
        body,
        out_shape=jax.ShapeDtypeStruct((total, domain, domain), jnp.bfloat16),
        in_specs=[pl.BlockSpec(memory_space=SMEM)]
        + [pl.BlockSpec(memory_space=VMEM)] * len(stores),
        out_specs=pl.BlockSpec(memory_space=ANY),
        scratch_shapes=[pltpu.SemaphoreType.DMA((total,))],
        cost_estimate=cost(0, total * domain * domain * 4),
        compiler_params=limits(8),
        name="put_in_slots",
    )(slots, *stores)


def add_over(values, name):
    size = lax.axis_size(name)
    if size & (size - 1):
        return lax.psum(values, name)
    step = 1
    while step < size:
        values = values + lax.ppermute(values, name, [(r, r ^ step) for r in range(size)])
        step *= 2
    return values


def per_device(
    amplitudes,
    integrals,
    fock_matrix,
    intersection,
    occ_energy,
    first_occ,
    second_occ,
    near_slot,
    near_count,
    near_weight,
    far_chip,
    far_slot,
    far_weight,
):
    pairs, domain = amplitudes.shape[:2]
    rows = lax.axis_size("row")
    half = pairs // 2
    cap = pairs // rows
    row = lax.axis_index("row")
    core = lax.axis_index("rep")
    occ_count = occ_energy.shape[0]
    slot_ids = jnp.arange(pairs, dtype=jnp.int32)
    source = far_chip[:, 0]
    packed = source * pairs + far_slot[:, 0]
    here = jnp.stack([row, core]).astype(jnp.int32)
    groups = [[1], list(range(2, rows))]
    request = lax.ppermute(packed, "row", asked_of(rows, 1))
    requests = [lax.ppermute(packed, "row", asked_of(rows, d)) for d in groups[1]]
    asked_lead, send_lead = gather_first([request], groups[0], here, amplitudes, rows, cap)

    step = step_of(rows, source, row)
    same = step[:, None] == step[None, :]
    before = (step[None, :] < step[:, None]) | (same & (slot_ids[None, :] < slot_ids[:, None]))
    turn = jnp.sum(before.astype(jnp.int32), axis=1)
    like = same & (turn[:, None] % 2 == turn[None, :] % 2) & (turn[None, :] < turn[:, None])
    place = jnp.sum(like.astype(jnp.int32), axis=1)
    mine = jnp.arange(half, dtype=jnp.int32) * 2 + core
    own_pick = mine[:, None] == turn[None, :]
    other_pick = (mine ^ 1)[:, None] == turn[None, :]

    def pick(chosen, values):
        return jnp.sum(jnp.where(chosen, values[None, :], jnp.zeros((), values.dtype)), axis=1)

    own = pick(own_pick, slot_ids)
    other = pick(other_pick, slot_ids)
    far_step = pick(own_pick, step)
    own_far = pick(own_pick, far_slot[:, 0])
    own_place = pick(own_pick, place)
    far_scale = pick(own_pick, far_weight[:, 0].astype(jnp.float32))
    first = pick(own_pick, first_occ)
    second = pick(own_pick, second_occ)
    orbitals = jnp.arange(occ_count, dtype=jnp.int32)

    def energy_of(index):
        found = index[:, None] == orbitals[None, :]
        return jnp.sum(jnp.where(found, occ_energy[None, :], jnp.float32(0.0)), axis=1)

    shift = energy_of(first) + energy_of(second)

    by_slot = turn // 2 + jnp.where(turn % 2 == core, 0, half)
    early = half - cap
    swap = [(0, 1), (1, 0)]
    remote = (rows - 1) * cap
    local_spots = [
        slot_ids,
        jnp.where(
            by_slot < half,
            by_slot + jnp.where(by_slot % half < early, 0, early),
            by_slot - half + jnp.where(by_slot % half < early, early, half),
        ),
    ]
    tables = []
    for where in (slot_ids, by_slot):
        at_home = remote + jnp.sum(
            jnp.where(own_far[:, None] == slot_ids[None, :], where[None, :], 0), axis=1
        )
        spot = jnp.where(far_step == 0, at_home, (far_step - 1) * cap + own_place)
        tables.append(jnp.concatenate([spot, first, second]))
    near = [near_slot, near_count[:, None], near_weight]
    columns = [slot_ids, jnp.concatenate([own, other])]
    ats = [own, jnp.arange(half, dtype=jnp.int32)]
    slots = jnp.concatenate([own[:early], other[:early], own[early:], other[early:]])
    (own, *moved, send_lead) = lax.optimization_barrier(
        (own, *tables, *columns, *ats, slots, send_lead)
    )
    tables, columns, ats, slots = moved[:2], moved[2:4], moved[4:6], moved[6]
    stores = [amplitudes]
    whole = [amplitudes]
    for sweep in range(ITERS):
        last = sweep == ITERS - 1
        again = min(sweep, 1)
        if sweep > 0:
            (send_lead,) = gather_again(asked_lead, local_spots[1], stores, cap)
        arrived = {}
        arrived[1] = lax.ppermute(send_lead, "row", sent(rows, 1))
        if sweep == 0:
            (*requests, _) = lax.optimization_barrier((*requests, send_lead))
            asked, *sends = gather_first(
                requests, groups[1], here, amplitudes, rows, cap
            )
        else:
            sends = gather_again(asked, local_spots[1], stores, cap)
        for d, send in zip(groups[1], sends):
            arrived[d] = lax.ppermute(send, "row", sent(rows, d))
        arrived = [arrived[d] for d in range(1, rows)]
        prepared = prepare(
            own, ats[again], columns[again], shift, near, whole,
            integrals, fock_matrix, intersection,
        )
        spots = laid(arrived)
        homes = laid(whole, remote)
        done_early = finish(
            0, early, tables[again], far_scale, prepared, spots[:-1], homes, occ_count,
            last,
        )
        given_early = lax.ppermute(done_early[0], "rep", swap)
        done_late = finish(
            early, cap, tables[again], far_scale, prepared, spots, homes, occ_count, last
        )
        given_late = lax.ppermute(done_late[0], "rep", swap)
        stores = [done_early[0], given_early, done_late[0], given_late]
        whole = [
            jnp.concatenate([done_early[0], done_late[0]], axis=0),
            jnp.concatenate([given_early, given_late], axis=0),
        ]
    final = put_in_slots(slots, stores)
    occ_sum = (done_early[1] + done_late[1])[0]
    occ_sum = add_over(occ_sum, "rep")
    occ_sum = add_over(occ_sum, "col")
    occ_sum = add_over(occ_sum, "row")
    total_pairs = pairs * rows * lax.axis_size("col")
    occ_density = occ_sum * (occ_count / (2.0 * total_pairs * domain * domain))
    return (final, occ_density)


def solution(mesh):
    pair_spec = P(("groups", "row", "col"), None, None)
    flat = P(("groups", "row", "col"))
    table = P(("groups", "row", "col"), None)
    return jax.shard_map(
        per_device,
        mesh=mesh,
        in_specs=(
            pair_spec, pair_spec, pair_spec, pair_spec,
            P("groups"), flat, flat, table, flat, table, table, table, table,
        ),
        out_specs=(pair_spec, P("groups")),
        check_vma=False,
    )
```

```python
import jax
import jax.numpy as jnp
from jax import lax
from jax.experimental import pallas as pl
from jax.experimental.pallas import tpu as pltpu
from jax.sharding import PartitionSpec as P


ITERS = 2
ANY = pl.ANY
SMEM = pltpu.SMEM
VMEM = pltpu.VMEM
LANES = 16
MIB = 1 << 20


def ring(rows, row):
    return row if rows & (rows - 1) else row ^ (row >> 1)


def sent(rows, step):
    hop = (step + 1) // 2 if step % 2 else rows - step // 2
    where = {ring(rows, r): r for r in range(rows)}
    return [(r, where[(ring(rows, r) + hop) % rows]) for r in range(rows)]


def asked_of(rows, step):
    return [(b, a) for a, b in sent(rows, step)]


def step_of(rows, source, row):
    hop = ring(rows, row) - ring(rows, source)
    hop = jnp.where(hop < 0, hop + rows, hop)
    step = jnp.where(2 * hop <= rows, 2 * hop - 1, 2 * (rows - hop))
    return jnp.where(hop == 0, 0, step)


def limits(mib):
    return pltpu.CompilerParams(vmem_limit_bytes=mib * MIB)


def cost(flops, size):
    return pl.CostEstimate(flops=flops, transcendentals=0, bytes_accessed=size)


def fetch(candidates, spot, target):
    for offset, ref in candidates:

        @pl.when((spot >= offset) & (spot < offset + ref.shape[0]))
        def _(offset=offset, ref=ref):
            target[...] = ref[spot - offset]


def laid(refs, offset=0):
    placed = []
    for ref in refs:
        placed.append((offset, ref))
        offset += ref.shape[0]
    return placed


def gather_first(requests, shifts, place, amplitudes, rows, cap):
    pairs, domain = amplitudes.shape[:2]
    count_of = len(shifts)
    blocks = count_of * cap
    bits = pairs.bit_length() - 1

    def body(place_ref, *refs):
        lists = refs[:count_of]
        store = refs[count_of]
        asked = refs[count_of + 1]
        outs = refs[count_of + 2 : -1]
        sem = refs[-1]
        me = place_ref[0]
        core = place_ref[1]
        for n, step in enumerate(shifts):
            base = n * (cap + 1)
            asker = jnp.int32(0)
            for a, b in sent(rows, step):
                asker = jnp.where(me == a, b, asker)
            served = [asker]
            for sooner in range(1, step):
                server = jnp.int32(0)
                for a, b in sent(rows, sooner):
                    server = jnp.where(asker == b, a, server)
                served.append(server)
            for k in range(cap):
                asked[base + k] = 0
            entries = [lists[n][p] for p in range(pairs)]
            sources = [entry // pairs if pairs & (pairs - 1) else entry >> bits for entry in entries]
            count = jnp.int32(0)
            for p in range(pairs):
                for server in served:
                    count = count + (sources[p] == server).astype(jnp.int32)
            filled = jnp.int32(0)
            for p in range(pairs):
                mine = (sources[p] == me).astype(jnp.int32)
                asked[base + jnp.minimum(filled, cap)] = entries[p] - sources[p] * pairs
                filled = filled + jnp.where((count & 1) == core, mine, 0)
                count = count + mine
            for k in range(cap):
                pltpu.make_async_copy(
                    store.at[asked[base + k]], outs[n].at[k], sem.at[n, k]
                ).start()
        for n in range(count_of):
            for k in range(cap):
                pltpu.make_async_copy(store.at[0], outs[n].at[k], sem.at[n, k]).wait()

    shape = (cap, domain, domain)
    return pl.pallas_call(
        body,
        out_shape=[jax.ShapeDtypeStruct((count_of * (cap + 1),), jnp.int32)]
        + [VMEM(shape, jnp.bfloat16)] * count_of,
        in_specs=[pl.BlockSpec(memory_space=SMEM)] * (count_of + 1)
        + [pl.BlockSpec(memory_space=pltpu.HBM)],
        out_specs=[pl.BlockSpec(memory_space=SMEM)]
        + [pl.BlockSpec(memory_space=VMEM)] * count_of,
        scratch_shapes=[pltpu.SemaphoreType.DMA((count_of, cap))],
        cost_estimate=cost(0, blocks * domain * domain * 4),
        compiler_params=limits(8),
        name="gather_first",
    )(place, *requests, pltpu.with_memory_space_constraint(amplitudes, pltpu.HBM))


def gather_again(asked, where, stores, cap):
    domain = stores[0].shape[1]
    lists = asked.shape[0] // (cap + 1)
    blocks = lists * cap

    def body(asked_ref, where_ref, *refs):
        sources = laid(refs[: len(stores)])
        outs = refs[len(stores) :]
        for b in range(blocks):
            spot = where_ref[asked_ref[b // cap * (cap + 1) + b % cap]]
            fetch(sources, spot, outs[b // cap].at[b % cap])

    return pl.pallas_call(
        body,
        out_shape=[VMEM((cap, domain, domain), jnp.bfloat16)] * lists,
        in_specs=[pl.BlockSpec(memory_space=SMEM)] * 2
        + [pl.BlockSpec(memory_space=VMEM)] * len(stores),
        out_specs=[pl.BlockSpec(memory_space=VMEM)] * lists,
        cost_estimate=cost(0, blocks * domain * domain * 4),
        compiler_params=limits(8),
        name="gather_again",
    )(asked, where, *stores)


def prepare(own, at, columns, counts, shift, near, stores, integrals, fock_matrix, intersection):
    half = own.shape[0]
    domain = integrals.shape[1]
    total = columns.shape[0]
    entries = near[0].shape[1]
    groups = domain // LANES // half
    strip = groups * LANES

    def spread_weights(own_ref, column_ref, slot_ref, count_ref, weight_ref, spread_ref):
        lane = lax.broadcasted_iota(jnp.int32, (total, total), 1)
        down = lax.broadcasted_iota(jnp.int32, (total, total), 0)
        used_count = jnp.zeros((total, total), jnp.int32)
        for n in range(total):
            used_count = jnp.where(down == n, count_ref[n], used_count)
        weights = jnp.zeros((total, total), jnp.float32)
        for k in range(entries):
            used = (slot_ref[:, k : k + 1] == lane) & (k < used_count)
            wide = weight_ref[:, k : k + 1].astype(jnp.float32)
            weights = weights + jnp.where(used, wide, jnp.float32(0.0))
        weights = weights.astype(jnp.bfloat16)
        shape = (half * LANES, total)
        row = lax.broadcasted_iota(jnp.int32, shape, 0) // LANES
        wanted = jnp.zeros(shape, jnp.int32)
        for n in range(half):
            wanted = jnp.where(row == n, own_ref[n], wanted)
        pick = lax.broadcasted_iota(jnp.int32, shape, 1) == wanted
        mine = jnp.dot(
            pick.astype(jnp.float32).astype(jnp.bfloat16),
            weights,
            preferred_element_type=jnp.float32,
        ).astype(jnp.bfloat16)
        shape = (total, total * LANES)
        column = lax.broadcasted_iota(jnp.int32, shape, 1) // LANES
        wanted = jnp.zeros(shape, jnp.int32)
        for n in range(total):
            wanted = jnp.where(column == n, column_ref[n], wanted)
        pick = lax.broadcasted_iota(jnp.int32, shape, 0) == wanted
        full = jnp.dot(
            mine,
            pick.astype(jnp.float32).astype(jnp.bfloat16),
            preferred_element_type=jnp.float32,
        )
        shape = (half * LANES, total * LANES)
        down = lax.broadcasted_iota(jnp.int32, shape, 0) % LANES
        along = lax.broadcasted_iota(jnp.int32, shape, 1) % LANES
        spread_ref[...] = jnp.where(down == along, full, 0.0).astype(jnp.bfloat16)

    def body(
        own_ref, at_ref, column_ref, count_ref, shift_ref, slot_ref, weight_ref, *refs
    ):
        sources = refs[: len(stores)]
        (integ_ref, fock_ref, over_ref, local_ref, rest_ref, recip_ref, keep_ref, spread_ref) = (
            refs[len(stores) :]
        )
        i = pl.program_id(0)

        @pl.when(i == 0)
        def _():
            spread_weights(own_ref, column_ref, slot_ref, count_ref, weight_ref, spread_ref)

        for g in range(groups):
            rows = pl.ds(pl.multiple_of(i * strip + g * LANES, LANES), LANES)
            part = [s[:, rows, :].reshape(s.shape[0] * LANES, domain) for s in sources]
            part = part[0] if len(part) == 1 else jnp.concatenate(part, axis=0)
            sums = jnp.dot(spread_ref[...], part, preferred_element_type=jnp.float32)
            local_ref[:, g * LANES : (g + 1) * LANES, :] = sums.reshape(half, LANES, domain)
        amps = sources[0][at_ref[i]]
        fock = fock_ref[0]
        wide = amps.astype(jnp.float32)
        left = jnp.dot(fock, amps, preferred_element_type=jnp.float32)
        right = jnp.dot(amps, fock, preferred_element_type=jnp.float32)
        row_id = lax.broadcasted_iota(jnp.int32, (domain, domain), 0)
        col_id = lax.broadcasted_iota(jnp.int32, (domain, domain), 1)
        diagonal = jnp.where(row_id == col_id, fock.astype(jnp.float32), 0.0)
        across = jnp.sum(diagonal, axis=0, keepdims=True)
        down = jnp.sum(diagonal, axis=1, keepdims=True)
        residual = integ_ref[0].astype(jnp.float32) + left + right - shift_ref[i] * wide
        recip = 1.0 / (down + across - shift_ref[i])
        recip_ref[0] = recip
        rest_ref[0] = wide - residual * recip
        keep_ref[0] = over_ref[0]

    block = (1, domain, domain)
    mine = pl.BlockSpec(block, lambda i, own, *_: (own[i], 0, 0))
    in_turn = pl.BlockSpec(block, lambda i, *_: (i, 0, 0))
    wide_shape = jax.ShapeDtypeStruct((half, domain, domain), jnp.float32)
    return pl.pallas_call(
        body,
        grid_spec=pltpu.PrefetchScalarGridSpec(
            num_scalar_prefetch=5,
            grid=(half,),
            in_specs=[pl.BlockSpec(n.shape, lambda i, *_: (0, 0)) for n in near]
            + [pl.BlockSpec(s.shape, lambda i, *_: (0, 0, 0)) for s in stores]
            + [mine, mine, mine],
            out_specs=[
                pl.BlockSpec((half, strip, domain), lambda i, *_: (0, i, 0)),
                in_turn,
                in_turn,
                in_turn,
            ],
            scratch_shapes=[VMEM((half * LANES, total * LANES), jnp.bfloat16)],
        ),
        out_shape=[
            wide_shape,
            wide_shape,
            wide_shape,
            jax.ShapeDtypeStruct((half, domain, domain), jnp.bfloat16),
        ],
        cost_estimate=cost(
            2 * half * domain**3 * 3,
            (total + 4 * half) * domain * domain * 2 + half * domain * domain * 12,
        ),
        compiler_params=limits(20),
        name="prepare",
    )(own, at, columns, counts, shift, *near, *stores, integrals, fock_matrix, intersection)


def finish(start, count, numbers, scale, prepared, arrived, stores, occ_count, last):
    half, domain = prepared[0].shape[:2]

    def body(number_ref, scale_ref, local_ref, rest_ref, recip_ref, over_ref, *refs):
        candidates = [
            (offset, ref) for offset, ref in zip([o for o, _ in arrived + stores], refs)
        ]
        outs = refs[len(candidates) : -1]
        hold = refs[-1]
        for n in range(count):
            fetch(candidates, number_ref[start + n], hold.at[n])
        if last:
            row_id = lax.broadcasted_iota(jnp.int32, (domain, domain), 0)
            col_id = lax.broadcasted_iota(jnp.int32, (domain, domain), 1)
            on_diagonal = row_id == col_id
            orbital = lax.broadcasted_iota(jnp.int32, (1, occ_count), 1)
            density = jnp.zeros((1, occ_count), jnp.float32)
        for n in range(count):
            i = start + n
            coupled = local_ref[i] + scale_ref[i] * hold[n].astype(jnp.float32)
            over = over_ref[i]
            projected = jnp.dot(
                over, coupled.astype(jnp.bfloat16), preferred_element_type=jnp.float32
            )
            back = lax.dot_general(
                projected.astype(jnp.bfloat16),
                over,
                (((1,), (1,)), ((), ())),
                preferred_element_type=jnp.float32,
            )
            fresh = (rest_ref[i] + back * recip_ref[i]).astype(jnp.bfloat16)
            outs[0][n] = fresh
            if last:
                wide = fresh.astype(jnp.float32)
                square = jnp.dot(fresh, fresh, preferred_element_type=jnp.float32)
                terms = 2.0 * wide * wide - jnp.where(on_diagonal, square, 0.0)
                norm = jnp.sum(jnp.sum(terms, axis=0, keepdims=True), axis=1, keepdims=True)
                picks = (orbital == number_ref[half + i]).astype(jnp.float32)
                picks = picks + (orbital == number_ref[2 * half + i]).astype(jnp.float32)
                density = density + norm * picks
        if last:
            outs[1][...] = density

    out_shape = [VMEM((count, domain, domain), jnp.bfloat16)]
    if last:
        out_shape.append(VMEM((1, occ_count), jnp.float32))
    return pl.pallas_call(
        body,
        out_shape=out_shape,
        in_specs=[pl.BlockSpec(memory_space=SMEM)] * 2
        + [pl.BlockSpec(memory_space=VMEM)] * 4
        + [pl.BlockSpec(memory_space=VMEM)] * len(arrived + stores),
        out_specs=[pl.BlockSpec(memory_space=VMEM)] * len(out_shape),
        scratch_shapes=[VMEM((count, domain, domain), jnp.bfloat16)],
        cost_estimate=cost(2 * count * domain**3 * 2, count * domain * domain * 18),
        compiler_params=limits(16),
        name="finish",
    )(numbers, scale, *prepared, *[a for _, a in arrived + stores])


def put_in_slots(slots, stores):
    domain = stores[0].shape[1]
    total = slots.shape[0]

    def body(slot_ref, *refs):
        sources = refs[: len(stores)]
        out_ref, sem = refs[-2:]
        copies = []
        for source in sources:
            for n in range(source.shape[0]):
                at = len(copies)
                copies.append(
                    pltpu.make_async_copy(source.at[n], out_ref.at[slot_ref[at]], sem.at[at])
                )
        for copy in copies:
            copy.start()
        for copy in copies:
            copy.wait()

    return pl.pallas_call(
        body,
        out_shape=jax.ShapeDtypeStruct((total, domain, domain), jnp.bfloat16),
        in_specs=[pl.BlockSpec(memory_space=SMEM)]
        + [pl.BlockSpec(memory_space=VMEM)] * len(stores),
        out_specs=pl.BlockSpec(memory_space=ANY),
        scratch_shapes=[pltpu.SemaphoreType.DMA((total,))],
        cost_estimate=cost(0, total * domain * domain * 4),
        compiler_params=limits(8),
        name="put_in_slots",
    )(slots, *stores)


def add_over(values, name):
    size = lax.axis_size(name)
    if size & (size - 1):
        return lax.psum(values, name)
    step = 1
    while step < size:
        values = values + lax.ppermute(values, name, [(r, r ^ step) for r in range(size)])
        step *= 2
    return values


def per_device(
    amplitudes,
    integrals,
    fock_matrix,
    intersection,
    occ_energy,
    first_occ,
    second_occ,
    near_slot,
    near_count,
    near_weight,
    far_chip,
    far_slot,
    far_weight,
):
    pairs, domain = amplitudes.shape[:2]
    rows = lax.axis_size("row")
    half = pairs // 2
    cap = pairs // rows
    row = lax.axis_index("row")
    core = lax.axis_index("rep")
    occ_count = occ_energy.shape[0]
    slot_ids = jnp.arange(pairs, dtype=jnp.int32)
    source = far_chip[:, 0]
    packed = source * pairs + far_slot[:, 0]
    here = jnp.stack([row, core]).astype(jnp.int32)
    groups = [[1], list(range(2, rows))]
    request = lax.ppermute(packed, "row", asked_of(rows, 1))
    requests = [lax.ppermute(packed, "row", asked_of(rows, d)) for d in groups[1]]
    asked_lead, send_lead = gather_first([request], groups[0], here, amplitudes, rows, cap)

    step = step_of(rows, source, row)
    same = step[:, None] == step[None, :]
    before = (step[None, :] < step[:, None]) | (same & (slot_ids[None, :] < slot_ids[:, None]))
    turn = jnp.sum(before.astype(jnp.int32), axis=1)
    like = same & (turn[:, None] % 2 == turn[None, :] % 2) & (turn[None, :] < turn[:, None])
    place = jnp.sum(like.astype(jnp.int32), axis=1)
    mine = jnp.arange(half, dtype=jnp.int32) * 2 + core
    own_pick = mine[:, None] == turn[None, :]
    other_pick = (mine ^ 1)[:, None] == turn[None, :]

    def pick(chosen, values):
        return jnp.sum(jnp.where(chosen, values[None, :], jnp.zeros((), values.dtype)), axis=1)

    own = pick(own_pick, slot_ids)
    other = pick(other_pick, slot_ids)
    far_step = pick(own_pick, step)
    own_far = pick(own_pick, far_slot[:, 0])
    own_place = pick(own_pick, place)

    occ_energy, first_occ, second_occ, far_weight, _ = lax.optimization_barrier(
        (occ_energy, first_occ, second_occ, far_weight, asked_lead)
    )
    orbitals = jnp.arange(occ_count, dtype=jnp.int32)

    def energy_of(index):
        found = index[:, None] == orbitals[None, :]
        return jnp.sum(jnp.where(found, occ_energy[None, :], jnp.float32(0.0)), axis=1)

    far_scale = pick(own_pick, far_weight[:, 0].astype(jnp.float32))
    first = pick(own_pick, first_occ)
    second = pick(own_pick, second_occ)
    shift = energy_of(first) + energy_of(second)

    by_slot = turn // 2 + jnp.where(turn % 2 == core, 0, half)
    early = half - cap
    swap = [(0, 1), (1, 0)]
    remote = (rows - 1) * cap
    local_spots = [
        slot_ids,
        jnp.where(
            by_slot < half,
            by_slot + jnp.where(by_slot % half < early, 0, early),
            by_slot - half + jnp.where(by_slot % half < early, early, half),
        ),
    ]
    tables = []
    for where in (slot_ids, by_slot):
        at_home = remote + jnp.sum(
            jnp.where(own_far[:, None] == slot_ids[None, :], where[None, :], 0), axis=1
        )
        spot = jnp.where(far_step == 0, at_home, (far_step - 1) * cap + own_place)
        tables.append(jnp.concatenate([spot, first, second]))
    near = [near_slot, near_weight]
    columns = [slot_ids, jnp.concatenate([own, other])]
    ats = [own, jnp.arange(half, dtype=jnp.int32)]
    slots = jnp.concatenate([own[:early], other[:early], own[early:], other[early:]])
    stores = [amplitudes]
    whole = [amplitudes]
    for sweep in range(ITERS):
        last = sweep == ITERS - 1
        again = min(sweep, 1)
        if sweep > 0:
            (send_lead,) = gather_again(asked_lead, local_spots[1], stores, cap)
        arrived = {}
        arrived[1] = lax.ppermute(send_lead, "row", sent(rows, 1))
        if sweep == 0:
            (*requests, _) = lax.optimization_barrier((*requests, send_lead))
            asked, *sends = gather_first(
                requests, groups[1], here, amplitudes, rows, cap
            )
        else:
            sends = gather_again(asked, local_spots[1], stores, cap)
        for d, send in zip(groups[1], sends):
            arrived[d] = lax.ppermute(send, "row", sent(rows, d))
        arrived = [arrived[d] for d in range(1, rows)]
        prepared = prepare(
            own, ats[again], columns[again], near_count, shift, near, whole,
            integrals, fock_matrix, intersection,
        )
        spots = laid(arrived)
        homes = laid(whole, remote)
        done_early = finish(
            0, early, tables[again], far_scale, prepared, spots[:-1], homes, occ_count,
            last,
        )
        given_early = lax.ppermute(done_early[0], "rep", swap)
        done_late = finish(
            early, cap, tables[again], far_scale, prepared, spots, homes, occ_count, last
        )
        given_late = lax.ppermute(done_late[0], "rep", swap)
        stores = [done_early[0], given_early, done_late[0], given_late]
        whole = [
            jnp.concatenate([done_early[0], done_late[0]], axis=0),
            jnp.concatenate([given_early, given_late], axis=0),
        ]
    final = put_in_slots(slots, stores)
    occ_sum = (done_early[1] + done_late[1])[0]
    occ_sum = add_over(occ_sum, "rep")
    occ_sum = add_over(occ_sum, "col")
    occ_sum = add_over(occ_sum, "row")
    total_pairs = pairs * rows * lax.axis_size("col")
    occ_density = occ_sum * (occ_count / (2.0 * total_pairs * domain * domain))
    return (final, occ_density)


def solution(mesh):
    pair_spec = P(("groups", "row", "col"), None, None)
    flat = P(("groups", "row", "col"))
    table = P(("groups", "row", "col"), None)
    return jax.shard_map(
        per_device,
        mesh=mesh,
        in_specs=(
            pair_spec, pair_spec, pair_spec, pair_spec,
            P("groups"), flat, flat, table, flat, table, table, table, table,
        ),
        out_specs=(pair_spec, P("groups")),
        check_vma=False,
    )
```

```python
import jax
import jax.numpy as jnp
from jax import lax
from jax.experimental import pallas as pl
from jax.experimental.pallas import tpu as pltpu
from jax.sharding import PartitionSpec as P


ITERS = 2
ANY = pl.ANY
SMEM = pltpu.SMEM
VMEM = pltpu.VMEM
LANES = 16
MIB = 1 << 20


def ring(rows, row):
    return row if rows & (rows - 1) else row ^ (row >> 1)


def sent(rows, step):
    hop = (step + 1) // 2 if step % 2 else rows - step // 2
    where = {ring(rows, r): r for r in range(rows)}
    return [(r, where[(ring(rows, r) + hop) % rows]) for r in range(rows)]


def asked_of(rows, step):
    return [(b, a) for a, b in sent(rows, step)]


def step_of(rows, source, row):
    hop = ring(rows, row) - ring(rows, source)
    hop = jnp.where(hop < 0, hop + rows, hop)
    step = jnp.where(2 * hop <= rows, 2 * hop - 1, 2 * (rows - hop))
    return jnp.where(hop == 0, 0, step)


def limits(mib):
    return pltpu.CompilerParams(vmem_limit_bytes=mib * MIB)


def cost(flops, size):
    return pl.CostEstimate(flops=flops, transcendentals=0, bytes_accessed=size)


def fetch(candidates, spot, target):
    for offset, ref in candidates:

        @pl.when((spot >= offset) & (spot < offset + ref.shape[0]))
        def _(offset=offset, ref=ref):
            target[...] = ref[spot - offset]


def laid(refs, offset=0):
    placed = []
    for ref in refs:
        placed.append((offset, ref))
        offset += ref.shape[0]
    return placed


def gather_first(requests, parts, place, amplitudes, rows, cap):
    pairs, domain = amplitudes.shape[:2]
    steps = sorted({step for step, _, _ in parts})
    count_of = len(steps)
    blocks = sum(size for _, _, size in parts)
    bits = pairs.bit_length() - 1

    def body(place_ref, *refs):
        lists = refs[:count_of]
        store = refs[count_of]
        asked = refs[count_of + 1]
        outs = refs[count_of + 2 : -1]
        sem = refs[-1]
        me = place_ref[0]
        core = place_ref[1]
        for n, step in enumerate(steps):
            base = n * (cap + 1)
            asker = jnp.int32(0)
            for a, b in sent(rows, step):
                asker = jnp.where(me == a, b, asker)
            served = [asker]
            for sooner in range(1, step):
                server = jnp.int32(0)
                for a, b in sent(rows, sooner):
                    server = jnp.where(asker == b, a, server)
                served.append(server)
            for k in range(cap):
                asked[base + k] = 0
            entries = [lists[n][p] for p in range(pairs)]
            sources = [entry // pairs if pairs & (pairs - 1) else entry >> bits for entry in entries]
            count = jnp.int32(0)
            for p in range(pairs):
                for server in served:
                    count = count + (sources[p] == server).astype(jnp.int32)
            filled = jnp.int32(0)
            for p in range(pairs):
                mine = (sources[p] == me).astype(jnp.int32)
                asked[base + jnp.minimum(filled, cap)] = entries[p] - sources[p] * pairs
                filled = filled + jnp.where((count & 1) == core, mine, 0)
                count = count + mine
            for m, (of, begin, size) in enumerate(parts):
                for k in range(size if of == step else 0):
                    pltpu.make_async_copy(
                        store.at[asked[base + begin + k]], outs[m].at[k], sem.at[m, k]
                    ).start()
        for m, (_, _, size) in enumerate(parts):
            for k in range(size):
                pltpu.make_async_copy(store.at[0], outs[m].at[k], sem.at[m, k]).wait()

    return pl.pallas_call(
        body,
        out_shape=[jax.ShapeDtypeStruct((count_of * (cap + 1),), jnp.int32)]
        + [VMEM((size, domain, domain), jnp.bfloat16) for _, _, size in parts],
        in_specs=[pl.BlockSpec(memory_space=SMEM)] * (count_of + 1)
        + [pl.BlockSpec(memory_space=pltpu.HBM)],
        out_specs=[pl.BlockSpec(memory_space=SMEM)]
        + [pl.BlockSpec(memory_space=VMEM)] * len(parts),
        scratch_shapes=[pltpu.SemaphoreType.DMA((len(parts), cap))],
        cost_estimate=cost(0, blocks * domain * domain * 4),
        compiler_params=limits(8),
        name="gather_first",
    )(place, *requests, pltpu.with_memory_space_constraint(amplitudes, pltpu.HBM))


def gather_again(asked, where, stores, parts, cap):
    domain = stores[0].shape[1]
    steps = sorted({step for step, _, _ in parts})
    blocks = sum(size for _, _, size in parts)

    def body(asked_ref, where_ref, *refs):
        sources = laid(refs[: len(stores)])
        outs = refs[len(stores) :]
        for m, (step, begin, size) in enumerate(parts):
            for k in range(size):
                spot = where_ref[asked_ref[steps.index(step) * (cap + 1) + begin + k]]
                fetch(sources, spot, outs[m].at[k])

    return pl.pallas_call(
        body,
        out_shape=[VMEM((size, domain, domain), jnp.bfloat16) for _, _, size in parts],
        in_specs=[pl.BlockSpec(memory_space=SMEM)] * 2
        + [pl.BlockSpec(memory_space=VMEM)] * len(stores),
        out_specs=[pl.BlockSpec(memory_space=VMEM)] * len(parts),
        cost_estimate=cost(0, blocks * domain * domain * 4),
        compiler_params=limits(8),
        name="gather_again",
    )(asked, where, *stores)


def prepare(own, at, columns, counts, shift, near, stores, integrals, fock_matrix, intersection):
    half = own.shape[0]
    domain = integrals.shape[1]
    total = columns.shape[0]
    entries = near[0].shape[1]
    groups = domain // LANES // half
    strip = groups * LANES

    def spread_weights(own_ref, column_ref, slot_ref, count_ref, weight_ref, spread_ref):
        lane = lax.broadcasted_iota(jnp.int32, (total, total), 1)
        down = lax.broadcasted_iota(jnp.int32, (total, total), 0)
        used_count = jnp.zeros((total, total), jnp.int32)
        for n in range(total):
            used_count = jnp.where(down == n, count_ref[n], used_count)
        weights = jnp.zeros((total, total), jnp.float32)
        for k in range(entries):
            used = (slot_ref[:, k : k + 1] == lane) & (k < used_count)
            wide = weight_ref[:, k : k + 1].astype(jnp.float32)
            weights = weights + jnp.where(used, wide, jnp.float32(0.0))
        weights = weights.astype(jnp.bfloat16)
        shape = (half * LANES, total)
        row = lax.broadcasted_iota(jnp.int32, shape, 0) // LANES
        wanted = jnp.zeros(shape, jnp.int32)
        for n in range(half):
            wanted = jnp.where(row == n, own_ref[n], wanted)
        pick = lax.broadcasted_iota(jnp.int32, shape, 1) == wanted
        mine = jnp.dot(
            pick.astype(jnp.float32).astype(jnp.bfloat16),
            weights,
            preferred_element_type=jnp.float32,
        ).astype(jnp.bfloat16)
        shape = (total, total * LANES)
        column = lax.broadcasted_iota(jnp.int32, shape, 1) // LANES
        wanted = jnp.zeros(shape, jnp.int32)
        for n in range(total):
            wanted = jnp.where(column == n, column_ref[n], wanted)
        pick = lax.broadcasted_iota(jnp.int32, shape, 0) == wanted
        full = jnp.dot(
            mine,
            pick.astype(jnp.float32).astype(jnp.bfloat16),
            preferred_element_type=jnp.float32,
        )
        shape = (half * LANES, total * LANES)
        down = lax.broadcasted_iota(jnp.int32, shape, 0) % LANES
        along = lax.broadcasted_iota(jnp.int32, shape, 1) % LANES
        spread_ref[...] = jnp.where(down == along, full, 0.0).astype(jnp.bfloat16)

    def body(
        own_ref, at_ref, column_ref, count_ref, shift_ref, slot_ref, weight_ref, *refs
    ):
        sources = refs[: len(stores)]
        (integ_ref, fock_ref, over_ref, local_ref, rest_ref, recip_ref, keep_ref, spread_ref) = (
            refs[len(stores) :]
        )
        i = pl.program_id(0)

        @pl.when(i == 0)
        def _():
            spread_weights(own_ref, column_ref, slot_ref, count_ref, weight_ref, spread_ref)

        for g in range(groups):
            rows = pl.ds(pl.multiple_of(i * strip + g * LANES, LANES), LANES)
            part = [s[:, rows, :].reshape(s.shape[0] * LANES, domain) for s in sources]
            part = part[0] if len(part) == 1 else jnp.concatenate(part, axis=0)
            sums = jnp.dot(spread_ref[...], part, preferred_element_type=jnp.float32)
            local_ref[:, g * LANES : (g + 1) * LANES, :] = sums.reshape(half, LANES, domain)
        amps = sources[0][at_ref[i]]
        fock = fock_ref[0]
        wide = amps.astype(jnp.float32)
        left = jnp.dot(fock, amps, preferred_element_type=jnp.float32)
        right = jnp.dot(amps, fock, preferred_element_type=jnp.float32)
        row_id = lax.broadcasted_iota(jnp.int32, (domain, domain), 0)
        col_id = lax.broadcasted_iota(jnp.int32, (domain, domain), 1)
        diagonal = jnp.where(row_id == col_id, fock.astype(jnp.float32), 0.0)
        across = jnp.sum(diagonal, axis=0, keepdims=True)
        down = jnp.sum(diagonal, axis=1, keepdims=True)
        residual = integ_ref[0].astype(jnp.float32) + left + right - shift_ref[i] * wide
        recip = 1.0 / (down + across - shift_ref[i])
        recip_ref[0] = recip
        rest_ref[0] = wide - residual * recip
        keep_ref[0] = over_ref[0]

    block = (1, domain, domain)
    mine = pl.BlockSpec(block, lambda i, own, *_: (own[i], 0, 0))
    in_turn = pl.BlockSpec(block, lambda i, *_: (i, 0, 0))
    wide_shape = jax.ShapeDtypeStruct((half, domain, domain), jnp.float32)
    return pl.pallas_call(
        body,
        grid_spec=pltpu.PrefetchScalarGridSpec(
            num_scalar_prefetch=5,
            grid=(half,),
            in_specs=[pl.BlockSpec(n.shape, lambda i, *_: (0, 0)) for n in near]
            + [pl.BlockSpec(s.shape, lambda i, *_: (0, 0, 0)) for s in stores]
            + [mine, mine, mine],
            out_specs=[
                pl.BlockSpec((half, strip, domain), lambda i, *_: (0, i, 0)),
                in_turn,
                in_turn,
                in_turn,
            ],
            scratch_shapes=[VMEM((half * LANES, total * LANES), jnp.bfloat16)],
        ),
        out_shape=[
            wide_shape,
            wide_shape,
            wide_shape,
            jax.ShapeDtypeStruct((half, domain, domain), jnp.bfloat16),
        ],
        cost_estimate=cost(
            2 * half * domain**3 * 3,
            (total + 4 * half) * domain * domain * 2 + half * domain * domain * 12,
        ),
        compiler_params=limits(20),
        name="prepare",
    )(own, at, columns, counts, shift, *near, *stores, integrals, fock_matrix, intersection)


def finish(start, count, numbers, scale, prepared, arrived, stores, occ_count, last):
    half, domain = prepared[0].shape[:2]

    def body(number_ref, scale_ref, local_ref, rest_ref, recip_ref, over_ref, *refs):
        candidates = [
            (offset, ref) for offset, ref in zip([o for o, _ in arrived + stores], refs)
        ]
        outs = refs[len(candidates) : -1]
        hold = refs[-1]
        for n in range(count):
            fetch(candidates, number_ref[start + n], hold.at[n])
        if last:
            row_id = lax.broadcasted_iota(jnp.int32, (domain, domain), 0)
            col_id = lax.broadcasted_iota(jnp.int32, (domain, domain), 1)
            on_diagonal = row_id == col_id
            orbital = lax.broadcasted_iota(jnp.int32, (1, occ_count), 1)
            density = jnp.zeros((1, occ_count), jnp.float32)
        for n in range(count):
            i = start + n
            coupled = local_ref[i] + scale_ref[i] * hold[n].astype(jnp.float32)
            over = over_ref[i]
            projected = jnp.dot(
                over, coupled.astype(jnp.bfloat16), preferred_element_type=jnp.float32
            )
            back = lax.dot_general(
                projected.astype(jnp.bfloat16),
                over,
                (((1,), (1,)), ((), ())),
                preferred_element_type=jnp.float32,
            )
            fresh = (rest_ref[i] + back * recip_ref[i]).astype(jnp.bfloat16)
            outs[0][n] = fresh
            if last:
                wide = fresh.astype(jnp.float32)
                square = jnp.dot(fresh, fresh, preferred_element_type=jnp.float32)
                terms = 2.0 * wide * wide - jnp.where(on_diagonal, square, 0.0)
                norm = jnp.sum(jnp.sum(terms, axis=0, keepdims=True), axis=1, keepdims=True)
                picks = (orbital == number_ref[half + i]).astype(jnp.float32)
                picks = picks + (orbital == number_ref[2 * half + i]).astype(jnp.float32)
                density = density + norm * picks
        if last:
            outs[1][...] = density

    out_shape = [VMEM((count, domain, domain), jnp.bfloat16)]
    if last:
        out_shape.append(VMEM((1, occ_count), jnp.float32))
    return pl.pallas_call(
        body,
        out_shape=out_shape,
        in_specs=[pl.BlockSpec(memory_space=SMEM)] * 2
        + [pl.BlockSpec(memory_space=VMEM)] * 4
        + [pl.BlockSpec(memory_space=VMEM)] * len(arrived + stores),
        out_specs=[pl.BlockSpec(memory_space=VMEM)] * len(out_shape),
        scratch_shapes=[VMEM((count, domain, domain), jnp.bfloat16)],
        cost_estimate=cost(2 * count * domain**3 * 2, count * domain * domain * 18),
        compiler_params=limits(16),
        name="finish",
    )(numbers, scale, *prepared, *[a for _, a in arrived + stores])


def put_in_slots(slots, stores):
    domain = stores[0].shape[1]
    total = slots.shape[0]

    def body(slot_ref, *refs):
        sources = refs[: len(stores)]
        out_ref, sem = refs[-2:]
        copies = []
        for source in sources:
            for n in range(source.shape[0]):
                at = len(copies)
                copies.append(
                    pltpu.make_async_copy(source.at[n], out_ref.at[slot_ref[at]], sem.at[at])
                )
        for copy in copies:
            copy.start()
        for copy in copies:
            copy.wait()

    return pl.pallas_call(
        body,
        out_shape=jax.ShapeDtypeStruct((total, domain, domain), jnp.bfloat16),
        in_specs=[pl.BlockSpec(memory_space=SMEM)]
        + [pl.BlockSpec(memory_space=VMEM)] * len(stores),
        out_specs=pl.BlockSpec(memory_space=ANY),
        scratch_shapes=[pltpu.SemaphoreType.DMA((total,))],
        cost_estimate=cost(0, total * domain * domain * 4),
        compiler_params=limits(8),
        name="put_in_slots",
    )(slots, *stores)


def add_over(values, name):
    size = lax.axis_size(name)
    if size & (size - 1):
        return lax.psum(values, name)
    step = 1
    while step < size:
        values = values + lax.ppermute(values, name, [(r, r ^ step) for r in range(size)])
        step *= 2
    return values


def per_device(
    amplitudes,
    integrals,
    fock_matrix,
    intersection,
    occ_energy,
    first_occ,
    second_occ,
    near_slot,
    near_count,
    near_weight,
    far_chip,
    far_slot,
    far_weight,
):
    pairs, domain = amplitudes.shape[:2]
    rows = lax.axis_size("row")
    half = pairs // 2
    cap = pairs // rows
    row = lax.axis_index("row")
    core = lax.axis_index("rep")
    occ_count = occ_energy.shape[0]
    slot_ids = jnp.arange(pairs, dtype=jnp.int32)
    source = far_chip[:, 0]
    packed = source * pairs + far_slot[:, 0]
    here = jnp.stack([row, core]).astype(jnp.int32)
    tail = max(1, cap // 2)
    lead = [(1, 0, cap)]
    rest = [(step, 0, cap) for step in range(2, rows - 1)]
    rest += [(rows - 1, 0, cap - tail)] * (cap > tail) + [(rows - 1, cap - tail, tail)]
    request = lax.ppermute(packed, "row", asked_of(rows, 1))
    requests = [
        lax.ppermute(packed, "row", asked_of(rows, d)) for d in range(2, rows)
    ]
    asked_lead, send_lead = gather_first([request], lead, here, amplitudes, rows, cap)

    step = step_of(rows, source, row)
    same = step[:, None] == step[None, :]
    before = (step[None, :] < step[:, None]) | (same & (slot_ids[None, :] < slot_ids[:, None]))
    turn = jnp.sum(before.astype(jnp.int32), axis=1)
    like = same & (turn[:, None] % 2 == turn[None, :] % 2) & (turn[None, :] < turn[:, None])
    place = jnp.sum(like.astype(jnp.int32), axis=1)
    mine = jnp.arange(half, dtype=jnp.int32) * 2 + core
    own_pick = mine[:, None] == turn[None, :]
    other_pick = (mine ^ 1)[:, None] == turn[None, :]

    def pick(chosen, values):
        return jnp.sum(jnp.where(chosen, values[None, :], jnp.zeros((), values.dtype)), axis=1)

    own = pick(own_pick, slot_ids)
    other = pick(other_pick, slot_ids)
    far_step = pick(own_pick, step)
    own_far = pick(own_pick, far_slot[:, 0])
    own_place = pick(own_pick, place)

    occ_energy, first_occ, second_occ, far_weight, _ = lax.optimization_barrier(
        (occ_energy, first_occ, second_occ, far_weight, asked_lead)
    )
    orbitals = jnp.arange(occ_count, dtype=jnp.int32)

    def energy_of(index):
        found = index[:, None] == orbitals[None, :]
        return jnp.sum(jnp.where(found, occ_energy[None, :], jnp.float32(0.0)), axis=1)

    far_scale = pick(own_pick, far_weight[:, 0].astype(jnp.float32))
    first = pick(own_pick, first_occ)
    second = pick(own_pick, second_occ)
    shift = energy_of(first) + energy_of(second)

    by_slot = turn // 2 + jnp.where(turn % 2 == core, 0, half)
    early = half - tail
    swap = [(0, 1), (1, 0)]
    remote = (rows - 1) * cap
    local_spots = [
        slot_ids,
        jnp.where(
            by_slot < half,
            by_slot + jnp.where(by_slot % half < early, 0, early),
            by_slot - half + jnp.where(by_slot % half < early, early, half),
        ),
    ]
    tables = []
    for where in (slot_ids, by_slot):
        at_home = remote + jnp.sum(
            jnp.where(own_far[:, None] == slot_ids[None, :], where[None, :], 0), axis=1
        )
        spot = jnp.where(far_step == 0, at_home, (far_step - 1) * cap + own_place)
        tables.append(jnp.concatenate([spot, first, second]))
    near = [near_slot, near_weight]
    columns = [slot_ids, jnp.concatenate([own, other])]
    ats = [own, jnp.arange(half, dtype=jnp.int32)]
    slots = jnp.concatenate([own[:early], other[:early], own[early:], other[early:]])
    stores = [amplitudes]
    whole = [amplitudes]
    for sweep in range(ITERS):
        last = sweep == ITERS - 1
        again = min(sweep, 1)
        if sweep > 0:
            (send_lead,) = gather_again(asked_lead, local_spots[1], stores, lead, cap)
        arrived = [lax.ppermute(send_lead, "row", sent(rows, 1))]
        if sweep == 0:
            (*requests, _) = lax.optimization_barrier((*requests, send_lead))
            asked, *sends = gather_first(requests, rest, here, amplitudes, rows, cap)
        else:
            sends = gather_again(asked, local_spots[1], stores, rest, cap)
        for part, send in zip(rest, sends):
            arrived.append(lax.ppermute(send, "row", sent(rows, part[0])))
        prepared = prepare(
            own, ats[again], columns[again], near_count, shift, near, whole,
            integrals, fock_matrix, intersection,
        )
        spots = laid(arrived)
        homes = laid(whole, remote)
        done_early = finish(
            0, early, tables[again], far_scale, prepared, spots[:-1], homes, occ_count,
            last,
        )
        given_early = lax.ppermute(done_early[0], "rep", swap)
        done_late = finish(
            early, tail, tables[again], far_scale, prepared, spots, homes, occ_count, last
        )
        given_late = lax.ppermute(done_late[0], "rep", swap)
        stores = [done_early[0], given_early, done_late[0], given_late]
        whole = [
            jnp.concatenate([done_early[0], done_late[0]], axis=0),
            jnp.concatenate([given_early, given_late], axis=0),
        ]
    final = put_in_slots(slots, stores)
    occ_sum = (done_early[1] + done_late[1])[0]
    occ_sum = add_over(occ_sum, "rep")
    occ_sum = add_over(occ_sum, "col")
    occ_sum = add_over(occ_sum, "row")
    total_pairs = pairs * rows * lax.axis_size("col")
    occ_density = occ_sum * (occ_count / (2.0 * total_pairs * domain * domain))
    return (final, occ_density)


def solution(mesh):
    pair_spec = P(("groups", "row", "col"), None, None)
    flat = P(("groups", "row", "col"))
    table = P(("groups", "row", "col"), None)
    return jax.shard_map(
        per_device,
        mesh=mesh,
        in_specs=(
            pair_spec, pair_spec, pair_spec, pair_spec,
            P("groups"), flat, flat, table, flat, table, table, table, table,
        ),
        out_specs=(pair_spec, P("groups")),
        check_vma=False,
    )
```

```python
import jax
import jax.numpy as jnp
from jax import lax
from jax.experimental import pallas as pl
from jax.experimental.pallas import tpu as pltpu
from jax.sharding import PartitionSpec as P


ITERS = 2
ANY = pl.ANY
SMEM = pltpu.SMEM
VMEM = pltpu.VMEM
LANES = 16
MIB = 1 << 20


def ring(rows, row):
    return row if rows & (rows - 1) else row ^ (row >> 1)


def sent(rows, step):
    hop = (step + 1) // 2 if step % 2 else rows - step // 2
    where = {ring(rows, r): r for r in range(rows)}
    return [(r, where[(ring(rows, r) + hop) % rows]) for r in range(rows)]


def asked_of(rows, step):
    return [(b, a) for a, b in sent(rows, step)]


def step_of(rows, source, row):
    hop = ring(rows, row) - ring(rows, source)
    hop = jnp.where(hop < 0, hop + rows, hop)
    step = jnp.where(2 * hop <= rows, 2 * hop - 1, 2 * (rows - hop))
    return jnp.where(hop == 0, 0, step)


def in_hbm(array):
    return pltpu.with_memory_space_constraint(array, pltpu.HBM)


def limits(mib):
    return pltpu.CompilerParams(vmem_limit_bytes=mib * MIB)


def cost(flops, size):
    return pl.CostEstimate(flops=flops, transcendentals=0, bytes_accessed=size)


def fetch(candidates, spot, target):
    for offset, ref in candidates:

        @pl.when((spot >= offset) & (spot < offset + ref.shape[0]))
        def _(offset=offset, ref=ref):
            target[...] = ref[spot - offset]


def laid(refs, offset=0):
    placed = []
    for ref in refs:
        placed.append((offset, ref))
        offset += ref.shape[0]
    return placed


def gather_first(requests, parts, place, amplitudes, rows, cap):
    pairs, domain = amplitudes.shape[:2]
    steps = sorted({step for step, _, _ in parts})
    count_of = len(steps)
    blocks = sum(size for _, _, size in parts)
    bits = pairs.bit_length() - 1

    def body(place_ref, *refs):
        lists = refs[:count_of]
        store = refs[count_of]
        asked = refs[count_of + 1]
        outs = refs[count_of + 2 : -1]
        sem = refs[-1]
        me = place_ref[0]
        core = place_ref[1]
        for n, step in enumerate(steps):
            base = n * (cap + 1)
            asker = jnp.int32(0)
            for a, b in sent(rows, step):
                asker = jnp.where(me == a, b, asker)
            served = [asker]
            for sooner in range(1, step):
                server = jnp.int32(0)
                for a, b in sent(rows, sooner):
                    server = jnp.where(asker == b, a, server)
                served.append(server)
            for k in range(cap):
                asked[base + k] = 0
            entries = [lists[n][p] for p in range(pairs)]
            sources = [entry // pairs if pairs & (pairs - 1) else entry >> bits for entry in entries]
            count = jnp.int32(0)
            for p in range(pairs):
                for server in served:
                    count = count + (sources[p] == server).astype(jnp.int32)
            filled = jnp.int32(0)
            for p in range(pairs):
                mine = (sources[p] == me).astype(jnp.int32)
                asked[base + jnp.minimum(filled, cap)] = entries[p] - sources[p] * pairs
                filled = filled + jnp.where((count & 1) == core, mine, 0)
                count = count + mine
            for m, (of, begin, size) in enumerate(parts):
                for k in range(size if of == step else 0):
                    pltpu.make_async_copy(
                        store.at[asked[base + begin + k]], outs[m].at[k], sem.at[m, k]
                    ).start()
        for m, (_, _, size) in enumerate(parts):
            for k in range(size):
                pltpu.make_async_copy(store.at[0], outs[m].at[k], sem.at[m, k]).wait()

    return pl.pallas_call(
        body,
        out_shape=[jax.ShapeDtypeStruct((count_of * (cap + 1),), jnp.int32)]
        + [VMEM((size, domain, domain), jnp.bfloat16) for _, _, size in parts],
        in_specs=[pl.BlockSpec(memory_space=SMEM)] * (count_of + 1)
        + [pl.BlockSpec(memory_space=pltpu.HBM)],
        out_specs=[pl.BlockSpec(memory_space=SMEM)]
        + [pl.BlockSpec(memory_space=VMEM)] * len(parts),
        scratch_shapes=[pltpu.SemaphoreType.DMA((len(parts), cap))],
        cost_estimate=cost(0, blocks * domain * domain * 4),
        compiler_params=limits(8),
        name="gather_first",
    )(place, *requests, in_hbm(amplitudes))


def gather_again(asked, where, stores, parts, cap):
    domain = stores[0].shape[1]
    steps = sorted({step for step, _, _ in parts})
    blocks = sum(size for _, _, size in parts)

    def body(asked_ref, where_ref, *refs):
        sources = laid(refs[: len(stores)])
        outs = refs[len(stores) :]
        for m, (step, begin, size) in enumerate(parts):
            for k in range(size):
                spot = where_ref[asked_ref[steps.index(step) * (cap + 1) + begin + k]]
                fetch(sources, spot, outs[m].at[k])

    return pl.pallas_call(
        body,
        out_shape=[VMEM((size, domain, domain), jnp.bfloat16) for _, _, size in parts],
        in_specs=[pl.BlockSpec(memory_space=SMEM)] * 2
        + [pl.BlockSpec(memory_space=VMEM)] * len(stores),
        out_specs=[pl.BlockSpec(memory_space=VMEM)] * len(parts),
        cost_estimate=cost(0, blocks * domain * domain * 4),
        compiler_params=limits(8),
        name="gather_again",
    )(asked, where, *stores)


def prepare(
    own, at, home, columns, counts, shift, near, stores, integrals, fock_matrix, intersection
):
    half = own.shape[0]
    domain = integrals.shape[1]
    total = columns.shape[0]
    entries = near[0].shape[1]
    groups = domain // LANES // half
    strip = groups * LANES

    def spread_weights(own_ref, column_ref, slot_ref, count_ref, weight_ref, spread_ref):
        lane = lax.broadcasted_iota(jnp.int32, (total, total), 1)
        down = lax.broadcasted_iota(jnp.int32, (total, total), 0)
        used_count = jnp.zeros((total, total), jnp.int32)
        for n in range(total):
            used_count = jnp.where(down == n, count_ref[n], used_count)
        weights = jnp.zeros((total, total), jnp.float32)
        for k in range(entries):
            used = (slot_ref[:, k : k + 1] == lane) & (k < used_count)
            wide = weight_ref[:, k : k + 1].astype(jnp.float32)
            weights = weights + jnp.where(used, wide, jnp.float32(0.0))
        weights = weights.astype(jnp.bfloat16)
        shape = (half * LANES, total)
        row = lax.broadcasted_iota(jnp.int32, shape, 0) // LANES
        wanted = jnp.zeros(shape, jnp.int32)
        for n in range(half):
            wanted = jnp.where(row == n, own_ref[n], wanted)
        pick = lax.broadcasted_iota(jnp.int32, shape, 1) == wanted
        mine = jnp.dot(
            pick.astype(jnp.float32).astype(jnp.bfloat16),
            weights,
            preferred_element_type=jnp.float32,
        ).astype(jnp.bfloat16)
        shape = (total, total * LANES)
        column = lax.broadcasted_iota(jnp.int32, shape, 1) // LANES
        wanted = jnp.zeros(shape, jnp.int32)
        for n in range(total):
            wanted = jnp.where(column == n, column_ref[n], wanted)
        pick = lax.broadcasted_iota(jnp.int32, shape, 0) == wanted
        full = jnp.dot(
            mine,
            pick.astype(jnp.float32).astype(jnp.bfloat16),
            preferred_element_type=jnp.float32,
        )
        shape = (half * LANES, total * LANES)
        down = lax.broadcasted_iota(jnp.int32, shape, 0) % LANES
        along = lax.broadcasted_iota(jnp.int32, shape, 1) % LANES
        spread_ref[...] = jnp.where(down == along, full, 0.0).astype(jnp.bfloat16)

    def body(
        own_ref, at_ref, home_ref, column_ref, count_ref, shift_ref, slot_ref, weight_ref, *refs
    ):
        sources = refs[: len(stores)]
        (
            integ_ref, fock_ref, over_ref,
            local_ref, rest_ref, recip_ref, keep_ref, near_by_ref, spread_ref,
        ) = refs[len(stores) :]
        i = pl.program_id(0)

        @pl.when(i == 0)
        def _():
            spread_weights(own_ref, column_ref, slot_ref, count_ref, weight_ref, spread_ref)

        for g in range(groups):
            rows = pl.ds(pl.multiple_of(i * strip + g * LANES, LANES), LANES)
            part = [s[:, rows, :].reshape(s.shape[0] * LANES, domain) for s in sources]
            part = part[0] if len(part) == 1 else jnp.concatenate(part, axis=0)
            sums = jnp.dot(spread_ref[...], part, preferred_element_type=jnp.float32)
            local_ref[:, g * LANES : (g + 1) * LANES, :] = sums.reshape(half, LANES, domain)
        amps = sources[0][at_ref[i]]
        fock = fock_ref[0]
        wide = amps.astype(jnp.float32)
        left = jnp.dot(fock, amps, preferred_element_type=jnp.float32)
        right = jnp.dot(amps, fock, preferred_element_type=jnp.float32)
        row_id = lax.broadcasted_iota(jnp.int32, (domain, domain), 0)
        col_id = lax.broadcasted_iota(jnp.int32, (domain, domain), 1)
        diagonal = jnp.where(row_id == col_id, fock.astype(jnp.float32), 0.0)
        across = jnp.sum(diagonal, axis=0, keepdims=True)
        down = jnp.sum(diagonal, axis=1, keepdims=True)
        residual = integ_ref[0].astype(jnp.float32) + left + right - shift_ref[i] * wide
        recip = 1.0 / (down + across - shift_ref[i])
        recip_ref[0] = recip
        rest_ref[0] = wide - residual * recip
        keep_ref[0] = over_ref[0]
        fetch(laid(sources), home_ref[i], near_by_ref.at[0])

    block = (1, domain, domain)
    mine = pl.BlockSpec(block, lambda i, own, *_: (own[i], 0, 0))
    in_turn = pl.BlockSpec(block, lambda i, *_: (i, 0, 0))
    wide_shape = jax.ShapeDtypeStruct((half, domain, domain), jnp.float32)
    return pl.pallas_call(
        body,
        grid_spec=pltpu.PrefetchScalarGridSpec(
            num_scalar_prefetch=6,
            grid=(half,),
            in_specs=[pl.BlockSpec(n.shape, lambda i, *_: (0, 0)) for n in near]
            + [pl.BlockSpec(s.shape, lambda i, *_: (0, 0, 0)) for s in stores]
            + [mine, mine, mine],
            out_specs=[
                pl.BlockSpec((half, strip, domain), lambda i, *_: (0, i, 0)),
                in_turn,
                in_turn,
                in_turn,
                in_turn,
            ],
            scratch_shapes=[VMEM((half * LANES, total * LANES), jnp.bfloat16)],
        ),
        out_shape=[
            wide_shape,
            wide_shape,
            wide_shape,
            jax.ShapeDtypeStruct((half, domain, domain), jnp.bfloat16),
            jax.ShapeDtypeStruct((half, domain, domain), jnp.bfloat16),
        ],
        cost_estimate=cost(
            2 * half * domain**3 * 3,
            (total + 4 * half) * domain * domain * 2 + half * domain * domain * 12,
        ),
        compiler_params=limits(20),
        name="prepare",
    )(
        own, at, home, columns, counts, shift, *near,
        *[in_hbm(s) if s.shape[0] > half else s for s in stores],
        in_hbm(integrals), in_hbm(fock_matrix), in_hbm(intersection),
    )


def finish(start, count, numbers, scale, prepared, arrived, occ_count, last):
    half, domain = prepared[0].shape[:2]

    def body(number_ref, scale_ref, local_ref, rest_ref, recip_ref, over_ref, *refs):
        candidates = [
            (offset, ref) for offset, ref in zip([o for o, _ in arrived], refs)
        ]
        outs = refs[len(candidates) : -1]
        hold = refs[-1]
        for n in range(count):
            fetch(candidates, number_ref[start + n], hold.at[n])
        if last:
            row_id = lax.broadcasted_iota(jnp.int32, (domain, domain), 0)
            col_id = lax.broadcasted_iota(jnp.int32, (domain, domain), 1)
            on_diagonal = row_id == col_id
            orbital = lax.broadcasted_iota(jnp.int32, (1, occ_count), 1)
            density = jnp.zeros((1, occ_count), jnp.float32)
        for n in range(count):
            i = start + n
            coupled = local_ref[i] + scale_ref[i] * hold[n].astype(jnp.float32)
            over = over_ref[i]
            projected = jnp.dot(
                over, coupled.astype(jnp.bfloat16), preferred_element_type=jnp.float32
            )
            back = lax.dot_general(
                projected.astype(jnp.bfloat16),
                over,
                (((1,), (1,)), ((), ())),
                preferred_element_type=jnp.float32,
            )
            fresh = (rest_ref[i] + back * recip_ref[i]).astype(jnp.bfloat16)
            outs[0][n] = fresh
            if last:
                wide = fresh.astype(jnp.float32)
                square = jnp.dot(fresh, fresh, preferred_element_type=jnp.float32)
                terms = 2.0 * wide * wide - jnp.where(on_diagonal, square, 0.0)
                norm = jnp.sum(jnp.sum(terms, axis=0, keepdims=True), axis=1, keepdims=True)
                picks = (orbital == number_ref[half + i]).astype(jnp.float32)
                picks = picks + (orbital == number_ref[2 * half + i]).astype(jnp.float32)
                density = density + norm * picks
        if last:
            outs[1][...] = density

    out_shape = [VMEM((count, domain, domain), jnp.bfloat16)]
    if last:
        out_shape.append(VMEM((1, occ_count), jnp.float32))
    return pl.pallas_call(
        body,
        out_shape=out_shape,
        in_specs=[pl.BlockSpec(memory_space=SMEM)] * 2
        + [pl.BlockSpec(memory_space=VMEM)] * 4
        + [pl.BlockSpec(memory_space=VMEM)] * len(arrived),
        out_specs=[pl.BlockSpec(memory_space=VMEM)] * len(out_shape),
        scratch_shapes=[VMEM((count, domain, domain), jnp.bfloat16)],
        cost_estimate=cost(2 * count * domain**3 * 2, count * domain * domain * 18),
        compiler_params=limits(16),
        name="finish",
    )(numbers, scale, *prepared, *[a for _, a in arrived])


def put_in_slots(slots, stores):
    domain = stores[0].shape[1]
    total = slots.shape[0]

    def body(slot_ref, *refs):
        sources = refs[: len(stores)]
        out_ref, sem = refs[-2:]
        copies = []
        for source in sources:
            for n in range(source.shape[0]):
                at = len(copies)
                copies.append(
                    pltpu.make_async_copy(source.at[n], out_ref.at[slot_ref[at]], sem.at[at])
                )
        for copy in copies:
            copy.start()
        for copy in copies:
            copy.wait()

    return pl.pallas_call(
        body,
        out_shape=jax.ShapeDtypeStruct((total, domain, domain), jnp.bfloat16),
        in_specs=[pl.BlockSpec(memory_space=SMEM)]
        + [pl.BlockSpec(memory_space=VMEM)] * len(stores),
        out_specs=pl.BlockSpec(memory_space=ANY),
        scratch_shapes=[pltpu.SemaphoreType.DMA((total,))],
        cost_estimate=cost(0, total * domain * domain * 4),
        compiler_params=limits(8),
        name="put_in_slots",
    )(slots, *stores)


def add_over(values, name):
    size = lax.axis_size(name)
    if size & (size - 1):
        return lax.psum(values, name)
    step = 1
    while step < size:
        values = values + lax.ppermute(values, name, [(r, r ^ step) for r in range(size)])
        step *= 2
    return values


def per_device(
    amplitudes,
    integrals,
    fock_matrix,
    intersection,
    occ_energy,
    first_occ,
    second_occ,
    near_slot,
    near_count,
    near_weight,
    far_chip,
    far_slot,
    far_weight,
):
    pairs, domain = amplitudes.shape[:2]
    rows = lax.axis_size("row")
    half = pairs // 2
    cap = pairs // rows
    row = lax.axis_index("row")
    core = lax.axis_index("rep")
    occ_count = occ_energy.shape[0]
    slot_ids = jnp.arange(pairs, dtype=jnp.int32)
    source = far_chip[:, 0]
    packed = source * pairs + far_slot[:, 0]
    here = jnp.stack([row, core]).astype(jnp.int32)
    tail = max(1, cap // 2)
    lead = [(1, 0, cap)]
    rest = [(step, 0, cap) for step in range(2, rows - 1)]
    rest += [(rows - 1, 0, cap - tail)] * (cap > tail) + [(rows - 1, cap - tail, tail)]
    request = lax.ppermute(packed, "row", asked_of(rows, 1))
    requests = [
        lax.ppermute(packed, "row", asked_of(rows, d)) for d in range(2, rows)
    ]
    asked_lead, send_lead = gather_first([request], lead, here, amplitudes, rows, cap)

    (
        source, far_slot, occ_energy, first_occ, second_occ, far_weight,
        _,
    ) = lax.optimization_barrier(
        (
            source, far_slot, occ_energy, first_occ, second_occ, far_weight,
            asked_lead,
        )
    )
    step = step_of(rows, source, row)
    same = step[:, None] == step[None, :]
    before = (step[None, :] < step[:, None]) | (same & (slot_ids[None, :] < slot_ids[:, None]))
    turn = jnp.sum(before.astype(jnp.int32), axis=1)
    like = same & (turn[:, None] % 2 == turn[None, :] % 2) & (turn[None, :] < turn[:, None])
    place = jnp.sum(like.astype(jnp.int32), axis=1)
    mine = jnp.arange(half, dtype=jnp.int32) * 2 + core
    own_pick = mine[:, None] == turn[None, :]
    other_pick = (mine ^ 1)[:, None] == turn[None, :]

    def pick(chosen, values):
        return jnp.sum(jnp.where(chosen, values[None, :], jnp.zeros((), values.dtype)), axis=1)

    own = pick(own_pick, slot_ids)
    other = pick(other_pick, slot_ids)
    far_step = pick(own_pick, step)
    own_far = pick(own_pick, far_slot[:, 0])
    own_place = pick(own_pick, place)

    orbitals = jnp.arange(occ_count, dtype=jnp.int32)

    def energy_of(index):
        found = index[:, None] == orbitals[None, :]
        return jnp.sum(jnp.where(found, occ_energy[None, :], jnp.float32(0.0)), axis=1)

    far_scale = pick(own_pick, far_weight[:, 0].astype(jnp.float32))
    first = pick(own_pick, first_occ)
    second = pick(own_pick, second_occ)
    shift = energy_of(first) + energy_of(second)

    by_slot = turn // 2 + jnp.where(turn % 2 == core, 0, half)
    early = half - tail
    swap = [(0, 1), (1, 0)]
    remote = (rows - 1) * cap
    local_spots = [
        slot_ids,
        jnp.where(
            by_slot < half,
            by_slot + jnp.where(by_slot % half < early, 0, early),
            by_slot - half + jnp.where(by_slot % half < early, early, half),
        ),
    ]
    homes = [
        jnp.sum(jnp.where(own_far[:, None] == slot_ids[None, :], where[None, :], 0), axis=1)
        for where in (slot_ids, by_slot)
    ]
    at_home = remote + jnp.arange(half, dtype=jnp.int32)
    spot = jnp.where(far_step == 0, at_home, (far_step - 1) * cap + own_place)
    numbers = jnp.concatenate([spot, first, second])
    near = [near_slot, near_weight]
    columns = [slot_ids, jnp.concatenate([own, other])]
    ats = [own, jnp.arange(half, dtype=jnp.int32)]
    slots = jnp.concatenate([own[:early], other[:early], own[early:], other[early:]])
    stores = [amplitudes]
    whole = [amplitudes]
    for sweep in range(ITERS):
        last = sweep == ITERS - 1
        again = min(sweep, 1)
        if sweep > 0:
            (send_lead,) = gather_again(asked_lead, local_spots[1], stores, lead, cap)
        arrived = [lax.ppermute(send_lead, "row", sent(rows, 1))]
        if sweep == 0:
            (*requests, _) = lax.optimization_barrier((*requests, send_lead))
            asked, *sends = gather_first(requests, rest, here, amplitudes, rows, cap)
        else:
            sends = gather_again(asked, local_spots[1], stores, rest, cap)
        for part, send in zip(rest, sends):
            arrived.append(lax.ppermute(send, "row", sent(rows, part[0])))
        *prepared, at_home = prepare(
            own, ats[again], homes[again], columns[again], near_count, shift, near, whole,
            integrals, fock_matrix, intersection,
        )
        spots = laid(arrived)
        at_home = [(remote, at_home)]
        done_early = finish(
            0, early, numbers, far_scale, prepared, spots[:-1] + at_home, occ_count,
            last,
        )
        given_early = lax.ppermute(done_early[0], "rep", swap)
        done_late = finish(
            early, tail, numbers, far_scale, prepared, spots + at_home, occ_count, last
        )
        given_late = lax.ppermute(done_late[0], "rep", swap)
        stores = [done_early[0], given_early, done_late[0], given_late]
        whole = [
            jnp.concatenate([done_early[0], done_late[0]], axis=0),
            jnp.concatenate([given_early, given_late], axis=0),
        ]
    final = put_in_slots(slots, stores)
    occ_sum = (done_early[1] + done_late[1])[0]
    occ_sum = add_over(occ_sum, "rep")
    occ_sum = add_over(occ_sum, "col")
    occ_sum = add_over(occ_sum, "row")
    total_pairs = pairs * rows * lax.axis_size("col")
    occ_density = occ_sum * (occ_count / (2.0 * total_pairs * domain * domain))
    return (final, occ_density)


def solution(mesh):
    pair_spec = P(("groups", "row", "col"), None, None)
    flat = P(("groups", "row", "col"))
    table = P(("groups", "row", "col"), None)
    return jax.shard_map(
        per_device,
        mesh=mesh,
        in_specs=(
            pair_spec, pair_spec, pair_spec, pair_spec,
            P("groups"), flat, flat, table, flat, table, table, table, table,
        ),
        out_specs=(pair_spec, P("groups")),
        check_vma=False,
    )
```

```python
import jax
import jax.numpy as jnp
from jax import lax
from jax.experimental import pallas as pl
from jax.experimental.pallas import tpu as pltpu
from jax.sharding import PartitionSpec as P


ITERS = 2
ANY = pl.ANY
SMEM = pltpu.SMEM
VMEM = pltpu.VMEM
LANES = 16
MIB = 1 << 20


def ring(rows, row):
    return row if rows & (rows - 1) else row ^ (row >> 1)


def sent(rows, step):
    hop = (step + 1) // 2 if step % 2 else rows - step // 2
    where = {ring(rows, r): r for r in range(rows)}
    return [(r, where[(ring(rows, r) + hop) % rows]) for r in range(rows)]


def asked_of(rows, step):
    return [(b, a) for a, b in sent(rows, step)]


def step_of(rows, source, row):
    hop = ring(rows, row) - ring(rows, source)
    hop = jnp.where(hop < 0, hop + rows, hop)
    step = jnp.where(2 * hop <= rows, 2 * hop - 1, 2 * (rows - hop))
    return jnp.where(hop == 0, 0, step)


def in_hbm(array):
    return pltpu.with_memory_space_constraint(array, pltpu.HBM)


def limits(mib):
    return pltpu.CompilerParams(vmem_limit_bytes=mib * MIB)


def cost(flops, size):
    return pl.CostEstimate(flops=flops, transcendentals=0, bytes_accessed=size)


def fetch(candidates, spot, target):
    for offset, ref in candidates:

        @pl.when((spot >= offset) & (spot < offset + ref.shape[0]))
        def _(offset=offset, ref=ref):
            target[...] = ref[spot - offset]


def laid(refs, offset=0):
    placed = []
    for ref in refs:
        placed.append((offset, ref))
        offset += ref.shape[0]
    return placed


def gather_first(requests, parts, place, amplitudes, rows, cap):
    pairs, domain = amplitudes.shape[:2]
    steps = sorted({step for step, _, _ in parts})
    count_of = len(steps)
    blocks = sum(size for _, _, size in parts)
    bits = pairs.bit_length() - 1

    def body(place_ref, *refs):
        lists = refs[:count_of]
        store = refs[count_of]
        asked = refs[count_of + 1]
        outs = refs[count_of + 2 : -1]
        sem = refs[-1]
        me = place_ref[0]
        core = place_ref[1]
        for n, step in enumerate(steps):
            base = n * (cap + 1)
            asker = jnp.int32(0)
            for a, b in sent(rows, step):
                asker = jnp.where(me == a, b, asker)
            served = [asker]
            for sooner in range(1, step):
                server = jnp.int32(0)
                for a, b in sent(rows, sooner):
                    server = jnp.where(asker == b, a, server)
                served.append(server)
            for k in range(cap):
                asked[base + k] = 0
            entries = [lists[n][p] for p in range(pairs)]
            sources = [entry // pairs if pairs & (pairs - 1) else entry >> bits for entry in entries]
            count = jnp.int32(0)
            for p in range(pairs):
                for server in served:
                    count = count + (sources[p] == server).astype(jnp.int32)
            filled = jnp.int32(0)
            for p in range(pairs):
                mine = (sources[p] == me).astype(jnp.int32)
                asked[base + jnp.minimum(filled, cap)] = entries[p] - sources[p] * pairs
                filled = filled + jnp.where((count & 1) == core, mine, 0)
                count = count + mine
            for m, (of, begin, size) in enumerate(parts):
                for k in range(size if of == step else 0):
                    pltpu.make_async_copy(
                        store.at[asked[base + begin + k]], outs[m].at[k], sem.at[m, k]
                    ).start()
        for m, (_, _, size) in enumerate(parts):
            for k in range(size):
                pltpu.make_async_copy(store.at[0], outs[m].at[k], sem.at[m, k]).wait()

    return pl.pallas_call(
        body,
        out_shape=[jax.ShapeDtypeStruct((count_of * (cap + 1),), jnp.int32)]
        + [VMEM((size, domain, domain), jnp.bfloat16) for _, _, size in parts],
        in_specs=[pl.BlockSpec(memory_space=SMEM)] * (count_of + 1)
        + [pl.BlockSpec(memory_space=pltpu.HBM)],
        out_specs=[pl.BlockSpec(memory_space=SMEM)]
        + [pl.BlockSpec(memory_space=VMEM)] * len(parts),
        scratch_shapes=[pltpu.SemaphoreType.DMA((len(parts), cap))],
        cost_estimate=cost(0, blocks * domain * domain * 4),
        compiler_params=limits(8),
        name="gather_first",
    )(place, *requests, in_hbm(amplitudes))


def gather_again(spots, stores, parts, cap):
    domain = stores[0].shape[1]
    steps = sorted({step for step, _, _ in parts})
    blocks = sum(size for _, _, size in parts)

    def body(spot_ref, *refs):
        sources = laid(refs[: len(stores)])
        outs = refs[len(stores) :]
        for m, (step, begin, size) in enumerate(parts):
            for k in range(size):
                spot = spot_ref[steps.index(step) * (cap + 1) + begin + k]
                fetch(sources, spot, outs[m].at[k])

    return pl.pallas_call(
        body,
        out_shape=[VMEM((size, domain, domain), jnp.bfloat16) for _, _, size in parts],
        in_specs=[pl.BlockSpec(memory_space=SMEM)]
        + [pl.BlockSpec(memory_space=VMEM)] * len(stores),
        out_specs=[pl.BlockSpec(memory_space=VMEM)] * len(parts),
        cost_estimate=cost(0, blocks * domain * domain * 4),
        compiler_params=limits(8),
        name="gather_again",
    )(spots, *stores)


def prepare(
    own, at, home, columns, counts, shift, near, stores, integrals, fock_matrix, intersection
):
    half = own.shape[0]
    domain = integrals.shape[1]
    total = columns.shape[0]
    entries = near[0].shape[1]
    groups = domain // LANES // half
    strip = groups * LANES

    def spread_weights(own_ref, column_ref, slot_ref, count_ref, weight_ref, spread_ref):
        lane = lax.broadcasted_iota(jnp.int32, (total, total), 1)
        down = lax.broadcasted_iota(jnp.int32, (total, total), 0)
        used_count = jnp.zeros((total, total), jnp.int32)
        for n in range(total):
            used_count = jnp.where(down == n, count_ref[n], used_count)
        weights = jnp.zeros((total, total), jnp.float32)
        for k in range(entries):
            used = (slot_ref[:, k : k + 1] == lane) & (k < used_count)
            wide = weight_ref[:, k : k + 1].astype(jnp.float32)
            weights = weights + jnp.where(used, wide, jnp.float32(0.0))
        weights = weights.astype(jnp.bfloat16)
        shape = (half * LANES, total)
        row = lax.broadcasted_iota(jnp.int32, shape, 0) // LANES
        wanted = jnp.zeros(shape, jnp.int32)
        for n in range(half):
            wanted = jnp.where(row == n, own_ref[n], wanted)
        pick = lax.broadcasted_iota(jnp.int32, shape, 1) == wanted
        mine = jnp.dot(
            pick.astype(jnp.float32).astype(jnp.bfloat16),
            weights,
            preferred_element_type=jnp.float32,
        ).astype(jnp.bfloat16)
        shape = (total, total * LANES)
        column = lax.broadcasted_iota(jnp.int32, shape, 1) // LANES
        wanted = jnp.zeros(shape, jnp.int32)
        for n in range(total):
            wanted = jnp.where(column == n, column_ref[n], wanted)
        pick = lax.broadcasted_iota(jnp.int32, shape, 0) == wanted
        full = jnp.dot(
            mine,
            pick.astype(jnp.float32).astype(jnp.bfloat16),
            preferred_element_type=jnp.float32,
        )
        shape = (half * LANES, total * LANES)
        down = lax.broadcasted_iota(jnp.int32, shape, 0) % LANES
        along = lax.broadcasted_iota(jnp.int32, shape, 1) % LANES
        spread_ref[...] = jnp.where(down == along, full, 0.0).astype(jnp.bfloat16)

    def body(
        own_ref, at_ref, home_ref, column_ref, count_ref, shift_ref, slot_ref, weight_ref, *refs
    ):
        sources = refs[: len(stores)]
        (
            integ_ref, fock_ref, over_ref,
            local_ref, rest_ref, recip_ref, keep_ref, near_by_ref, spread_ref,
        ) = refs[len(stores) :]
        i = pl.program_id(0)

        @pl.when(i == 0)
        def _():
            spread_weights(own_ref, column_ref, slot_ref, count_ref, weight_ref, spread_ref)

        for g in range(groups):
            rows = pl.ds(pl.multiple_of(i * strip + g * LANES, LANES), LANES)
            part = [s[:, rows, :].reshape(s.shape[0] * LANES, domain) for s in sources]
            part = part[0] if len(part) == 1 else jnp.concatenate(part, axis=0)
            sums = jnp.dot(spread_ref[...], part, preferred_element_type=jnp.float32)
            local_ref[:, g * LANES : (g + 1) * LANES, :] = sums.reshape(half, LANES, domain)
        amps = sources[0][at_ref[i]]
        fock = fock_ref[0]
        wide = amps.astype(jnp.float32)
        left = jnp.dot(fock, amps, preferred_element_type=jnp.float32)
        right = jnp.dot(amps, fock, preferred_element_type=jnp.float32)
        row_id = lax.broadcasted_iota(jnp.int32, (domain, domain), 0)
        col_id = lax.broadcasted_iota(jnp.int32, (domain, domain), 1)
        diagonal = jnp.where(row_id == col_id, fock.astype(jnp.float32), 0.0)
        across = jnp.sum(diagonal, axis=0, keepdims=True)
        down = jnp.sum(diagonal, axis=1, keepdims=True)
        residual = integ_ref[0].astype(jnp.float32) + left + right - shift_ref[i] * wide
        recip = 1.0 / (down + across - shift_ref[i])
        recip_ref[0] = recip
        rest_ref[0] = wide - residual * recip
        keep_ref[0] = over_ref[0]
        fetch(laid(sources), home_ref[i], near_by_ref.at[0])

    block = (1, domain, domain)
    mine = pl.BlockSpec(block, lambda i, own, *_: (own[i], 0, 0))
    in_turn = pl.BlockSpec(block, lambda i, *_: (i, 0, 0))
    wide_shape = jax.ShapeDtypeStruct((half, domain, domain), jnp.float32)
    return pl.pallas_call(
        body,
        grid_spec=pltpu.PrefetchScalarGridSpec(
            num_scalar_prefetch=6,
            grid=(half,),
            in_specs=[pl.BlockSpec(n.shape, lambda i, *_: (0, 0)) for n in near]
            + [pl.BlockSpec(s.shape, lambda i, *_: (0, 0, 0)) for s in stores]
            + [mine, mine, mine],
            out_specs=[
                pl.BlockSpec((half, strip, domain), lambda i, *_: (0, i, 0)),
                in_turn,
                in_turn,
                in_turn,
                in_turn,
            ],
            scratch_shapes=[VMEM((half * LANES, total * LANES), jnp.bfloat16)],
        ),
        out_shape=[
            wide_shape,
            wide_shape,
            wide_shape,
            jax.ShapeDtypeStruct((half, domain, domain), jnp.bfloat16),
            jax.ShapeDtypeStruct((half, domain, domain), jnp.bfloat16),
        ],
        cost_estimate=cost(
            2 * half * domain**3 * 3,
            (total + 4 * half) * domain * domain * 2 + half * domain * domain * 12,
        ),
        compiler_params=limits(20),
        name="prepare",
    )(
        own, at, home, columns, counts, shift, *near,
        *[in_hbm(s) if s.shape[0] > half else s for s in stores],
        in_hbm(integrals), in_hbm(fock_matrix), in_hbm(intersection),
    )


def finish(start, count, numbers, scale, prepared, arrived, occ_count, last):
    half, domain = prepared[0].shape[:2]

    def body(number_ref, scale_ref, local_ref, rest_ref, recip_ref, over_ref, *refs):
        candidates = [
            (offset, ref) for offset, ref in zip([o for o, _ in arrived], refs)
        ]
        outs = refs[len(candidates) : -1]
        hold = refs[-1]
        for n in range(count):
            fetch(candidates, number_ref[start + n], hold.at[n])
        if last:
            row_id = lax.broadcasted_iota(jnp.int32, (domain, domain), 0)
            col_id = lax.broadcasted_iota(jnp.int32, (domain, domain), 1)
            on_diagonal = row_id == col_id
            orbital = lax.broadcasted_iota(jnp.int32, (1, occ_count), 1)
            density = jnp.zeros((1, occ_count), jnp.float32)
        for n in range(count):
            i = start + n
            coupled = local_ref[i] + scale_ref[i : i + 1, :] * hold[n].astype(jnp.float32)
            over = over_ref[i]
            projected = jnp.dot(
                over, coupled.astype(jnp.bfloat16), preferred_element_type=jnp.float32
            )
            back = lax.dot_general(
                projected.astype(jnp.bfloat16),
                over,
                (((1,), (1,)), ((), ())),
                preferred_element_type=jnp.float32,
            )
            fresh = (rest_ref[i] + back * recip_ref[i]).astype(jnp.bfloat16)
            outs[0][n] = fresh
            if last:
                wide = fresh.astype(jnp.float32)
                square = jnp.dot(fresh, fresh, preferred_element_type=jnp.float32)
                terms = 2.0 * wide * wide - jnp.where(on_diagonal, square, 0.0)
                norm = jnp.sum(jnp.sum(terms, axis=0, keepdims=True), axis=1, keepdims=True)
                picks = (orbital == number_ref[half + i]).astype(jnp.float32)
                picks = picks + (orbital == number_ref[2 * half + i]).astype(jnp.float32)
                density = density + norm * picks
        if last:
            outs[1][...] = density

    out_shape = [VMEM((count, domain, domain), jnp.bfloat16)]
    if last:
        out_shape.append(VMEM((1, occ_count), jnp.float32))
    return pl.pallas_call(
        body,
        out_shape=out_shape,
        in_specs=[pl.BlockSpec(memory_space=SMEM)]
        + [pl.BlockSpec(memory_space=VMEM)] * 5
        + [pl.BlockSpec(memory_space=VMEM)] * len(arrived),
        out_specs=[pl.BlockSpec(memory_space=VMEM)] * len(out_shape),
        scratch_shapes=[VMEM((count, domain, domain), jnp.bfloat16)],
        cost_estimate=cost(2 * count * domain**3 * 2, count * domain * domain * 18),
        compiler_params=limits(16),
        name="finish",
    )(numbers, scale, *prepared, *[a for _, a in arrived])


def put_in_slots(slots, stores, total, whole=None):
    domain = stores[0].shape[1]
    blocks = sum(s.shape[0] for s in stores)
    given = [] if whole is None else [whole]

    def body(slot_ref, *refs):
        sources = refs[: len(stores)]
        out_ref, sem = refs[-2:]
        copies = []
        for source in sources:
            for n in range(source.shape[0]):
                at = len(copies)
                copies.append(
                    pltpu.make_async_copy(source.at[n], out_ref.at[slot_ref[at]], sem.at[at])
                )
        for copy in copies:
            copy.start()
        for copy in copies:
            copy.wait()

    return pl.pallas_call(
        body,
        out_shape=jax.ShapeDtypeStruct((total, domain, domain), jnp.bfloat16),
        in_specs=[pl.BlockSpec(memory_space=SMEM)]
        + [pl.BlockSpec(memory_space=VMEM)] * len(stores)
        + [pl.BlockSpec(memory_space=ANY)] * len(given),
        out_specs=pl.BlockSpec(memory_space=ANY),
        scratch_shapes=[pltpu.SemaphoreType.DMA((blocks,))],
        input_output_aliases={1 + len(stores): 0} if given else {},
        cost_estimate=cost(0, blocks * domain * domain * 4),
        compiler_params=limits(8),
        name="put_in_slots",
    )(slots, *stores, *given)


def add_over(values, name):
    size = lax.axis_size(name)
    if size & (size - 1):
        return lax.psum(values, name)
    steps = [1 << bit for bit in range(size.bit_length() - 1)]
    if name == "row":
        steps = [size - 1] + steps[:-1]
    for step in steps:
        values = values + lax.ppermute(values, name, [(r, r ^ step) for r in range(size)])
    return values


def per_device(
    amplitudes,
    integrals,
    fock_matrix,
    intersection,
    occ_energy,
    first_occ,
    second_occ,
    near_slot,
    near_count,
    near_weight,
    far_chip,
    far_slot,
    far_weight,
):
    pairs, domain = amplitudes.shape[:2]
    rows = lax.axis_size("row")
    half = pairs // 2
    cap = pairs // rows
    row = lax.axis_index("row")
    core = lax.axis_index("rep")
    occ_count = occ_energy.shape[0]
    slot_ids = jnp.arange(pairs, dtype=jnp.int32)
    source = far_chip[:, 0]
    packed = source * pairs + far_slot[:, 0]
    here = jnp.stack([row, core]).astype(jnp.int32)
    tail = max(1, cap // 2)
    lead = [(1, 0, cap)]
    rest = [(step, 0, cap) for step in range(2, rows - 1)]
    rest += [(rows - 1, 0, cap - tail)] * (cap > tail) + [(rows - 1, cap - tail, tail)]
    request = lax.ppermute(packed, "row", asked_of(rows, 1))
    requests = [
        lax.ppermute(packed, "row", asked_of(rows, d)) for d in range(2, rows)
    ]
    asked_lead, send_lead = gather_first([request], lead, here, amplitudes, rows, cap)

    (
        source, far_slot, occ_energy, first_occ, second_occ, far_weight,
        _,
    ) = lax.optimization_barrier(
        (
            source, far_slot, occ_energy, first_occ, second_occ, far_weight,
            asked_lead,
        )
    )
    step = step_of(rows, source, row)
    same = step[:, None] == step[None, :]
    before = (step[None, :] < step[:, None]) | (same & (slot_ids[None, :] < slot_ids[:, None]))
    turn = jnp.sum(before.astype(jnp.int32), axis=1)
    like = same & (turn[:, None] % 2 == turn[None, :] % 2) & (turn[None, :] < turn[:, None])
    place = jnp.sum(like.astype(jnp.int32), axis=1)
    mine = jnp.arange(half, dtype=jnp.int32) * 2 + core
    own_pick = mine[:, None] == turn[None, :]
    other_pick = (mine ^ 1)[:, None] == turn[None, :]

    def pick(chosen, values):
        return jnp.sum(jnp.where(chosen, values[None, :], jnp.zeros((), values.dtype)), axis=1)

    own = pick(own_pick, slot_ids)
    other = pick(other_pick, slot_ids)
    far_step = pick(own_pick, step)
    own_far = pick(own_pick, far_slot[:, 0])
    own_place = pick(own_pick, place)

    orbitals = jnp.arange(occ_count, dtype=jnp.int32)

    def energy_of(index):
        found = index[:, None] == orbitals[None, :]
        return jnp.sum(jnp.where(found, occ_energy[None, :], jnp.float32(0.0)), axis=1)

    far_scale = pick(own_pick, far_weight[:, 0].astype(jnp.float32))
    far_scale = jnp.broadcast_to(far_scale[:, None], (half, domain))
    first = pick(own_pick, first_occ)
    second = pick(own_pick, second_occ)
    shift = energy_of(first) + energy_of(second)

    by_slot = turn // 2 + jnp.where(turn % 2 == core, 0, half)
    early = half - tail
    swap = [(0, 1), (1, 0)]
    remote = (rows - 1) * cap
    local_spots = [
        slot_ids,
        jnp.where(
            by_slot < half,
            by_slot + jnp.where(by_slot % half < early, 0, early),
            by_slot - half + jnp.where(by_slot % half < early, early, half),
        ),
    ]
    homes = [
        jnp.sum(jnp.where(own_far[:, None] == slot_ids[None, :], where[None, :], 0), axis=1)
        for where in (slot_ids, by_slot)
    ]
    at_home = remote + jnp.arange(half, dtype=jnp.int32)
    spot = jnp.where(far_step == 0, at_home, (far_step - 1) * cap + own_place)
    numbers = jnp.concatenate([spot, first, second])
    near = [near_slot, near_weight]
    columns = [slot_ids, jnp.concatenate([own, other])]
    ats = [own, jnp.arange(half, dtype=jnp.int32)]
    slots = jnp.concatenate([other[:early], own[early:], other[early:]])

    def spots_of(slots_asked):
        found = slots_asked[:, None] == slot_ids[None, :]
        return jnp.sum(jnp.where(found, local_spots[1][None, :], 0), axis=1)

    stores = [amplitudes]
    whole = [amplitudes]
    for sweep in range(ITERS):
        last = sweep == ITERS - 1
        again = min(sweep, 1)
        if sweep > 0:
            (send_lead,) = gather_again(spots_of(asked_lead), stores, lead, cap)
        arrived = [lax.ppermute(send_lead, "row", sent(rows, 1))]
        if sweep == 0:
            (*requests, _) = lax.optimization_barrier((*requests, send_lead))
            asked, *sends = gather_first(requests, rest, here, amplitudes, rows, cap)
        else:
            sends = gather_again(spots_of(asked), stores, rest, cap)
        for part, send in zip(rest, sends):
            arrived.append(lax.ppermute(send, "row", sent(rows, part[0])))
        *prepared, at_home = prepare(
            own, ats[again], homes[again], columns[again], near_count, shift, near, whole,
            integrals, fock_matrix, intersection,
        )
        spots = laid(arrived)
        at_home = [(remote, at_home)]
        done_early = finish(
            0, early, numbers, far_scale, prepared, spots[:-1] + at_home, occ_count,
            last,
        )
        given_early = lax.ppermute(done_early[0], "rep", swap)
        if last:
            final = put_in_slots(own[:early], [done_early[0]], pairs)
        done_late = finish(
            early, tail, numbers, far_scale, prepared, spots + at_home, occ_count, last
        )
        given_late = lax.ppermute(done_late[0], "rep", swap)
        stores = [done_early[0], given_early, done_late[0], given_late]
        whole = [
            jnp.concatenate([done_early[0], done_late[0]], axis=0),
            jnp.concatenate([given_early, given_late], axis=0),
        ]
    final = put_in_slots(slots, stores[1:], pairs, final)
    occ_sum = (done_early[1] + done_late[1])[0]
    occ_sum = add_over(occ_sum, "rep")
    occ_sum = add_over(occ_sum, "col")
    occ_sum = add_over(occ_sum, "row")
    total_pairs = pairs * rows * lax.axis_size("col")
    occ_density = occ_sum * (occ_count / (2.0 * total_pairs * domain * domain))
    return (final, occ_density)


def solution(mesh):
    pair_spec = P(("groups", "row", "col"), None, None)
    flat = P(("groups", "row", "col"))
    table = P(("groups", "row", "col"), None)
    return jax.shard_map(
        per_device,
        mesh=mesh,
        in_specs=(
            pair_spec, pair_spec, pair_spec, pair_spec,
            P("groups"), flat, flat, table, flat, table, table, table, table,
        ),
        out_specs=(pair_spec, P("groups")),
        check_vma=False,
    )
```

```python
import jax
import jax.numpy as jnp
from jax import lax
from jax.experimental import pallas as pl
from jax.experimental.pallas import tpu as pltpu
from jax.sharding import PartitionSpec as P


ITERS = 2
ANY = pl.ANY
SMEM = pltpu.SMEM
VMEM = pltpu.VMEM
LANES = 16
MIB = 1 << 20


def ring(rows, row):
    return row if rows & (rows - 1) else row ^ (row >> 1)


def sent(rows, step):
    hop = (step + 1) // 2 if step % 2 else rows - step // 2
    where = {ring(rows, r): r for r in range(rows)}
    return [(r, where[(ring(rows, r) + hop) % rows]) for r in range(rows)]


def asked_of(rows, step):
    return [(b, a) for a, b in sent(rows, step)]


def step_of(rows, source, row):
    hop = ring(rows, row) - ring(rows, source)
    hop = jnp.where(hop < 0, hop + rows, hop)
    step = jnp.where(2 * hop <= rows, 2 * hop - 1, 2 * (rows - hop))
    return jnp.where(hop == 0, 0, step)


def in_hbm(array):
    return pltpu.with_memory_space_constraint(array, pltpu.HBM)


def limits(mib):
    return pltpu.CompilerParams(vmem_limit_bytes=mib * MIB)


def cost(flops, size):
    return pl.CostEstimate(flops=flops, transcendentals=0, bytes_accessed=size)


def fetch(candidates, spot, target):
    for offset, ref in candidates:

        @pl.when((spot >= offset) & (spot < offset + ref.shape[0]))
        def _(offset=offset, ref=ref):
            target[...] = ref[spot - offset]


def laid(refs, offset=0):
    placed = []
    for ref in refs:
        placed.append((offset, ref))
        offset += ref.shape[0]
    return placed


def gather_first(requests, parts, place, amplitudes, rows, cap):
    pairs, domain = amplitudes.shape[:2]
    steps = sorted({step for step, _, _ in parts})
    count_of = len(steps)
    blocks = sum(size for _, _, size in parts)
    bits = pairs.bit_length() - 1

    def body(place_ref, *refs):
        lists = refs[:count_of]
        store = refs[count_of]
        asked = refs[count_of + 1]
        outs = refs[count_of + 2 : -1]
        sem = refs[-1]
        me = place_ref[0]
        core = place_ref[1]
        for n, step in enumerate(steps):
            base = n * (cap + 1)
            asker = jnp.int32(0)
            for a, b in sent(rows, step):
                asker = jnp.where(me == a, b, asker)
            served = [asker]
            for sooner in range(1, step):
                server = jnp.int32(0)
                for a, b in sent(rows, sooner):
                    server = jnp.where(asker == b, a, server)
                served.append(server)
            for k in range(cap):
                asked[base + k] = 0
            entries = [lists[n][p] for p in range(pairs)]
            sources = [entry // pairs if pairs & (pairs - 1) else entry >> bits for entry in entries]
            count = jnp.int32(0)
            for p in range(pairs):
                for server in served:
                    count = count + (sources[p] == server).astype(jnp.int32)
            filled = jnp.int32(0)
            for p in range(pairs):
                mine = (sources[p] == me).astype(jnp.int32)
                asked[base + jnp.minimum(filled, cap)] = entries[p] - sources[p] * pairs
                filled = filled + jnp.where((count & 1) == core, mine, 0)
                count = count + mine
            for m, (of, begin, size) in enumerate(parts):
                for k in range(size if of == step else 0):
                    pltpu.make_async_copy(
                        store.at[asked[base + begin + k]], outs[m].at[k], sem.at[m, k]
                    ).start()
        for m, (_, _, size) in enumerate(parts):
            for k in range(size):
                pltpu.make_async_copy(store.at[0], outs[m].at[k], sem.at[m, k]).wait()

    return pl.pallas_call(
        body,
        out_shape=[jax.ShapeDtypeStruct((count_of * (cap + 1),), jnp.int32)]
        + [VMEM((size, domain, domain), jnp.bfloat16) for _, _, size in parts],
        in_specs=[pl.BlockSpec(memory_space=SMEM)] * (count_of + 1)
        + [pl.BlockSpec(memory_space=pltpu.HBM)],
        out_specs=[pl.BlockSpec(memory_space=SMEM)]
        + [pl.BlockSpec(memory_space=VMEM)] * len(parts),
        scratch_shapes=[pltpu.SemaphoreType.DMA((len(parts), cap))],
        cost_estimate=cost(0, blocks * domain * domain * 4),
        compiler_params=limits(8),
        name="gather_first",
    )(place, *requests, in_hbm(amplitudes))


def gather_again(asked, where, stores, parts, cap):
    domain = stores[0].shape[1]
    steps = sorted({step for step, _, _ in parts})
    blocks = sum(size for _, _, size in parts)

    def body(asked_ref, where_ref, *refs):
        sources = laid(refs[: len(stores)])
        outs = refs[len(stores) :]
        for m, (step, begin, size) in enumerate(parts):
            for k in range(size):
                spot = where_ref[asked_ref[steps.index(step) * (cap + 1) + begin + k]]
                fetch(sources, spot, outs[m].at[k])

    return pl.pallas_call(
        body,
        out_shape=[VMEM((size, domain, domain), jnp.bfloat16) for _, _, size in parts],
        in_specs=[pl.BlockSpec(memory_space=SMEM)] * 2
        + [pl.BlockSpec(memory_space=VMEM)] * len(stores),
        out_specs=[pl.BlockSpec(memory_space=VMEM)] * len(parts),
        cost_estimate=cost(0, blocks * domain * domain * 4),
        compiler_params=limits(8),
        name="gather_again",
    )(asked, where, *stores)


def prepare(
    own, at, home, columns, counts, shift, near, stores, integrals, fock_matrix, intersection
):
    half = own.shape[0]
    domain = integrals.shape[1]
    total = columns.shape[0]
    entries = near[0].shape[1]
    groups = domain // LANES // half
    strip = groups * LANES

    def spread_weights(own_ref, column_ref, slot_ref, count_ref, weight_ref, spread_ref):
        lane = lax.broadcasted_iota(jnp.int32, (total, total), 1)
        down = lax.broadcasted_iota(jnp.int32, (total, total), 0)
        used_count = jnp.zeros((total, total), jnp.int32)
        for n in range(total):
            used_count = jnp.where(down == n, count_ref[n], used_count)
        weights = jnp.zeros((total, total), jnp.float32)
        for k in range(entries):
            used = (slot_ref[:, k : k + 1] == lane) & (k < used_count)
            wide = weight_ref[:, k : k + 1].astype(jnp.float32)
            weights = weights + jnp.where(used, wide, jnp.float32(0.0))
        weights = weights.astype(jnp.bfloat16)
        shape = (half * LANES, total)
        row = lax.broadcasted_iota(jnp.int32, shape, 0) // LANES
        wanted = jnp.zeros(shape, jnp.int32)
        for n in range(half):
            wanted = jnp.where(row == n, own_ref[n], wanted)
        pick = lax.broadcasted_iota(jnp.int32, shape, 1) == wanted
        mine = jnp.dot(
            pick.astype(jnp.float32).astype(jnp.bfloat16),
            weights,
            preferred_element_type=jnp.float32,
        ).astype(jnp.bfloat16)
        shape = (total, total * LANES)
        column = lax.broadcasted_iota(jnp.int32, shape, 1) // LANES
        wanted = jnp.zeros(shape, jnp.int32)
        for n in range(total):
            wanted = jnp.where(column == n, column_ref[n], wanted)
        pick = lax.broadcasted_iota(jnp.int32, shape, 0) == wanted
        full = jnp.dot(
            mine,
            pick.astype(jnp.float32).astype(jnp.bfloat16),
            preferred_element_type=jnp.float32,
        )
        shape = (half * LANES, total * LANES)
        down = lax.broadcasted_iota(jnp.int32, shape, 0) % LANES
        along = lax.broadcasted_iota(jnp.int32, shape, 1) % LANES
        spread_ref[...] = jnp.where(down == along, full, 0.0).astype(jnp.bfloat16)

    def body(
        own_ref, at_ref, home_ref, column_ref, count_ref, shift_ref, slot_ref, weight_ref, *refs
    ):
        sources = refs[: len(stores)]
        (
            integ_ref, fock_ref, over_ref,
            local_ref, rest_ref, recip_ref, keep_ref, near_by_ref, spread_ref,
        ) = refs[len(stores) :]
        i = pl.program_id(0)

        @pl.when(i == 0)
        def _():
            spread_weights(own_ref, column_ref, slot_ref, count_ref, weight_ref, spread_ref)

        for g in range(groups):
            rows = pl.ds(pl.multiple_of(i * strip + g * LANES, LANES), LANES)
            part = [s[:, rows, :].reshape(s.shape[0] * LANES, domain) for s in sources]
            part = part[0] if len(part) == 1 else jnp.concatenate(part, axis=0)
            sums = jnp.dot(spread_ref[...], part, preferred_element_type=jnp.float32)
            local_ref[:, g * LANES : (g + 1) * LANES, :] = sums.reshape(half, LANES, domain)
        amps = sources[0][at_ref[i]]
        fock = fock_ref[0]
        wide = amps.astype(jnp.float32)
        left = jnp.dot(fock, amps, preferred_element_type=jnp.float32)
        right = jnp.dot(amps, fock, preferred_element_type=jnp.float32)
        row_id = lax.broadcasted_iota(jnp.int32, (domain, domain), 0)
        col_id = lax.broadcasted_iota(jnp.int32, (domain, domain), 1)
        diagonal = jnp.where(row_id == col_id, fock.astype(jnp.float32), 0.0)
        across = jnp.sum(diagonal, axis=0, keepdims=True)
        down = jnp.sum(diagonal, axis=1, keepdims=True)
        residual = integ_ref[0].astype(jnp.float32) + left + right - shift_ref[i] * wide
        recip = 1.0 / (down + across - shift_ref[i])
        recip_ref[0] = recip
        rest_ref[0] = wide - residual * recip
        keep_ref[0] = over_ref[0]
        fetch(laid(sources), home_ref[i], near_by_ref.at[0])

    block = (1, domain, domain)
    mine = pl.BlockSpec(block, lambda i, own, *_: (own[i], 0, 0))
    in_turn = pl.BlockSpec(block, lambda i, *_: (i, 0, 0))
    wide_shape = jax.ShapeDtypeStruct((half, domain, domain), jnp.float32)
    return pl.pallas_call(
        body,
        grid_spec=pltpu.PrefetchScalarGridSpec(
            num_scalar_prefetch=6,
            grid=(half,),
            in_specs=[pl.BlockSpec(n.shape, lambda i, *_: (0, 0)) for n in near]
            + [pl.BlockSpec(s.shape, lambda i, *_: (0, 0, 0)) for s in stores]
            + [mine, mine, mine],
            out_specs=[
                pl.BlockSpec((half, strip, domain), lambda i, *_: (0, i, 0)),
                in_turn,
                in_turn,
                in_turn,
                in_turn,
            ],
            scratch_shapes=[VMEM((half * LANES, total * LANES), jnp.bfloat16)],
        ),
        out_shape=[
            wide_shape,
            wide_shape,
            wide_shape,
            jax.ShapeDtypeStruct((half, domain, domain), jnp.bfloat16),
            jax.ShapeDtypeStruct((half, domain, domain), jnp.bfloat16),
        ],
        cost_estimate=cost(
            2 * half * domain**3 * 3,
            (total + 4 * half) * domain * domain * 2 + half * domain * domain * 12,
        ),
        compiler_params=limits(20),
        name="prepare",
    )(
        own, at, home, columns, counts, shift, *near,
        *[in_hbm(s) if s.shape[0] > half else s for s in stores],
        in_hbm(integrals), in_hbm(fock_matrix), in_hbm(intersection),
    )


def finish(start, count, numbers, scale, prepared, arrived, occ_count, last):
    half, domain = prepared[0].shape[:2]

    def body(number_ref, scale_ref, local_ref, rest_ref, recip_ref, over_ref, *refs):
        candidates = [
            (offset, ref) for offset, ref in zip([o for o, _ in arrived], refs)
        ]
        outs = refs[len(candidates) : -1]
        hold = refs[-1]
        for n in range(count):
            fetch(candidates, number_ref[start + n], hold.at[n])
        if last:
            row_id = lax.broadcasted_iota(jnp.int32, (domain, domain), 0)
            col_id = lax.broadcasted_iota(jnp.int32, (domain, domain), 1)
            on_diagonal = row_id == col_id
            orbital = lax.broadcasted_iota(jnp.int32, (1, occ_count), 1)
            density = jnp.zeros((1, occ_count), jnp.float32)
        for n in range(count):
            i = start + n
            coupled = local_ref[i] + scale_ref[i] * hold[n].astype(jnp.float32)
            over = over_ref[i]
            projected = jnp.dot(
                over, coupled.astype(jnp.bfloat16), preferred_element_type=jnp.float32
            )
            back = lax.dot_general(
                projected.astype(jnp.bfloat16),
                over,
                (((1,), (1,)), ((), ())),
                preferred_element_type=jnp.float32,
            )
            fresh = (rest_ref[i] + back * recip_ref[i]).astype(jnp.bfloat16)
            outs[0][n] = fresh
            if last:
                wide = fresh.astype(jnp.float32)
                square = jnp.dot(fresh, fresh, preferred_element_type=jnp.float32)
                terms = 2.0 * wide * wide - jnp.where(on_diagonal, square, 0.0)
                norm = jnp.sum(jnp.sum(terms, axis=0, keepdims=True), axis=1, keepdims=True)
                picks = (orbital == number_ref[half + i]).astype(jnp.float32)
                picks = picks + (orbital == number_ref[2 * half + i]).astype(jnp.float32)
                density = density + norm * picks
        if last:
            outs[1][...] = density

    out_shape = [VMEM((count, domain, domain), jnp.bfloat16)]
    if last:
        out_shape.append(VMEM((1, occ_count), jnp.float32))
    return pl.pallas_call(
        body,
        out_shape=out_shape,
        in_specs=[pl.BlockSpec(memory_space=SMEM)] * 2
        + [pl.BlockSpec(memory_space=VMEM)] * 4
        + [pl.BlockSpec(memory_space=VMEM)] * len(arrived),
        out_specs=[pl.BlockSpec(memory_space=VMEM)] * len(out_shape),
        scratch_shapes=[VMEM((count, domain, domain), jnp.bfloat16)],
        cost_estimate=cost(2 * count * domain**3 * 2, count * domain * domain * 18),
        compiler_params=limits(16),
        name="finish",
    )(numbers, scale, *prepared, *[a for _, a in arrived])


def put_in_slots(slots, stores, total, whole=None):
    domain = stores[0].shape[1]
    blocks = sum(s.shape[0] for s in stores)
    given = [] if whole is None else [whole]

    def body(slot_ref, *refs):
        sources = refs[: len(stores)]
        out_ref, sem = refs[-2:]
        copies = []
        for source in sources:
            for n in range(source.shape[0]):
                at = len(copies)
                copies.append(
                    pltpu.make_async_copy(source.at[n], out_ref.at[slot_ref[at]], sem.at[at])
                )
        for copy in copies:
            copy.start()
        for copy in copies:
            copy.wait()

    return pl.pallas_call(
        body,
        out_shape=jax.ShapeDtypeStruct((total, domain, domain), jnp.bfloat16),
        in_specs=[pl.BlockSpec(memory_space=SMEM)]
        + [pl.BlockSpec(memory_space=VMEM)] * len(stores)
        + [pl.BlockSpec(memory_space=ANY)] * len(given),
        out_specs=pl.BlockSpec(memory_space=ANY),
        scratch_shapes=[pltpu.SemaphoreType.DMA((blocks,))],
        input_output_aliases={1 + len(stores): 0} if given else {},
        cost_estimate=cost(0, blocks * domain * domain * 4),
        compiler_params=limits(8),
        name="put_in_slots",
    )(slots, *stores, *given)


def add_over(values, name):
    size = lax.axis_size(name)
    if size & (size - 1):
        return lax.psum(values, name)
    steps = [1 << bit for bit in range(size.bit_length() - 1)]
    if name == "row":
        steps = [size - 1] + steps[:-1]
    for step in steps:
        values = values + lax.ppermute(values, name, [(r, r ^ step) for r in range(size)])
    return values


def per_device(
    amplitudes,
    integrals,
    fock_matrix,
    intersection,
    occ_energy,
    first_occ,
    second_occ,
    near_slot,
    near_count,
    near_weight,
    far_chip,
    far_slot,
    far_weight,
):
    pairs, domain = amplitudes.shape[:2]
    rows = lax.axis_size("row")
    half = pairs // 2
    cap = pairs // rows
    row = lax.axis_index("row")
    core = lax.axis_index("rep")
    occ_count = occ_energy.shape[0]
    slot_ids = jnp.arange(pairs, dtype=jnp.int32)
    source = far_chip[:, 0]
    packed = source * pairs + far_slot[:, 0]
    here = jnp.stack([row, core]).astype(jnp.int32)
    tail = max(1, cap // 2)
    lead = [(1, 0, cap)]
    inner = [(step, 0, cap) for step in range(2, rows - 1)]
    outer = [(rows - 1, 0, cap - tail)] * (cap > tail) + [(rows - 1, cap - tail, tail)]
    request = lax.ppermute(packed, "row", asked_of(rows, 1))
    requests = [
        lax.ppermute(packed, "row", asked_of(rows, d)) for d in range(2, rows - 1)
    ]
    asked_lead, send_lead = gather_first([request], lead, here, amplitudes, rows, cap)

    (
        source, far_slot, occ_energy, first_occ, second_occ, far_weight,
        _,
    ) = lax.optimization_barrier(
        (
            source, far_slot, occ_energy, first_occ, second_occ, far_weight,
            asked_lead,
        )
    )
    step = step_of(rows, source, row)
    same = step[:, None] == step[None, :]
    before = (step[None, :] < step[:, None]) | (same & (slot_ids[None, :] < slot_ids[:, None]))
    turn = jnp.sum(before.astype(jnp.int32), axis=1)
    like = same & (turn[:, None] % 2 == turn[None, :] % 2) & (turn[None, :] < turn[:, None])
    place = jnp.sum(like.astype(jnp.int32), axis=1)
    mine = jnp.arange(half, dtype=jnp.int32) * 2 + core
    own_pick = mine[:, None] == turn[None, :]
    other_pick = (mine ^ 1)[:, None] == turn[None, :]

    def pick(chosen, values):
        return jnp.sum(jnp.where(chosen, values[None, :], jnp.zeros((), values.dtype)), axis=1)

    own = pick(own_pick, slot_ids)
    other = pick(other_pick, slot_ids)
    far_step = pick(own_pick, step)
    own_far = pick(own_pick, far_slot[:, 0])
    own_place = pick(own_pick, place)

    orbitals = jnp.arange(occ_count, dtype=jnp.int32)

    def energy_of(index):
        found = index[:, None] == orbitals[None, :]
        return jnp.sum(jnp.where(found, occ_energy[None, :], jnp.float32(0.0)), axis=1)

    far_scale = pick(own_pick, far_weight[:, 0].astype(jnp.float32))
    first = pick(own_pick, first_occ)
    second = pick(own_pick, second_occ)
    shift = energy_of(first) + energy_of(second)

    by_slot = turn // 2 + jnp.where(turn % 2 == core, 0, half)
    early = half - tail
    swap = [(0, 1), (1, 0)]
    remote = (rows - 1) * cap
    local_spots = [
        slot_ids,
        jnp.where(
            by_slot < half,
            by_slot + jnp.where(by_slot % half < early, 0, early),
            by_slot - half + jnp.where(by_slot % half < early, early, half),
        ),
    ]
    homes = [
        jnp.sum(jnp.where(own_far[:, None] == slot_ids[None, :], where[None, :], 0), axis=1)
        for where in (slot_ids, by_slot)
    ]
    at_home = remote + jnp.arange(half, dtype=jnp.int32)
    spot = jnp.where(far_step == 0, at_home, (far_step - 1) * cap + own_place)
    numbers = jnp.concatenate([spot, first, second])
    near = [near_slot, near_weight]
    columns = [slot_ids, jnp.concatenate([own, other])]
    ats = [own, jnp.arange(half, dtype=jnp.int32)]
    slots = jnp.concatenate([other[:early], own[early:], other[early:]])
    stores = [amplitudes]
    whole = [amplitudes]
    for sweep in range(ITERS):
        last = sweep == ITERS - 1
        again = min(sweep, 1)
        if sweep > 0:
            (send_lead,) = gather_again(asked_lead, local_spots[1], stores, lead, cap)
        arrived = [lax.ppermute(send_lead, "row", sent(rows, 1))]
        if sweep == 0:
            request = lax.ppermute(packed, "row", asked_of(rows, rows - 1))
            (*requests, _) = lax.optimization_barrier((*requests, send_lead))
            asked, *sends = gather_first(requests, inner, here, amplitudes, rows, cap)
            request, _ = lax.optimization_barrier((request, sends[0]))
            asked_last, *sends_last = gather_first([request], outer, here, amplitudes, rows, cap)
        else:
            sends = gather_again(asked, local_spots[1], stores, inner, cap)
            sends_last = gather_again(asked_last, local_spots[1], stores, outer, cap)
        for part, send in zip(inner + outer, [*sends, *sends_last]):
            arrived.append(lax.ppermute(send, "row", sent(rows, part[0])))
        *prepared, at_home = prepare(
            own, ats[again], homes[again], columns[again], near_count, shift, near, whole,
            integrals, fock_matrix, intersection,
        )
        spots = laid(arrived)
        at_home = [(remote, at_home)]
        done_early = finish(
            0, early, numbers, far_scale, prepared, spots[:-1] + at_home, occ_count,
            last,
        )
        given_early = lax.ppermute(done_early[0], "rep", swap)
        if last:
            final = put_in_slots(own[:early], [done_early[0]], pairs)
        done_late = finish(
            early, tail, numbers, far_scale, prepared, spots + at_home, occ_count, last
        )
        given_late = lax.ppermute(done_late[0], "rep", swap)
        stores = [done_early[0], given_early, done_late[0], given_late]
        whole = [
            jnp.concatenate([done_early[0], done_late[0]], axis=0),
            jnp.concatenate([given_early, given_late], axis=0),
        ]
    final = put_in_slots(slots, stores[1:], pairs, final)
    occ_sum = (done_early[1] + done_late[1])[0]
    occ_sum = add_over(occ_sum, "rep")
    occ_sum = add_over(occ_sum, "col")
    occ_sum = add_over(occ_sum, "row")
    total_pairs = pairs * rows * lax.axis_size("col")
    occ_density = occ_sum * (occ_count / (2.0 * total_pairs * domain * domain))
    return (final, occ_density)


def solution(mesh):
    pair_spec = P(("groups", "row", "col"), None, None)
    flat = P(("groups", "row", "col"))
    table = P(("groups", "row", "col"), None)
    return jax.shard_map(
        per_device,
        mesh=mesh,
        in_specs=(
            pair_spec, pair_spec, pair_spec, pair_spec,
            P("groups"), flat, flat, table, flat, table, table, table, table,
        ),
        out_specs=(pair_spec, P("groups")),
        check_vma=False,
    )
```

```python
import jax
import jax.numpy as jnp
from jax import lax
from jax.experimental import pallas as pl
from jax.experimental.pallas import tpu as pltpu
from jax.sharding import PartitionSpec as P


ITERS = 2
ANY = pl.ANY
SMEM = pltpu.SMEM
VMEM = pltpu.VMEM
LANES = 16
MIB = 1 << 20


def ring(rows, row):
    return row if rows & (rows - 1) else row ^ (row >> 1)


def sent(rows, step):
    hop = (step + 1) // 2 if step % 2 else rows - step // 2
    where = {ring(rows, r): r for r in range(rows)}
    return [(r, where[(ring(rows, r) + hop) % rows]) for r in range(rows)]


def asked_of(rows, step):
    return [(b, a) for a, b in sent(rows, step)]


def step_of(rows, source, row):
    hop = ring(rows, row) - ring(rows, source)
    hop = jnp.where(hop < 0, hop + rows, hop)
    step = jnp.where(2 * hop <= rows, 2 * hop - 1, 2 * (rows - hop))
    return jnp.where(hop == 0, 0, step)


def in_hbm(array):
    return pltpu.with_memory_space_constraint(array, pltpu.HBM)


def limits(mib):
    return pltpu.CompilerParams(vmem_limit_bytes=mib * MIB)


def cost(flops, size):
    return pl.CostEstimate(flops=flops, transcendentals=0, bytes_accessed=size)


def fetch(candidates, spot, target):
    for offset, ref in candidates:

        @pl.when((spot >= offset) & (spot < offset + ref.shape[0]))
        def _(offset=offset, ref=ref):
            target[...] = ref[spot - offset]


def laid(refs, offset=0):
    placed = []
    for ref in refs:
        placed.append((offset, ref))
        offset += ref.shape[0]
    return placed


def gather_first(requests, parts, place, amplitudes, rows, cap):
    pairs, domain = amplitudes.shape[:2]
    steps = sorted({step for step, _, _ in parts})
    count_of = len(steps)
    blocks = sum(size for _, _, size in parts)
    bits = pairs.bit_length() - 1

    def body(place_ref, *refs):
        lists = refs[:count_of]
        store = refs[count_of]
        asked = refs[count_of + 1]
        outs = refs[count_of + 2 : -1]
        sem = refs[-1]
        me = place_ref[0]
        core = place_ref[1]
        for n, step in enumerate(steps):
            base = n * (cap + 1)
            asker = jnp.int32(0)
            for a, b in sent(rows, step):
                asker = jnp.where(me == a, b, asker)
            served = [asker]
            for sooner in range(1, step):
                server = jnp.int32(0)
                for a, b in sent(rows, sooner):
                    server = jnp.where(asker == b, a, server)
                served.append(server)
            for k in range(cap):
                asked[base + k] = 0
            entries = [lists[n][p] for p in range(pairs)]
            sources = [entry // pairs if pairs & (pairs - 1) else entry >> bits for entry in entries]
            count = jnp.int32(0)
            for p in range(pairs):
                for server in served:
                    count = count + (sources[p] == server).astype(jnp.int32)
            filled = jnp.int32(0)
            for p in range(pairs):
                mine = (sources[p] == me).astype(jnp.int32)
                asked[base + jnp.minimum(filled, cap)] = entries[p] - sources[p] * pairs
                filled = filled + jnp.where((count & 1) == core, mine, 0)
                count = count + mine
            for m, (of, begin, size) in enumerate(parts):
                for k in range(size if of == step else 0):
                    pltpu.make_async_copy(
                        store.at[asked[base + begin + k]], outs[m].at[k], sem.at[m, k]
                    ).start()
        for m, (_, _, size) in enumerate(parts):
            for k in range(size):
                pltpu.make_async_copy(store.at[0], outs[m].at[k], sem.at[m, k]).wait()

    return pl.pallas_call(
        body,
        out_shape=[jax.ShapeDtypeStruct((count_of * (cap + 1),), jnp.int32)]
        + [VMEM((size, domain, domain), jnp.bfloat16) for _, _, size in parts],
        in_specs=[pl.BlockSpec(memory_space=SMEM)] * (count_of + 1)
        + [pl.BlockSpec(memory_space=pltpu.HBM)],
        out_specs=[pl.BlockSpec(memory_space=SMEM)]
        + [pl.BlockSpec(memory_space=VMEM)] * len(parts),
        scratch_shapes=[pltpu.SemaphoreType.DMA((len(parts), cap))],
        cost_estimate=cost(0, blocks * domain * domain * 4),
        compiler_params=limits(8),
        name="gather_first",
    )(place, *requests, in_hbm(amplitudes))


def gather_again(asked, where, stores, parts, cap):
    domain = stores[0].shape[1]
    steps = sorted({step for step, _, _ in parts})
    blocks = sum(size for _, _, size in parts)

    def body(asked_ref, where_ref, *refs):
        sources = laid(refs[: len(stores)])
        outs = refs[len(stores) :]
        for m, (step, begin, size) in enumerate(parts):
            for k in range(size):
                spot = where_ref[asked_ref[steps.index(step) * (cap + 1) + begin + k]]
                fetch(sources, spot, outs[m].at[k])

    return pl.pallas_call(
        body,
        out_shape=[VMEM((size, domain, domain), jnp.bfloat16) for _, _, size in parts],
        in_specs=[pl.BlockSpec(memory_space=SMEM)] * 2
        + [pl.BlockSpec(memory_space=VMEM)] * len(stores),
        out_specs=[pl.BlockSpec(memory_space=VMEM)] * len(parts),
        cost_estimate=cost(0, blocks * domain * domain * 4),
        compiler_params=limits(8),
        name="gather_again",
    )(asked, where, *stores)


def prepare(
    own, at, home, columns, counts, shift, near, stores, integrals, fock_matrix, intersection
):
    half = own.shape[0]
    domain = integrals.shape[1]
    total = columns.shape[0]
    entries = near[0].shape[1]
    groups = domain // LANES // half
    strip = groups * LANES

    def spread_weights(own_ref, column_ref, slot_ref, count_ref, weight_ref, spread_ref):
        lane = lax.broadcasted_iota(jnp.int32, (total, total), 1)
        down = lax.broadcasted_iota(jnp.int32, (total, total), 0)
        used_count = jnp.zeros((total, total), jnp.int32)
        for n in range(total):
            used_count = jnp.where(down == n, count_ref[n], used_count)
        weights = jnp.zeros((total, total), jnp.float32)
        for k in range(entries):
            used = (slot_ref[:, k : k + 1] == lane) & (k < used_count)
            wide = weight_ref[:, k : k + 1].astype(jnp.float32)
            weights = weights + jnp.where(used, wide, jnp.float32(0.0))
        weights = weights.astype(jnp.bfloat16)
        shape = (half * LANES, total)
        row = lax.broadcasted_iota(jnp.int32, shape, 0) // LANES
        wanted = jnp.zeros(shape, jnp.int32)
        for n in range(half):
            wanted = jnp.where(row == n, own_ref[n], wanted)
        pick = lax.broadcasted_iota(jnp.int32, shape, 1) == wanted
        mine = jnp.dot(
            pick.astype(jnp.float32).astype(jnp.bfloat16),
            weights,
            preferred_element_type=jnp.float32,
        ).astype(jnp.bfloat16)
        shape = (total, total * LANES)
        column = lax.broadcasted_iota(jnp.int32, shape, 1) // LANES
        wanted = jnp.zeros(shape, jnp.int32)
        for n in range(total):
            wanted = jnp.where(column == n, column_ref[n], wanted)
        pick = lax.broadcasted_iota(jnp.int32, shape, 0) == wanted
        full = jnp.dot(
            mine,
            pick.astype(jnp.float32).astype(jnp.bfloat16),
            preferred_element_type=jnp.float32,
        )
        shape = (half * LANES, total * LANES)
        down = lax.broadcasted_iota(jnp.int32, shape, 0) % LANES
        along = lax.broadcasted_iota(jnp.int32, shape, 1) % LANES
        spread_ref[...] = jnp.where(down == along, full, 0.0).astype(jnp.bfloat16)

    def body(
        own_ref, at_ref, home_ref, column_ref, count_ref, shift_ref, slot_ref, weight_ref, *refs
    ):
        sources = refs[: len(stores)]
        (
            integ_ref, fock_ref, over_ref,
            local_ref, rest_ref, recip_ref, keep_ref, near_by_ref, spread_ref,
        ) = refs[len(stores) :]
        i = pl.program_id(0)

        @pl.when(i == 0)
        def _():
            spread_weights(own_ref, column_ref, slot_ref, count_ref, weight_ref, spread_ref)

        for g in range(groups):
            rows = pl.ds(pl.multiple_of(i * strip + g * LANES, LANES), LANES)
            part = [s[:, rows, :].reshape(s.shape[0] * LANES, domain) for s in sources]
            part = part[0] if len(part) == 1 else jnp.concatenate(part, axis=0)
            sums = jnp.dot(spread_ref[...], part, preferred_element_type=jnp.float32)
            local_ref[:, g * LANES : (g + 1) * LANES, :] = sums.reshape(half, LANES, domain)
        amps = sources[0][at_ref[i]]
        fock = fock_ref[0]
        wide = amps.astype(jnp.float32)
        left = jnp.dot(fock, amps, preferred_element_type=jnp.float32)
        right = jnp.dot(amps, fock, preferred_element_type=jnp.float32)
        row_id = lax.broadcasted_iota(jnp.int32, (domain, domain), 0)
        col_id = lax.broadcasted_iota(jnp.int32, (domain, domain), 1)
        diagonal = jnp.where(row_id == col_id, fock.astype(jnp.float32), 0.0)
        across = jnp.sum(diagonal, axis=0, keepdims=True)
        down = jnp.sum(diagonal, axis=1, keepdims=True)
        residual = integ_ref[0].astype(jnp.float32) + left + right - shift_ref[i] * wide
        recip = 1.0 / (down + across - shift_ref[i])
        recip_ref[0] = recip
        rest_ref[0] = wide - residual * recip
        keep_ref[0] = over_ref[0]
        fetch(laid(sources), home_ref[i], near_by_ref.at[0])

    block = (1, domain, domain)
    mine = pl.BlockSpec(block, lambda i, own, *_: (own[i], 0, 0))
    in_turn = pl.BlockSpec(block, lambda i, *_: (i, 0, 0))
    wide_shape = jax.ShapeDtypeStruct((half, domain, domain), jnp.float32)
    return pl.pallas_call(
        body,
        grid_spec=pltpu.PrefetchScalarGridSpec(
            num_scalar_prefetch=6,
            grid=(half,),
            in_specs=[pl.BlockSpec(n.shape, lambda i, *_: (0, 0)) for n in near]
            + [pl.BlockSpec(s.shape, lambda i, *_: (0, 0, 0)) for s in stores]
            + [mine, mine, mine],
            out_specs=[
                pl.BlockSpec((half, strip, domain), lambda i, *_: (0, i, 0)),
                in_turn,
                in_turn,
                in_turn,
                in_turn,
            ],
            scratch_shapes=[VMEM((half * LANES, total * LANES), jnp.bfloat16)],
        ),
        out_shape=[
            wide_shape,
            wide_shape,
            wide_shape,
            jax.ShapeDtypeStruct((half, domain, domain), jnp.bfloat16),
            jax.ShapeDtypeStruct((half, domain, domain), jnp.bfloat16),
        ],
        cost_estimate=cost(
            2 * half * domain**3 * 3,
            (total + 4 * half) * domain * domain * 2 + half * domain * domain * 12,
        ),
        compiler_params=limits(20),
        name="prepare",
    )(
        own, at, home, columns, counts, shift, *near,
        *[in_hbm(s) if s.shape[0] > half else s for s in stores],
        in_hbm(integrals), in_hbm(fock_matrix), in_hbm(intersection),
    )


def finish(start, count, numbers, scale, prepared, arrived, occ_count, last):
    half, domain = prepared[0].shape[:2]

    def body(number_ref, scale_ref, local_ref, rest_ref, recip_ref, over_ref, *refs):
        candidates = [
            (offset, ref) for offset, ref in zip([o for o, _ in arrived], refs)
        ]
        outs = refs[len(candidates) : -1]
        hold = refs[-1]
        for n in range(count):
            fetch(candidates, number_ref[start + n], hold.at[n])
        if last:
            row_id = lax.broadcasted_iota(jnp.int32, (domain, domain), 0)
            col_id = lax.broadcasted_iota(jnp.int32, (domain, domain), 1)
            on_diagonal = row_id == col_id
            orbital = lax.broadcasted_iota(jnp.int32, (1, occ_count), 1)
            density = jnp.zeros((1, occ_count), jnp.float32)
        for n in range(count):
            i = start + n
            coupled = local_ref[i] + scale_ref[i] * hold[n].astype(jnp.float32)
            over = over_ref[i]
            projected = jnp.dot(
                over, coupled.astype(jnp.bfloat16), preferred_element_type=jnp.float32
            )
            back = lax.dot_general(
                projected.astype(jnp.bfloat16),
                over,
                (((1,), (1,)), ((), ())),
                preferred_element_type=jnp.float32,
            )
            fresh = (rest_ref[i] + back * recip_ref[i]).astype(jnp.bfloat16)
            outs[0][n] = fresh
            if last:
                wide = fresh.astype(jnp.float32)
                square = jnp.dot(fresh, fresh, preferred_element_type=jnp.float32)
                terms = 2.0 * wide * wide - jnp.where(on_diagonal, square, 0.0)
                norm = jnp.sum(jnp.sum(terms, axis=0, keepdims=True), axis=1, keepdims=True)
                picks = (orbital == number_ref[half + i]).astype(jnp.float32)
                picks = picks + (orbital == number_ref[2 * half + i]).astype(jnp.float32)
                density = density + norm * picks
        if last:
            outs[1][...] = density

    out_shape = [VMEM((count, domain, domain), jnp.bfloat16)]
    if last:
        out_shape.append(VMEM((1, occ_count), jnp.float32))
    return pl.pallas_call(
        body,
        out_shape=out_shape,
        in_specs=[pl.BlockSpec(memory_space=SMEM)] * 2
        + [pl.BlockSpec(memory_space=VMEM)] * 4
        + [pl.BlockSpec(memory_space=VMEM)] * len(arrived),
        out_specs=[pl.BlockSpec(memory_space=VMEM)] * len(out_shape),
        scratch_shapes=[VMEM((count, domain, domain), jnp.bfloat16)],
        cost_estimate=cost(2 * count * domain**3 * 2, count * domain * domain * 18),
        compiler_params=limits(16),
        name="finish",
    )(numbers, scale, *prepared, *[a for _, a in arrived])


def put_in_slots(slots, stores, total, whole=None):
    domain = stores[0].shape[1]
    blocks = sum(s.shape[0] for s in stores)
    given = [] if whole is None else [whole]

    def body(slot_ref, *refs):
        sources = refs[: len(stores)]
        out_ref, sem = refs[-2:]
        copies = []
        for source in sources:
            for n in range(source.shape[0]):
                at = len(copies)
                copies.append(
                    pltpu.make_async_copy(source.at[n], out_ref.at[slot_ref[at]], sem.at[at])
                )
        for copy in copies:
            copy.start()
        for copy in copies:
            copy.wait()

    return pl.pallas_call(
        body,
        out_shape=jax.ShapeDtypeStruct((total, domain, domain), jnp.bfloat16),
        in_specs=[pl.BlockSpec(memory_space=SMEM)]
        + [pl.BlockSpec(memory_space=VMEM)] * len(stores)
        + [pl.BlockSpec(memory_space=ANY)] * len(given),
        out_specs=pl.BlockSpec(memory_space=ANY),
        scratch_shapes=[pltpu.SemaphoreType.DMA((blocks,))],
        input_output_aliases={1 + len(stores): 0} if given else {},
        cost_estimate=cost(0, blocks * domain * domain * 4),
        compiler_params=limits(8),
        name="put_in_slots",
    )(slots, *stores, *given)


def add_over(values, name):
    size = lax.axis_size(name)
    if size & (size - 1):
        return lax.psum(values, name)
    steps = [1 << bit for bit in range(size.bit_length() - 1)]
    if name == "row":
        steps = [size - 1] + steps[:-1]
    for step in steps:
        values = values + lax.ppermute(values, name, [(r, r ^ step) for r in range(size)])
    return values


def per_device(
    amplitudes,
    integrals,
    fock_matrix,
    intersection,
    occ_energy,
    first_occ,
    second_occ,
    near_slot,
    near_count,
    near_weight,
    far_chip,
    far_slot,
    far_weight,
):
    pairs, domain = amplitudes.shape[:2]
    rows = lax.axis_size("row")
    half = pairs // 2
    cap = pairs // rows
    row = lax.axis_index("row")
    core = lax.axis_index("rep")
    occ_count = occ_energy.shape[0]
    slot_ids = jnp.arange(pairs, dtype=jnp.int32)
    source = far_chip[:, 0]
    packed = source * pairs + far_slot[:, 0]
    here = jnp.stack([row, core]).astype(jnp.int32)
    tail = max(1, cap // 2)
    lead = [(1, 0, cap)]
    rest = [(step, 0, cap) for step in range(2, rows - 1)]
    rest += [(rows - 1, 0, cap - tail)] * (cap > tail) + [(rows - 1, cap - tail, tail)]
    request = lax.ppermute(packed, "row", asked_of(rows, 1))
    requests = [
        lax.ppermute(packed, "row", asked_of(rows, d)) for d in range(2, rows)
    ]
    asked_lead, send_lead = gather_first([request], lead, here, amplitudes, rows, cap)

    (
        source, far_slot, occ_energy, first_occ, second_occ, far_weight,
        _,
    ) = lax.optimization_barrier(
        (
            source, far_slot, occ_energy, first_occ, second_occ, far_weight,
            asked_lead,
        )
    )
    step = step_of(rows, source, row)
    same = step[:, None] == step[None, :]
    before = (step[None, :] < step[:, None]) | (same & (slot_ids[None, :] < slot_ids[:, None]))
    turn = jnp.sum(before.astype(jnp.int32), axis=1)
    like = same & (turn[:, None] % 2 == turn[None, :] % 2) & (turn[None, :] < turn[:, None])
    place = jnp.sum(like.astype(jnp.int32), axis=1)
    mine = jnp.arange(half, dtype=jnp.int32) * 2 + core
    own_pick = mine[:, None] == turn[None, :]
    other_pick = (mine ^ 1)[:, None] == turn[None, :]

    def pick(chosen, values):
        return jnp.sum(jnp.where(chosen, values[None, :], jnp.zeros((), values.dtype)), axis=1)

    own = pick(own_pick, slot_ids)
    other = pick(other_pick, slot_ids)
    far_step = pick(own_pick, step)
    own_far = pick(own_pick, far_slot[:, 0])
    own_place = pick(own_pick, place)

    orbitals = jnp.arange(occ_count, dtype=jnp.int32)

    def energy_of(index):
        found = index[:, None] == orbitals[None, :]
        return jnp.sum(jnp.where(found, occ_energy[None, :], jnp.float32(0.0)), axis=1)

    far_scale = pick(own_pick, far_weight[:, 0].astype(jnp.float32))
    first = pick(own_pick, first_occ)
    second = pick(own_pick, second_occ)
    shift = energy_of(first) + energy_of(second)

    by_slot = turn // 2 + jnp.where(turn % 2 == core, 0, half)
    early = half - tail
    swap = [(0, 1), (1, 0)]
    remote = (rows - 1) * cap
    local_spots = [
        slot_ids,
        jnp.where(
            by_slot < half,
            by_slot + jnp.where(by_slot % half < early, 0, early),
            by_slot - half + jnp.where(by_slot % half < early, early, half),
        ),
    ]
    homes = [
        jnp.sum(jnp.where(own_far[:, None] == slot_ids[None, :], where[None, :], 0), axis=1)
        for where in (slot_ids, by_slot)
    ]
    at_home = remote + jnp.arange(half, dtype=jnp.int32)
    spot = jnp.where(far_step == 0, at_home, (far_step - 1) * cap + own_place)
    numbers = jnp.concatenate([spot, first, second])
    near = [near_slot, near_weight]
    columns = [slot_ids, jnp.concatenate([own, other])]
    ats = [own, jnp.arange(half, dtype=jnp.int32)]
    slots = jnp.concatenate([other[:early], own[early:], other[early:]])
    stores = [amplitudes]
    whole = [amplitudes]
    for sweep in range(ITERS):
        last = sweep == ITERS - 1
        again = min(sweep, 1)
        if sweep > 0:
            (send_lead,) = gather_again(asked_lead, local_spots[1], stores, lead, cap)
        arrived = [lax.ppermute(send_lead, "row", sent(rows, 1))]
        if sweep == 0:
            (*requests, _) = lax.optimization_barrier((*requests, send_lead))
            asked, *sends = gather_first(requests, rest, here, amplitudes, rows, cap)
        else:
            sends = gather_again(asked, local_spots[1], stores, rest, cap)
        for part, send in zip(rest, sends):
            arrived.append(lax.ppermute(send, "row", sent(rows, part[0])))
        *prepared, at_home = prepare(
            own, ats[again], homes[again], columns[again], near_count, shift, near, whole,
            integrals, fock_matrix, intersection,
        )
        spots = laid(arrived)
        at_home = [(remote, at_home)]
        done_early = finish(
            0, early, numbers, far_scale, prepared, spots[:-1] + at_home, occ_count,
            last,
        )
        given_early = lax.ppermute(done_early[0], "rep", swap)
        if last:
            final = put_in_slots(own[:early], [done_early[0]], pairs)
        done_late = finish(
            early, tail, numbers, far_scale, prepared, spots + at_home, occ_count, last
        )
        given_late = lax.ppermute(done_late[0], "rep", swap)
        stores = [done_early[0], given_early, done_late[0], given_late]
        whole = [
            jnp.concatenate([done_early[0], done_late[0]], axis=0),
            jnp.concatenate([given_early, given_late], axis=0),
        ]
    final = put_in_slots(slots, stores[1:], pairs, final)
    occ_sum = (done_early[1] + done_late[1])[0]
    occ_sum = add_over(occ_sum, "rep")
    occ_sum = add_over(occ_sum, "col")
    occ_sum = add_over(occ_sum, "row")
    total_pairs = pairs * rows * lax.axis_size("col")
    occ_density = occ_sum * (occ_count / (2.0 * total_pairs * domain * domain))
    return (final, occ_density)


def solution(mesh):
    pair_spec = P(("groups", "row", "col"), None, None)
    flat = P(("groups", "row", "col"))
    table = P(("groups", "row", "col"), None)
    return jax.shard_map(
        per_device,
        mesh=mesh,
        in_specs=(
            pair_spec, pair_spec, pair_spec, pair_spec,
            P("groups"), flat, flat, table, flat, table, table, table, table,
        ),
        out_specs=(pair_spec, P("groups")),
        check_vma=False,
    )
```
